32 devices in a mesh: shot: 4 (over y, core), gx: 4 (over z), gy: 2 (over x).
Axes of the slice: x: 2, y: 2, z: 4, core: 2. Of those that a mesh axis runs over, the one named last changes fastest.
Arguments:
- latent: float32 [32, 24, 1024], P('shot', 'gx', 'gy'), may hold values from -6 to 6
- w_first: float32 [64, 64], replicated, may hold values from -0.75 to 0.75
- w_second: float32 [64, 128], replicated, may hold values from -0.75 to 0.75
- fwd_press: float32 [4, 96, 64, 128], P('shot', 'gx', 'gy'), may hold values from -1.5 to 8
- fwd_vel: float32 [4, 3, 96, 64, 128], P('shot', None, 'gx', 'gy'), may hold values from -1.5 to 8
- adj_press: float32 [4, 96, 64, 128], P('shot', 'gx', 'gy'), may hold values from -1.5 to 8
- adj_vel: float32 [4, 3, 96, 64, 128], P('shot', None, 'gx', 'gy'), may hold values from -1.5 to 8
- src_pos: int32 [3, 4], P(None, 'shot'), may hold values from 0 to 127, as said below
- src_amp: float32 [3, 4], P(None, 'shot'), may hold values from -24 to 24
- rec_pos: int32 [4, 3, 2048], P('shot'), may hold values from 0 to 127, as said below
- observed: float32 [4, 3, 2048], P('shot'), may hold values from -6 to 6
Outputs:
- grad_latent: float32 [32, 24, 1024], P('shot', 'gx', 'gy')
- grad_first: float32 [64, 64], replicated
- grad_second: float32 [64, 128], replicated
The draws below stay inside these ranges and needn't reach their ends.
Inputs may be any that keep to these rules, and one draw needn't show every extreme that they name: `src_pos`: row 0 is an x cell below 96, row 1 a y cell below 64, row 2 a depth cell below 128. `rec_pos`: component 0 is an x cell below 96, component 1 a y cell below 64, component 2 a depth cell below 128; cells may repeat.
All inputs are finite; a program needn't handle non-finite values.
Results may differ from the reference program's by a relative error of at most 0.0003.
Values sent between devices are 32-bit elements; how exact they have to be, the bound alone decides.
A program may use at most 64 MiB of HBM per device.

```python
import jax
import jax.numpy as jnp
from jax import lax

NZ = 128
NREC = 2048
CH = 64
STEPS = 3
OUTS = 128
NX = 96
NY = 64
SHOTS = 4
XC = 24
YC = 16
ZC = 32


def draw_src_pos(key, part):
    subkeys = jax.random.split(jax.random.fold_in(key, 11), 3)
    along_x = jax.random.randint(subkeys[0], (SHOTS,), 0, NX).at[0].set(NX - 1).at[1].set(0)
    along_y = jax.random.randint(subkeys[1], (SHOTS,), 0, NY).at[0].set(NY - 1)
    along_z = jax.random.randint(subkeys[2], (SHOTS,), 0, NZ).at[0].set(NZ - 1)
    return jnp.stack([along_x, along_y, along_z]).astype(jnp.int32)


def draw_rec_pos(key, part):
    subkeys = jax.random.split(jax.random.fold_in(key, 23), 3)
    along_x = jax.random.randint(subkeys[0], (SHOTS, NREC), 0, NX).at[:, 0].set(NX - 1).at[:, 1].set(0)
    along_y = jax.random.randint(subkeys[1], (SHOTS, NREC), 0, NY).at[:, 0].set(NY - 1)
    along_z = jax.random.randint(subkeys[2], (SHOTS, NREC), 0, NZ).at[:, 0].set(NZ - 1)
    return jnp.stack([along_x, along_y, along_z], axis=1).astype(jnp.int32)


def smooth_along(values_in, axis_id, spread):
    length = values_in.shape[axis_id]
    places = jnp.arange(length, dtype=jnp.float32)
    kernel = jnp.exp(-0.5 * jnp.square((places[:, None] - places[None, :]) / spread))
    kernel = kernel / jnp.sum(kernel, axis=1, keepdims=True)
    rotated = jnp.moveaxis(values_in, axis_id, -1)
    return jnp.moveaxis(jnp.dot(rotated, kernel.T), -1, axis_id)


def taper(length):
    places = jnp.arange(length, dtype=jnp.float32)
    distance = jnp.minimum(places, length - 1.0 - places)
    return jnp.square(jnp.sin(0.5 * jnp.pi * jnp.minimum(1.0, (distance + 0.5) / 6.0)))


def wavefield(key, leading):
    subkeys = jax.random.split(key, 2)
    full_shape = leading + (NX, NY, NZ)
    dimensions = len(full_shape)
    white_noise = jax.random.normal(subkeys[0], full_shape, jnp.float32)
    spread = 3.0
    smooth = white_noise
    for axis_id in (dimensions - 3, dimensions - 2, dimensions - 1):
        smooth = smooth_along(smooth, axis_id, spread)
    smooth = smooth / jnp.sqrt(jnp.mean(jnp.square(smooth)) + 1e-12)
    smooth = jnp.clip(smooth, -3.0, 3.0)
    envelope = taper(NX)[:, None, None] * taper(NY)[None, :, None] * taper(NZ)[None, None, :]
    rough_part = 0.12 * jax.random.normal(subkeys[1], full_shape, jnp.float32)
    wave_field = envelope * (2.5 + smooth) + rough_part
    return jnp.clip(wave_field, -1.5, 8.0).astype(jnp.float32)


def draw_fwd_press(key, part):
    return wavefield(jax.random.fold_in(key, 31), (SHOTS,))


def draw_fwd_vel(key, part):
    return wavefield(jax.random.fold_in(key, 37), (SHOTS, 3))


def draw_adj_press(key, part):
    return wavefield(jax.random.fold_in(key, 41), (SHOTS,))


def draw_adj_vel(key, part):
    return wavefield(jax.random.fold_in(key, 43), (SHOTS, 3))


def shard_levels(key, dims, cuts, smallest, high):
    def one(position, blocks):
        steps = jax.random.uniform(jax.random.fold_in(jax.random.fold_in(key, 6), position), (blocks,), jnp.float32, smallest / len(cuts), high / len(cuts))
        return jnp.repeat(jnp.exp(steps), dims[position] // blocks).reshape((-1,) + (1,) * (len(dims) - position - 1))

    loudness = one(*cuts[0])
    for cut in cuts[1:]:
        loudness = loudness * one(*cut)
    return loudness


def scatter_about(key, extent, width, reach, cuts=(), kind=jnp.bfloat16):
    level = shard_levels(key, extent, cuts, -0.22, 0.18) if cuts else 1.0
    result = jax.random.normal(key, extent, jnp.float32) * width * level
    return jnp.minimum(jnp.maximum(result, -reach), reach).astype(kind)


def setup_inputs(seed: int = 0) -> dict:
    streams_of = jax.random.split(jax.random.key(seed), 12)
    latent = scatter_about(streams_of[0], (ZC, XC, YC * CH), 1.0, 6.0, ((0, 4), (1, 4), (2, 2)), jnp.float32)
    w_first = scatter_about(streams_of[1], (CH, CH), CH ** -0.5, 0.75, (), jnp.float32)
    w_second = scatter_about(streams_of[2], (CH, OUTS), CH ** -0.5, 0.75, (), jnp.float32)
    fwd_press = draw_fwd_press(jax.random.fold_in(streams_of[11], 71), 0)
    fwd_vel = draw_fwd_vel(jax.random.fold_in(streams_of[11], 71), 0)
    adj_press = draw_adj_press(jax.random.fold_in(streams_of[11], 71), 0)
    adj_vel = draw_adj_vel(jax.random.fold_in(streams_of[11], 71), 0)
    src_pos = draw_src_pos(jax.random.fold_in(streams_of[11], 71), 0)
    src_amp = scatter_about(streams_of[8], (STEPS, SHOTS), 4.0, 24.0, ((1, 4),), jnp.float32)
    rec_pos = draw_rec_pos(jax.random.fold_in(streams_of[11], 71), 0)
    observed = scatter_about(streams_of[10], (SHOTS, STEPS, NREC), 1.0, 6.0, ((0, 4),), jnp.float32)
    return dict(latent=latent, w_first=w_first, w_second=w_second, fwd_press=fwd_press, fwd_vel=fwd_vel, adj_press=adj_press, adj_vel=adj_vel, src_pos=src_pos, src_amp=src_amp, rec_pos=rec_pos, observed=observed)


coeffs = (1225.0 / 1024.0, -245.0 / 3072.0, 49.0 / 5120.0, -5.0 / 7168.0)


def take_slab(values_in, axis_id, start_at, length):
    return lax.slice_in_dim(values_in, start_at, start_at + length, axis=axis_id)


def diff_plus(extended, axis_id, start_at, length):
    summed = 0.0
    for order, weight in enumerate(coeffs):
        offset = order + 1
        summed = summed + weight * (take_slab(extended, axis_id, start_at + offset, length) - take_slab(extended, axis_id, start_at - offset + 1, length))
    return summed


def diff_minus(extended, axis_id, start_at, length):
    summed = 0.0
    for order, weight in enumerate(coeffs):
        offset = order + 1
        summed = summed + weight * (take_slab(extended, axis_id, start_at + offset - 1, length) - take_slab(extended, axis_id, start_at - offset, length))
    return summed


def edge_pad(field_in, axis_id):
    widths = [(0, 0), (0, 0), (0, 0)]
    widths[axis_id] = (4, 4)
    return jnp.pad(field_in, widths)


def wave_step(pressure, vel_x, vel_y, vel_z, modulus, buoyancy):
    size_x, size_y, size_z = pressure.shape
    grad_x = diff_plus(edge_pad(pressure, 0), 0, 4, size_x)
    grad_y = diff_plus(edge_pad(pressure, 1), 1, 4, size_y)
    grad_z = diff_plus(edge_pad(pressure, 2), 2, 4, size_z)
    vel_x = vel_x - buoyancy * grad_x
    vel_y = vel_y - buoyancy * grad_y
    vel_z = vel_z - buoyancy * grad_z
    diverge = diff_minus(edge_pad(vel_x, 0), 0, 4, size_x) + diff_minus(edge_pad(vel_y, 1), 1, 4, size_y) + diff_minus(edge_pad(vel_z, 2), 2, 4, size_z)
    pressure = pressure - modulus * diverge
    return pressure, vel_x, vel_y, vel_z, diverge, grad_x, grad_y, grad_z


def decode(latent, w_first, w_second):
    depth_c, rows_x, merged = latent.shape
    rows_y = merged // CH
    flattened = latent.reshape(-1, CH)
    hidden = jnp.tanh(jnp.dot(flattened, w_first, precision=lax.Precision.HIGHEST))
    outputs = jnp.dot(hidden, w_second, precision=lax.Precision.HIGHEST)
    fine_out = outputs.reshape(depth_c, rows_x, rows_y, 2, 4, 4, 4).transpose(3, 1, 4, 2, 5, 0, 6).reshape(2, rows_x * 4, rows_y * 4, depth_c * 4)
    return flattened, hidden, fine_out


def materials(fine_out):
    wave_speed = 0.15 + 0.25 * jax.nn.sigmoid(fine_out[0])
    density = 1.0 + 1.5 * jax.nn.sigmoid(fine_out[1])
    return density * wave_speed * wave_speed, 1.0 / density


def decoder_grads(flattened, hidden, fine_out, grad_mod, grad_buoy, w_first, w_second):
    sig_speed = jax.nn.sigmoid(fine_out[0])
    sig_dens = jax.nn.sigmoid(fine_out[1])
    wave_speed = 0.15 + 0.25 * sig_speed
    density = 1.0 + 1.5 * sig_dens
    grad_speed = grad_mod * 2.0 * density * wave_speed
    grad_dens = grad_mod * wave_speed * wave_speed - grad_buoy / (density * density)
    grad_fine = jnp.stack([grad_speed * 0.25 * sig_speed * (1.0 - sig_speed), grad_dens * 1.5 * sig_dens * (1.0 - sig_dens)])
    size_x, size_y, size_z = grad_fine.shape[1], grad_fine.shape[2], grad_fine.shape[3]
    grad_out = grad_fine.reshape(2, size_x // 4, 4, size_y // 4, 4, size_z // 4, 4).transpose(5, 1, 3, 0, 2, 4, 6).reshape(-1, 128)
    grad_hidden = jnp.dot(grad_out, w_second.T, precision=lax.Precision.HIGHEST)
    grad_pre = grad_hidden * (1.0 - hidden * hidden)
    grad_latent = jnp.dot(grad_pre, w_first.T, precision=lax.Precision.HIGHEST).reshape(size_z // 4, size_x // 4, (size_y // 4) * CH)
    grad_second = jnp.dot(hidden.T, grad_out, precision=lax.Precision.HIGHEST)
    grad_first = jnp.dot(flattened.T, grad_pre, precision=lax.Precision.HIGHEST)
    return grad_latent, grad_first, grad_second


def reference(latent, w_first, w_second, fwd_press, fwd_vel, adj_press, adj_vel, src_pos, src_amp, rec_pos, observed):
    flattened, hidden, fine_out = decode(latent, w_first, w_second)
    modulus, buoyancy = materials(fine_out)

    def one_shot(totals, inputs):
        grad_mod, grad_buoy = totals
        start_press, start_vel, back_press, back_vel, source, amplitudes, receivers, observed_now = inputs
        pressure, vel_x, vel_y, vel_z = start_press, start_vel[0], start_vel[1], start_vel[2]
        stored = []
        misfits = []
        for moment in range(STEPS):
            pressure, vel_x, vel_y, vel_z, diverge, grad_x, grad_y, grad_z = wave_step(pressure, vel_x, vel_y, vel_z, modulus, buoyancy)
            pressure = pressure.at[source[0], source[1], source[2]].add(amplitudes[moment])
            misfits.append(pressure[receivers[0], receivers[1], receivers[2]] - observed_now[moment])
            stored.append((diverge, grad_x, grad_y, grad_z))
        pressure, vel_x, vel_y, vel_z = back_press, back_vel[0], back_vel[1], back_vel[2]
        for moment in reversed(range(STEPS)):
            pressure = pressure.at[receivers[0], receivers[1], receivers[2]].add(misfits[moment])
            pressure, vel_x, vel_y, vel_z, diverge, grad_x, grad_y, grad_z = wave_step(pressure, vel_x, vel_y, vel_z, modulus, buoyancy)
            grad_mod = grad_mod - pressure * stored[moment][0]
            grad_buoy = grad_buoy - (vel_x * stored[moment][1] + vel_y * stored[moment][2] + vel_z * stored[moment][3])
        return (grad_mod, grad_buoy), None

    zeros = jnp.zeros(modulus.shape, jnp.float32)
    totals, _ignored = lax.scan(one_shot, (zeros, zeros), (fwd_press, fwd_vel, adj_press, adj_vel, src_pos.T, src_amp.T, rec_pos, observed))
    grad_latent, grad_first, grad_second = decoder_grads(flattened, hidden, fine_out, totals[0], totals[1], w_first, w_second)
    return grad_latent, grad_first, grad_second
```

```python
import jax
import jax.numpy as jnp
from jax import lax
from jax.experimental import pallas as pl
from jax.experimental.pallas import tpu as pltpu
from jax.sharding import PartitionSpec as P

CH = 64
STEPS = 3
RIM = 7
VRIM = 4
PAD = 8
GROUP = 4
LANES = 128

coeffs = (1225.0 / 1024.0, -245.0 / 3072.0, 49.0 / 5120.0, -5.0 / 7168.0)

rows_by_cols = (((1,), (0,)), ((), ()))
rows_by_rows = (((1,), (1,)), ((), ()))
half = jnp.bfloat16


def split(values):
    high = values.astype(half)
    return high, (values - high.astype(jnp.float32)).astype(half)


def mm(left, right, how=rows_by_cols):
    return lax.dot_general(left, right, how, preferred_element_type=jnp.float32)


def mm3(left, right, how=rows_by_cols):
    return (
        mm(left[0], right[0], how) + mm(left[1], right[0], how) + mm(left[0], right[1], how)
    )


def mm2(left, pick, how=rows_by_cols):
    return mm(left[0], pick, how) + mm(left[1], pick, how)


def one_hot(shape, rule):
    rows = lax.broadcasted_iota(jnp.int32, shape, 0)
    cols = lax.broadcasted_iota(jnp.int32, shape, 1)
    return rule(rows, cols)


def as_pick(mask):
    return jnp.where(mask, 1.0, 0.0).astype(half)


def axis_peers(axis, distance):
    count = lax.axis_size(axis)
    return {axis: lax.rem(lax.axis_index(axis) + distance, count)}


def plane_peers():
    near, wide = lax.axis_size("gy"), lax.axis_size("gx")
    for dx in range(wide):
        for dy in range(near):
            if dx or dy:
                yield {
                    "gx": lax.rem(lax.axis_index("gx") + dx, wide),
                    "gy": lax.rem(lax.axis_index("gy") + dy, near),
                }


def everyone():
    for d in range(1, lax.axis_size("shot")):
        yield axis_peers("shot", d)
    yield from plane_peers()


def remote(source, dest, send_sem, recv_sem, peer):
    return pltpu.make_async_remote_copy(
        src_ref=source,
        dst_ref=dest,
        send_sem=send_sem,
        recv_sem=recv_sem,
        device_id=peer,
        device_id_type=pl.DeviceIdType.MESH,
    )


def logistic(values):
    return 0.5 * jnp.tanh(0.5 * values) + 0.5


def whole_kernel(
    latent_ref,
    first_ref,
    second_ref,
    fwd_press,
    fwd_vel,
    adj_press,
    adj_vel,
    src_pos,
    src_amp,
    rec_pos,
    observed,
    own_ref,
    sums_ref,
    w_first,
    w_second,
    place,
    amps,
    rec_at,
    seen,
    start_adj,
    slabs,
    latents,
    hidden,
    gates,
    hits,
    recorded,
    rec_weights,
    mod,
    press,
    buoy,
    vel_x,
    vel_y,
    vel_z,
    diverge_z,
    misfit,
    div_at,
    slope_x,
    slope_y,
    slope_z,
    totals,
    turned,
    share,
    landed,
    w_share,
    w_landed,
    w_plane,
    local_sem,
    send_sem,
    recv_sem,
    shot_send,
    shot_recv,
    plane_send,
    plane_recv,
):
    size_x, size_y, size_z = mod.shape
    cells = size_z // 4
    tall = size_y + 2 * PAD
    mid_y = pl.ds(PAD, size_y)
    mid_v = pl.ds(VRIM, size_x)
    rows_a = size_x // 4
    wide = GROUP * CH
    halves = size_y // (4 * GROUP)
    shots = lax.axis_size("shot")
    me = lax.axis_index("shot")
    me_x, me_y = lax.axis_index("gx"), lax.axis_index("gy")
    has = (
        me_x > 0,
        me_x < lax.axis_size("gx") - 1,
        me_y > 0,
        me_y < lax.axis_size("gy") - 1,
    )
    target = ({"gx": me_x - 1}, {"gx": me_x + 1}, {"gy": me_y - 1}, {"gy": me_y + 1})

    barrier = pltpu.get_barrier_semaphore()
    greeted = 0
    for peer in everyone():
        pl.semaphore_signal(
            barrier, inc=1, device_id=peer, device_id_type=pl.DeviceIdType.MESH
        )
        greeted += 1

    loads = [
        (first_ref, w_first),
        (second_ref, w_second),
        (rec_pos, rec_at),
        (observed, seen),
        (src_pos, place),
        (src_amp, amps),
        (latent_ref, slabs.at[me]),
        (fwd_press, press.at[0, pl.ds(RIM, size_x), mid_y]),
        (adj_press, start_adj),
    ]
    for way, vel in enumerate((fwd_vel, adj_vel)):
        loads.append((vel.at[0], vel_x.at[way, pl.ds(VRIM, size_x)]))
        loads.append((vel.at[1], vel_y.at[way, :, mid_y]))
        loads.append((vel.at[2], vel_z.at[way]))
    moves = [
        pltpu.make_async_copy(source, dest, local_sem.at[n])
        for n, (source, dest) in enumerate(loads)
    ]
    for move in moves:
        move.start()

    def channel(slot, pairs):
        return [
            remote(
                pairs[side][0],
                pairs[side][1],
                send_sem.at[slot, side],
                recv_sem.at[slot, side ^ 1],
                target[side],
            )
            for side in range(4)
        ]

    def press_pairs(state, edges):
        low_x, high_x = pl.ds(0, RIM), pl.ds(size_x + RIM, RIM)
        low_y, high_y = pl.ds(0, PAD), pl.ds(size_y + PAD, PAD)
        mid_x = pl.ds(RIM, size_x)
        return [
            (edges[0], press.at[state, high_x, mid_y]),
            (edges[1], press.at[state, low_x, mid_y]),
            (edges[2], press.at[state, mid_x, high_y]),
            (edges[3], press.at[state, mid_x, low_y]),
        ]

    def own_edges(state):
        mid_x = pl.ds(RIM, size_x)
        return [
            press.at[state, pl.ds(RIM, RIM), mid_y],
            press.at[state, pl.ds(size_x, RIM), mid_y],
            press.at[state, mid_x, pl.ds(PAD, PAD)],
            press.at[state, mid_x, pl.ds(size_y, PAD)],
        ]

    first_edges = [
        fwd_press.at[pl.ds(0, RIM)],
        fwd_press.at[pl.ds(size_x - RIM, RIM)],
        fwd_press.at[:, pl.ds(0, PAD)],
        fwd_press.at[:, pl.ds(size_y - PAD, PAD)],
    ]
    channels = [channel(0, press_pairs(0, first_edges))]
    for state in range(1, 2 * STEPS):
        channels.append(channel(state, press_pairs(state, own_edges(state))))
    for way, vel in enumerate((fwd_vel, adj_vel)):
        channels.append(
            channel(
                2 * STEPS + way,
                [
                    (vel.at[0, pl.ds(0, VRIM)], vel_x.at[way, pl.ds(size_x + VRIM, VRIM)]),
                    (vel.at[0, pl.ds(size_x - VRIM, VRIM)], vel_x.at[way, pl.ds(0, VRIM)]),
                    (vel.at[1, :, pl.ds(0, PAD)], vel_y.at[way, :, pl.ds(size_y + PAD, PAD)]),
                    (vel.at[1, :, pl.ds(size_y - PAD, PAD)], vel_y.at[way, :, pl.ds(0, PAD)]),
                ],
            )
        )
    channels.append(
        channel(
            2 * STEPS + 2,
            [
                (buoy.at[pl.ds(VRIM, VRIM), mid_y], buoy.at[pl.ds(size_x + VRIM, VRIM), mid_y]),
                (buoy.at[pl.ds(size_x, VRIM), mid_y], buoy.at[pl.ds(0, VRIM), mid_y]),
                (buoy.at[mid_v, pl.ds(PAD, PAD)], buoy.at[mid_v, pl.ds(size_y + PAD, PAD)]),
                (buoy.at[mid_v, pl.ds(size_y, PAD)], buoy.at[mid_v, pl.ds(0, PAD)]),
            ],
        )
    )

    def send(slot, sides):
        for side in sides:

            @pl.when(has[side])
            def _():
                channels[slot][side].start()

    def receive(slot):
        for side in range(4):

            @pl.when(has[side])
            def _():
                channels[slot][side ^ 1].wait_recv()

    def sent(slot):
        for side in range(4):

            @pl.when(has[side])
            def _():
                channels[slot][side].wait_send()

    for side in range(4):

        @pl.when(jnp.logical_not(has[side]))
        def _():
            far = side % 2
            if side < 2:
                rows = pl.ds(far * (size_x + RIM), RIM)
                vrows = pl.ds(far * (size_x + VRIM), VRIM)
                for state in range(2 * STEPS):
                    press[state, rows, mid_y] = jnp.zeros((RIM, size_y, size_z), jnp.float32)
                buoy[vrows, mid_y] = jnp.zeros((VRIM, size_y, size_z), jnp.float32)
                for way in range(2):
                    vel_x[way, vrows] = jnp.zeros((VRIM, size_y, size_z), jnp.float32)
            else:
                cols = pl.ds(far * (size_y + PAD), PAD)
                blank = jnp.zeros((size_x, PAD, size_z), jnp.float32)
                for state in range(2 * STEPS):
                    press[state, pl.ds(RIM, size_x), cols] = blank
                buoy[mid_v, cols] = blank
                for way in range(2):
                    vel_y[way, :, cols] = blank

    pl.semaphore_wait(barrier, greeted)

    gathers = [
        remote(
            latent_ref,
            slabs.at[me],
            shot_send.at[0, d - 1],
            shot_recv.at[0, d - 1],
            axis_peers("shot", d),
        )
        for d in range(1, shots)
    ]
    for copy in gathers:
        copy.start()
    every = range(4)
    send(0, every)
    send(2 * STEPS, every)
    send(2 * STEPS + 1, every)
    for move in moves:
        move.wait()

    spread_rows = as_pick(one_hot((wide, CH), lambda r, c: r % CH == c))
    same_cell = one_hot((wide, wide), lambda r, c: r // CH == c // CH)
    big_first = tuple(
        jnp.where(same_cell, mm(mm(spread_rows, part).astype(half), spread_rows, rows_by_rows), 0.0)
        .astype(half)
        for part in split(w_first[...])
    )
    outs = w_second.shape[1]
    block = outs // 4 * GROUP

    def source_of(c):
        return c % block // 64 * 64 + c % 64 // 16 * 16 + c % 4 * 4 + c // block

    order = as_pick(one_hot((outs, 4 * block), lambda r, c: source_of(c) == r))
    same_out = one_hot((wide, 4 * block), lambda r, c: c % 16 // 4 == r // CH)
    big_second = tuple(
        jnp.where(same_out, mm(mm(spread_rows, part).astype(half), order), 0.0).astype(half)
        for part in split(w_second[...])
    )
    depth_pick = as_pick(one_hot((size_z, size_z), lambda r, c: 4 * (r % cells) + r // cells == c))

    count = rec_at.shape[1]
    local_x = rec_at[0:1] - me_x * size_x
    local_y = rec_at[1:2] - me_y * size_y
    inside = (local_x >= 0) & (local_x < size_x) & (local_y >= 0) & (local_y < size_y)
    column = jnp.where(inside, local_x * size_y + local_y, -1)
    deep = jnp.where(
        lax.broadcasted_iota(jnp.int32, (size_z, count), 0) == rec_at[2:3], 1.0, 0.0
    )
    rec_weights[pl.ds(0, size_z)] = deep.astype(half)
    for moment in range(STEPS):
        for part, values in enumerate(split(seen[moment : moment + 1])):
            rec_weights[pl.ds((1 + 2 * moment + part) * size_z, size_z)] = (
                deep * values.astype(jnp.float32)
            ).astype(half)
    chunk = 8 if size_x % 8 == 0 else 1
    some = chunk * size_y

    def planes(step, carry):
        index = lax.broadcasted_iota(jnp.int32, (some, count), 0) + step * some
        summed = mm(as_pick(index == column), rec_weights[...], rows_by_rows).reshape(
            chunk, size_y, (2 * STEPS + 1) * size_z
        )
        here = pl.ds(step * chunk, chunk)
        hits[here] = summed[:, :, :size_z]
        for moment in range(STEPS):
            first = (1 + 2 * moment) * size_z
            recorded[moment, here] = (
                summed[:, :, first : first + size_z]
                + summed[:, :, first + size_z : first + 2 * size_z]
            )
        return carry

    lax.fori_loop(0, size_x // chunk, planes, 0)

    for copy in gathers:
        copy.wait()
    depth_c = slabs.shape[1]
    for s in range(shots):
        slab = jnp.transpose(slabs[s], (1, 0, 2))
        for a in range(rows_a):
            latents[pl.ds(a * cells + s * depth_c, depth_c)] = slab[a]
    for h in range(halves):
        lanes = slice(h * wide, (h + 1) * wide)
        state = jnp.tanh(mm3(split(latents[:, lanes]), big_first))
        hidden[:, lanes] = state
        outputs = mm3(split(state), big_second)
        for a in range(rows_a):
            rows = slice(a * cells, (a + 1) * cells)
            stacked = jnp.concatenate(
                [outputs[rows, k * block : (k + 1) * block] for k in range(4)], axis=0
            )
            sig = logistic(mm2(split(jnp.transpose(stacked)), depth_pick))
            gates[h, a] = sig
            speed = 0.15 + 0.25 * sig[: block // 2]
            density = 1.0 + 1.5 * sig[block // 2 :]
            modulus = density * speed * speed
            buoyancy = 1.0 / density
            deep_y = 4 * GROUP
            for i in range(4):
                part = slice(i * deep_y, (i + 1) * deep_y)
                mod[4 * a + i, pl.ds(h * deep_y, deep_y)] = modulus[part]
                buoy[VRIM + 4 * a + i, pl.ds(PAD + h * deep_y, deep_y)] = buoyancy[part]
    send(2 * STEPS + 2, every)

    along = [
        split(matrix) for matrix in depth_matrices(size_z)
    ]
    tables = [
        jnp.concatenate(
            [
                jnp.concatenate([high, low], axis=1),
                jnp.concatenate([high, jnp.zeros_like(low)], axis=1),
            ],
            axis=0,
        )
        for high, low in along
    ]

    def along_z(values, table):
        flat = values.reshape(values.shape[0] * size_y, size_z)
        both = mm(jnp.concatenate(split(flat), axis=1), table)
        return (both[:, :size_z] + both[:, size_z:]).reshape(values.shape)

    src_x = place[0:1] - me_x * size_x
    src_y = place[1:2] - me_y * size_y
    at_source = jnp.where(
        (lax.broadcasted_iota(jnp.int32, (size_y, size_z), 0) == src_y)
        & (lax.broadcasted_iota(jnp.int32, (size_y, size_z), 1) == place[2:3]),
        1.0,
        0.0,
    )
    def step(state, way, moment):
        def depth_part(turn, carry):
            here = pl.ds(turn * chunk, chunk)
            inner = press[state, pl.ds(turn * chunk + RIM, chunk), mid_y]
            slope = along_z(inner, tables[0])
            if way == 0:
                slope_z[moment, here] = slope
            moved = vel_z[way, here] - buoy_ref_in(turn) * slope
            vel_z[way, here] = moved
            diverge_z[here] = along_z(moved, tables[1])
            return carry

        def buoy_ref_in(turn):
            return buoy[pl.ds(turn * chunk + VRIM, chunk), mid_y]

        lax.fori_loop(0, size_x // chunk, depth_part, 0)

        if state == 0:
            receive(2 * STEPS + 2)
        if state % STEPS == 0:
            receive(2 * STEPS + way)
        receive(state)

        def along_x(i):
            slope = 0.0
            for order, weight in enumerate(coeffs):
                r = order + 1
                slope = slope + weight * (
                    press[state, i + VRIM - 1 + r, mid_y] - press[state, i + VRIM - r, mid_y]
                )
            vel_x[way, i] = vel_x[way, i] - buoy[i, mid_y] * slope
            return slope

        def ghost_low(i, carry):
            along_x(i)
            return carry

        def faces(x, carry):
            slope = along_x(x + VRIM)
            plane = press[state, x + RIM]
            slope_b = 0.0
            for order, weight in enumerate(coeffs):
                r = order + 1
                back = plane if r == 1 else pltpu.roll(plane, r - 1, 0)
                slope_b = slope_b + weight * (pltpu.roll(plane, tall - r, 0) - back)
            vel_y[way, x] = vel_y[way, x] - buoy[x + VRIM] * slope_b
            if way == 0:
                slope_x[moment, x] = slope
                slope_y[moment, x] = slope_b[PAD : PAD + size_y]
            return carry

        lax.fori_loop(0, VRIM, ghost_low, 0)
        lax.fori_loop(size_x + VRIM, size_x + 2 * VRIM - 1, ghost_low, 0)
        lax.fori_loop(0, size_x, faces, 0, unroll=2)

        def finish(k, carry):
            x = lax.rem(k + size_x - RIM, size_x)
            plane = vel_y[way, x]
            div = diverge_z[x]
            across = 0.0
            for order, weight in enumerate(coeffs):
                r = order + 1
                ahead = plane if r == 1 else pltpu.roll(plane, tall - r + 1, 0)
                across = across + weight * (ahead - pltpu.roll(plane, r, 0))
                div = div + weight * (
                    vel_x[way, x + VRIM + r - 1] - vel_x[way, x + VRIM - r]
                )
            div = div + across[PAD : PAD + size_y]
            value = press[state, x + RIM, mid_y] - mod[x] * div
            if way == 0:
                value = value + at_source * jnp.where(src_x == x, amps[moment : moment + 1], 0.0)
                residue = hits[x] * value - recorded[moment, x]
                div_at[moment, x] = div
                if moment == STEPS - 1:
                    press[state + 1, x + RIM, mid_y] = start_adj[x] + residue
                else:
                    misfit[moment, x] = residue
                    press[state + 1, x + RIM, mid_y] = value
            else:
                part_mod = value * div_at[moment, x]
                part_buoy = (
                    vel_x[way, x + VRIM] * slope_x[moment, x]
                    + plane[PAD : PAD + size_y] * slope_y[moment, x]
                    + vel_z[way, x] * slope_z[moment, x]
                )
                if moment == STEPS - 1:
                    totals[0, x] = -part_mod
                    totals[1, x] = -part_buoy
                else:
                    totals[0, x] = totals[0, x] - part_mod
                    totals[1, x] = totals[1, x] - part_buoy
                if moment > 0:
                    press[state + 1, x + RIM, mid_y] = value + misfit[moment - 1, x]
            return carry

        edge = min(2 * RIM, size_x)
        lax.fori_loop(0, edge, finish, 0, unroll=2)
        more = state + 1 < 2 * STEPS
        if more:
            send(state + 1, (0, 1))
        lax.fori_loop(edge, size_x, finish, 0, unroll=2)
        if more:
            send(state + 1, (2, 3))

    for moment in range(STEPS):
        step(moment, 0, moment)
    for turn in range(STEPS):
        step(STEPS + turn, 1, STEPS - 1 - turn)

    for h in range(halves):
        for a in range(rows_a):
            sig = gates[h, a]
            deep_y = 4 * GROUP
            here = pl.ds(h * deep_y, deep_y)
            grad_mod = jnp.concatenate([totals[0, 4 * a + i, here] for i in range(4)], axis=0)
            grad_buoy = jnp.concatenate([totals[1, 4 * a + i, here] for i in range(4)], axis=0)
            sig_speed, sig_dens = sig[: block // 2], sig[block // 2 :]
            speed = 0.15 + 0.25 * sig_speed
            density = 1.0 + 1.5 * sig_dens
            grad_speed = grad_mod * 2.0 * density * speed
            grad_dens = grad_mod * speed * speed - grad_buoy / (density * density)
            fine = jnp.concatenate(
                [
                    grad_speed * 0.25 * sig_speed * (1.0 - sig_speed),
                    grad_dens * 1.5 * sig_dens * (1.0 - sig_dens),
                ],
                axis=0,
            )
            rows = jnp.transpose(mm2(split(fine), depth_pick, rows_by_rows))
            for k in range(4):
                turned[h, pl.ds(a * cells, cells), k * block : (k + 1) * block] = rows[
                    k * cells : (k + 1) * cells
                ]
    big_gf = 0.0
    big_gs = 0.0
    scatters = []
    for h in range(halves):
        lanes = slice(h * wide, (h + 1) * wide)
        state = hidden[:, lanes]
        outer = split(turned[h])
        grad_pre = mm3(outer, big_second, rows_by_rows) * (1.0 - state * state)
        inner = split(grad_pre)
        grad_rows = mm3(inner, big_first, rows_by_rows)
        for s in range(shots):
            for a in range(rows_a):
                first = a * cells + s * depth_c
                share[s, a, :, lanes] = grad_rows[first : first + depth_c]
        for d in range(1, shots):
            there = axis_peers("shot", d)
            window = pl.ds(h * wide, wide)
            copy = remote(
                share.at[there["shot"], :, :, window],
                landed.at[me, :, :, window],
                shot_send.at[1 + h, d - 1],
                shot_recv.at[1 + h, d - 1],
                there,
            )
            copy.start()
            scatters.append(copy)
        big_gf = big_gf + mm3(split(jnp.transpose(latents[:, lanes])), inner)
        big_gs = big_gs + mm3(split(jnp.transpose(state)), outer)
    landed[me] = share[me]

    sum_f = 0.0
    sum_s = 0.0
    for b in range(GROUP):
        mine = slice(b * CH, (b + 1) * CH)
        sum_f = sum_f + jnp.where(
            one_hot((CH, wide), lambda r, c: c // CH == b), big_gf[mine], 0.0
        )
        sum_s = sum_s + jnp.where(
            one_hot((CH, 4 * block), lambda r, c: c % 16 // 4 == b), big_gs[mine], 0.0
        )
    grad_second = mm2(split(sum_s), order, rows_by_rows)
    grad_first = 0.0
    for side in range(2):
        fold = as_pick(one_hot((wide, outs), lambda r, c: r % CH + side * CH == c))
        grad_first = grad_first + mm2(
            split(sum_f[side * CH // 2 : (side + 1) * CH // 2]), fold
        )
    weights = jnp.concatenate([grad_second, grad_first], axis=0)
    piece = weights.shape[0] // shots
    for s in range(shots):
        w_share[s] = weights[s * piece : (s + 1) * piece]

    def total(stack):
        summed = stack[0]
        for n in range(1, stack.shape[0]):
            summed = summed + stack[n]
        return summed

    hops = [
        remote(
            w_share.at[axis_peers("shot", d)["shot"]],
            w_landed.at[me],
            shot_send.at[1 + halves, d - 1],
            shot_recv.at[1 + halves, d - 1],
            axis_peers("shot", d),
        )
        for d in range(1, shots)
    ]
    for hop in hops:
        hop.start()
    w_landed[me] = w_share[me]
    for hop in hops:
        hop.wait()
    spot = me_x * lax.axis_size("gy") + me_y
    w_plane[spot] = total(w_landed)
    hops = [
        remote(w_plane.at[spot], w_plane.at[spot], plane_send.at[n], plane_recv.at[n], peer)
        for n, peer in enumerate(plane_peers())
    ]
    for hop in hops:
        hop.start()
    for hop in hops:
        hop.wait()
    sums_ref[me] = total(w_plane)
    hops = [
        remote(
            sums_ref.at[me],
            sums_ref.at[me],
            shot_send.at[2 + halves, d - 1],
            shot_recv.at[2 + halves, d - 1],
            axis_peers("shot", d),
        )
        for d in range(1, shots)
    ]
    for hop in hops:
        hop.start()
    for copy in scatters:
        copy.wait()
    own_ref[...] = jnp.transpose(total(landed), (1, 0, 2))
    for hop in hops:
        hop.wait()
    for slot in range(2 * STEPS + 3):
        sent(slot)


def depth_matrices(size_z):
    source = lax.broadcasted_iota(jnp.int32, (size_z, size_z), 0)
    dest = lax.broadcasted_iota(jnp.int32, (size_z, size_z), 1)
    plus = jnp.zeros((size_z, size_z), jnp.float32)
    minus = plus
    for order, weight in enumerate(coeffs):
        r = order + 1
        plus = plus + jnp.where(source == dest + r, weight, 0.0)
        plus = plus - jnp.where(source == dest - r + 1, weight, 0.0)
        minus = minus + jnp.where(source == dest + r - 1, weight, 0.0)
        minus = minus - jnp.where(source == dest - r, weight, 0.0)
    return plus, minus


def finish_kernel(own_ref, sums_ref, latent_ref, first_ref, second_ref, joined):
    latent_ref[...] = own_ref[...]
    piece = sums_ref.shape[1]
    for s in range(sums_ref.shape[0]):
        joined[pl.ds(s * piece, piece)] = sums_ref[s]
    second_ref[...] = joined[pl.ds(0, CH)]
    packed = joined[pl.ds(CH, CH // 2)]
    first_ref[pl.ds(0, CH // 2)] = packed[:, :CH]
    first_ref[pl.ds(CH // 2, CH // 2)] = packed[:, CH:]


def body(
    latent,
    w_first,
    w_second,
    fwd_press,
    fwd_vel,
    adj_press,
    adj_vel,
    src_pos,
    src_amp,
    rec_pos,
    observed,
):
    field = fwd_press.shape[1:]
    size_x, size_y, size_z = field
    tall = size_y + 2 * PAD
    depth_c, rows_a, merged = latent.shape
    cells = size_z // 4
    shots = lax.axis_size("shot")
    tiles = lax.axis_size("gx") * lax.axis_size("gy")
    halves = size_y // (4 * GROUP)
    outs = w_second.shape[1]
    count = rec_pos.shape[2]
    anywhere = pl.BlockSpec(memory_space=pl.ANY)
    vmem = pl.BlockSpec(memory_space=pltpu.VMEM)
    slots = 2 * STEPS + 3
    piece = (CH + CH // 2) // shots

    def scratch(*shape, kind=jnp.float32):
        return pltpu.VMEM(shape, kind)

    def sems(*shape):
        return pltpu.SemaphoreType.DMA(shape)

    own, sums = pl.pallas_call(
        whole_kernel,
        out_shape=(
            jax.ShapeDtypeStruct(latent.shape, jnp.float32),
            jax.ShapeDtypeStruct((shots, piece, outs), jnp.float32),
        ),
        in_specs=[anywhere] * 11,
        out_specs=(vmem, vmem),
        scratch_shapes=[
            scratch(*w_first.shape),
            scratch(*w_second.shape),
            scratch(*src_pos.shape, kind=jnp.int32),
            scratch(*src_amp.shape),
            scratch(3, count, kind=jnp.int32),
            scratch(STEPS, count),
            scratch(*field),
            scratch(shots, *latent.shape),
            scratch(rows_a * cells, merged),
            scratch(rows_a * cells, merged),
            scratch(halves, rows_a, GROUP * outs // 4, size_z),
            scratch(*field),
            scratch(STEPS, *field),
            scratch((2 * STEPS + 1) * size_z, count, kind=half),
            scratch(*field),
            scratch(2 * STEPS, size_x + 2 * RIM, tall, size_z),
            scratch(size_x + 2 * VRIM, tall, size_z),
            scratch(2, size_x + 2 * VRIM, size_y, size_z),
            scratch(2, size_x, tall, size_z),
            scratch(2, *field),
            scratch(*field),
            scratch(STEPS - 1, *field),
            scratch(STEPS, *field),
            scratch(STEPS, *field),
            scratch(STEPS, *field),
            scratch(STEPS, *field),
            scratch(2, *field),
            scratch(halves, rows_a * cells, GROUP * outs),
            scratch(shots, rows_a, depth_c, merged),
            scratch(shots, rows_a, depth_c, merged),
            scratch(shots, piece, outs),
            scratch(shots, piece, outs),
            scratch(tiles, piece, outs),
            sems(15),
            sems(slots, 4),
            sems(slots, 4),
            sems(3 + halves, shots),
            sems(3 + halves, shots),
            sems(tiles),
            sems(tiles),
        ],
        compiler_params=pltpu.CompilerParams(
            collective_id=0, has_side_effects=True, vmem_limit_bytes=60 * 1024 * 1024
        ),
    )(
        latent,
        w_first,
        w_second,
        fwd_press[0],
        fwd_vel[0],
        adj_press[0],
        adj_vel[0],
        src_pos,
        src_amp,
        rec_pos[0],
        observed[0],
    )
    return pl.pallas_call(
        finish_kernel,
        out_shape=(
            jax.ShapeDtypeStruct(latent.shape, jnp.float32),
            jax.ShapeDtypeStruct(w_first.shape, jnp.float32),
            jax.ShapeDtypeStruct(w_second.shape, jnp.float32),
        ),
        scratch_shapes=[scratch(shots * piece, outs)],
    )(own, sums)


def solution(mesh):
    in_specs = (
        P("shot", "gx", "gy"),
        P(),
        P(),
        P("shot", "gx", "gy", None),
        P("shot", None, "gx", "gy", None),
        P("shot", "gx", "gy", None),
        P("shot", None, "gx", "gy", None),
        P(None, "shot"),
        P(None, "shot"),
        P("shot", None, None),
        P("shot", None, None),
    )
    out_specs = (P("shot", "gx", "gy"), P(), P())
    return jax.shard_map(body, mesh=mesh, in_specs=in_specs, out_specs=out_specs, check_vma=False)
```

```python
import jax
import jax.numpy as jnp
from jax import lax
from jax.experimental import pallas as pl
from jax.experimental.pallas import tpu as pltpu
from jax.sharding import PartitionSpec as P

CH = 64
STEPS = 3
RIM = 7
VRIM = 4
PAD = 8
GROUP = 4
LANES = 128

coeffs = (1225.0 / 1024.0, -245.0 / 3072.0, 49.0 / 5120.0, -5.0 / 7168.0)

rows_by_cols = (((1,), (0,)), ((), ()))
rows_by_rows = (((1,), (1,)), ((), ()))
half = jnp.bfloat16


def split(values):
    high = values.astype(half)
    return high, (values - high.astype(jnp.float32)).astype(half)


def mm(left, right, how=rows_by_cols):
    return lax.dot_general(left, right, how, preferred_element_type=jnp.float32)


def mm3(left, right, how=rows_by_cols):
    return (
        mm(left[0], right[0], how) + mm(left[1], right[0], how) + mm(left[0], right[1], how)
    )


def mm2(left, pick, how=rows_by_cols):
    return mm(left[0], pick, how) + mm(left[1], pick, how)


def one_hot(shape, rule):
    rows = lax.broadcasted_iota(jnp.int32, shape, 0)
    cols = lax.broadcasted_iota(jnp.int32, shape, 1)
    return rule(rows, cols)


def as_pick(mask):
    return jnp.where(mask, 1.0, 0.0).astype(half)


def axis_peers(axis, distance):
    count = lax.axis_size(axis)
    return {axis: lax.rem(lax.axis_index(axis) + distance, count)}


def plane_peers():
    near, wide = lax.axis_size("gy"), lax.axis_size("gx")
    for dx in range(wide):
        for dy in range(near):
            if dx or dy:
                yield {
                    "gx": lax.rem(lax.axis_index("gx") + dx, wide),
                    "gy": lax.rem(lax.axis_index("gy") + dy, near),
                }


def everyone():
    for d in range(1, lax.axis_size("shot")):
        yield axis_peers("shot", d)
    yield from plane_peers()


def remote(source, dest, send_sem, recv_sem, peer):
    return pltpu.make_async_remote_copy(
        src_ref=source,
        dst_ref=dest,
        send_sem=send_sem,
        recv_sem=recv_sem,
        device_id=peer,
        device_id_type=pl.DeviceIdType.MESH,
    )


def logistic(values):
    return 0.5 * jnp.tanh(0.5 * values) + 0.5


def whole_kernel(
    latent_ref,
    first_ref,
    second_ref,
    fwd_press,
    fwd_vel,
    adj_press,
    adj_vel,
    src_pos,
    src_amp,
    rec_pos,
    observed,
    own_ref,
    sums_ref,
    w_first,
    w_second,
    place,
    amps,
    rec_at,
    seen,
    start_adj,
    slabs,
    latents,
    hidden,
    gates,
    hits,
    recorded,
    rec_weights,
    mod,
    press,
    buoy_x,
    buoy_y,
    kicks,
    vel_x,
    vel_y,
    vel_z,
    diverge_z,
    misfit,
    div_at,
    slope_x,
    slope_y,
    slope_z,
    totals,
    turned,
    share,
    landed,
    w_share,
    w_landed,
    w_plane,
    local_sem,
    send_sem,
    recv_sem,
    shot_send,
    shot_recv,
    plane_send,
    plane_recv,
):
    size_x, size_y, size_z = mod.shape
    cells = size_z // 4
    mid_y = pl.ds(PAD, size_y)
    mid_v = pl.ds(VRIM, size_x)
    rows_a = size_x // 4
    wide = GROUP * CH
    halves = size_y // (4 * GROUP)
    shots = lax.axis_size("shot")
    me = lax.axis_index("shot")
    me_x, me_y = lax.axis_index("gx"), lax.axis_index("gy")
    has = (
        me_x > 0,
        me_x < lax.axis_size("gx") - 1,
        me_y > 0,
        me_y < lax.axis_size("gy") - 1,
    )
    target = ({"gx": me_x - 1}, {"gx": me_x + 1}, {"gy": me_y - 1}, {"gy": me_y + 1})

    barrier = pltpu.get_barrier_semaphore()
    greeted = 0
    for peer in everyone():
        pl.semaphore_signal(
            barrier, inc=1, device_id=peer, device_id_type=pl.DeviceIdType.MESH
        )
        greeted += 1

    loads = [
        (first_ref, w_first),
        (second_ref, w_second),
        (rec_pos, rec_at),
        (observed, seen),
        (src_pos, place),
        (src_amp, amps),
        (latent_ref, slabs.at[me]),
        (fwd_press, press.at[0, pl.ds(RIM, size_x), mid_y]),
        (adj_press, start_adj),
    ]
    for way, vel in enumerate((fwd_vel, adj_vel)):
        loads.append((vel.at[0], vel_x.at[way, pl.ds(VRIM, size_x)]))
        loads.append((vel.at[1], vel_y.at[way, :, pl.ds(VRIM, size_y)]))
        loads.append((vel.at[2], vel_z.at[way]))
    moves = [
        pltpu.make_async_copy(source, dest, local_sem.at[n])
        for n, (source, dest) in enumerate(loads)
    ]
    for move in moves:
        move.start()

    class Link:
        def __init__(self, slot, pairs):
            self.copies = {
                side: remote(
                    *pair,
                    send_sem.at[slot, side],
                    recv_sem.at[slot, side ^ 1],
                    target[side],
                )
                for side, pair in pairs.items()
            }

        def send(self, *sides):
            for side in sides or self.copies:
                pl.when(has[side])(self.copies[side].start)

        def receive(self, *sides):
            for side in sides or self.copies:
                pl.when(has[side])(self.copies[side ^ 1].wait_recv)

        def sent(self):
            for side in self.copies:
                pl.when(has[side])(self.copies[side].wait_send)

    def x_pairs(low, high, dest, rim):
        return {0: (low, dest(size_x + rim, rim)), 1: (high, dest(0, rim))}

    def y_pairs(low, high, dest, at_low, at_high):
        return {2: (low, dest(at_high)), 3: (high, dest(at_low))}

    slot = 0
    links_x, links_y = [], []
    spans = (pl.ds(0, RIM), pl.ds(size_x - RIM, RIM), pl.ds(RIM, size_x - 2 * RIM))
    inner = (pl.ds(RIM, RIM), pl.ds(size_x, RIM), pl.ds(2 * RIM, size_x - 2 * RIM))
    for state in range(2 * STEPS):

        def plane(first, count, state=state):
            return press.at[state, pl.ds(first, count), mid_y]

        low, high = plane(RIM, RIM), plane(size_x, RIM)
        if state == 0:
            low, high = fwd_press.at[spans[0]], fwd_press.at[spans[1]]
        links_x.append(Link(slot, x_pairs(low, high, plane, RIM)))
        slot += 1
        parts = []
        for span, rows in zip(spans, inner):

            def strip(first, state=state, rows=rows):
                return press.at[state, rows, pl.ds(first, PAD)]

            low, high = strip(PAD), strip(size_y)
            if state == 0:
                low = fwd_press.at[span, pl.ds(0, PAD)]
                high = fwd_press.at[span, pl.ds(size_y - PAD, PAD)]
            parts.append(Link(slot, y_pairs(low, high, strip, 0, size_y + PAD)))
            slot += 1
        links_y.append(parts)

    def strips(ref):
        return lambda first: ref.at[:, pl.ds(first, VRIM)]

    def layers(ref):
        return lambda first, count: ref.at[pl.ds(first, count)]

    vel_links = []
    for way, vel in enumerate((fwd_vel, adj_vel)):
        pairs = x_pairs(
            vel.at[0, pl.ds(0, VRIM)],
            vel.at[0, pl.ds(size_x - VRIM, VRIM)],
            layers(vel_x.at[way]),
            VRIM,
        )
        pairs.update(
            y_pairs(
                vel.at[1, :, pl.ds(0, VRIM)],
                vel.at[1, :, pl.ds(size_y - VRIM, VRIM)],
                strips(vel_y.at[way]),
                0,
                size_y + VRIM,
            )
        )
        vel_links.append(Link(slot, pairs))
        slot += 1
    pairs = x_pairs(
        buoy_x.at[pl.ds(VRIM, VRIM)], buoy_x.at[pl.ds(size_x, VRIM)], layers(buoy_x), VRIM
    )
    pairs.update(
        y_pairs(
            buoy_y.at[:, pl.ds(VRIM, VRIM)],
            buoy_y.at[:, pl.ds(size_y, VRIM)],
            strips(buoy_y),
            0,
            size_y + VRIM,
        )
    )
    buoy_link = Link(slot, pairs)
    links = [*links_x, *sum(links_y, []), *vel_links, buoy_link]

    for side in range(4):

        @pl.when(jnp.logical_not(has[side]))
        def _():
            far = side % 2
            if side < 2:
                rows = pl.ds(far * (size_x + RIM), RIM)
                vrows = pl.ds(far * (size_x + VRIM), VRIM)
                for state in range(2 * STEPS):
                    press[state, rows, mid_y] = jnp.zeros((RIM, size_y, size_z), jnp.float32)
                blank = jnp.zeros((VRIM, size_y, size_z), jnp.float32)
                buoy_x[vrows] = blank
                for way in range(2):
                    vel_x[way, vrows] = blank
            else:
                cols = pl.ds(far * (size_y + PAD), PAD)
                for state in range(2 * STEPS):
                    press[state, pl.ds(RIM, size_x), cols] = jnp.zeros(
                        (size_x, PAD, size_z), jnp.float32
                    )
                vcols = pl.ds(far * (size_y + VRIM), VRIM)
                blank = jnp.zeros((size_x, VRIM, size_z), jnp.float32)
                buoy_y[:, vcols] = blank
                for way in range(2):
                    vel_y[way, :, vcols] = blank

    pl.semaphore_wait(barrier, greeted)

    gathers = [
        remote(
            latent_ref,
            slabs.at[me],
            shot_send.at[0, d - 1],
            shot_recv.at[0, d - 1],
            axis_peers("shot", d),
        )
        for d in range(1, shots)
    ]
    for copy in gathers:
        copy.start()
    for link in (links_x[0], *links_y[0], *vel_links):
        link.send()
    for move in moves:
        move.wait()

    spread_rows = as_pick(one_hot((wide, CH), lambda r, c: r % CH == c))
    same_cell = one_hot((wide, wide), lambda r, c: r // CH == c // CH)
    big_first = tuple(
        jnp.where(same_cell, mm(mm(spread_rows, part).astype(half), spread_rows, rows_by_rows), 0.0)
        .astype(half)
        for part in split(w_first[...])
    )
    outs = w_second.shape[1]
    block = outs // 4 * GROUP

    def source_of(c):
        return c % block // 64 * 64 + c % 64 // 16 * 16 + c % 4 * 4 + c // block

    order = as_pick(one_hot((outs, 4 * block), lambda r, c: source_of(c) == r))
    same_out = one_hot((wide, 4 * block), lambda r, c: c % 16 // 4 == r // CH)
    big_second = tuple(
        jnp.where(same_out, mm(mm(spread_rows, part).astype(half), order), 0.0).astype(half)
        for part in split(w_second[...])
    )
    depth_pick = as_pick(one_hot((size_z, size_z), lambda r, c: 4 * (r % cells) + r // cells == c))

    count = rec_at.shape[2]
    local_x = rec_at[0] - me_x * size_x
    local_y = rec_at[1] - me_y * size_y
    inside = (local_x >= 0) & (local_x < size_x) & (local_y >= 0) & (local_y < size_y)
    column = jnp.where(inside, local_x * size_y + local_y, -1)
    deep = jnp.where(
        lax.broadcasted_iota(jnp.int32, (size_z, count), 0) == rec_at[2], 1.0, 0.0
    )
    rec_weights[pl.ds(0, size_z)] = deep.astype(half)
    for moment in range(STEPS):
        for part, values in enumerate(split(seen[moment])):
            rec_weights[pl.ds((1 + 2 * moment + part) * size_z, size_z)] = (
                deep * values.astype(jnp.float32)
            ).astype(half)
    chunk = 8 if size_x % 8 == 0 else 1
    some = chunk * size_y

    def planes(step, carry):
        index = lax.broadcasted_iota(jnp.int32, (some, count), 0) + step * some
        summed = mm(as_pick(index == column), rec_weights[...], rows_by_rows).reshape(
            chunk, size_y, (2 * STEPS + 1) * size_z
        )
        here = pl.ds(step * chunk, chunk)
        hits[here] = summed[:, :, :size_z]
        for moment in range(STEPS):
            first = (1 + 2 * moment) * size_z
            recorded[moment, here] = (
                summed[:, :, first : first + size_z]
                + summed[:, :, first + size_z : first + 2 * size_z]
            )
        return carry

    lax.fori_loop(0, size_x // chunk, planes, 0)

    src_x = place[:, 0:1] - me_x * size_x
    src_y = place[:, 1:2] - me_y * size_y
    at_source = (lax.broadcasted_iota(jnp.int32, (size_y, size_z), 0) == src_y) & (
        lax.broadcasted_iota(jnp.int32, (size_y, size_z), 1) == place[:, 2:3]
    )
    impulses = [jnp.where(at_source, amps[:, n : n + 1], 0.0) for n in range(STEPS)]

    def kick(x, carry):
        for n in range(STEPS):
            kicks[n, x] = jnp.where(src_x == x, impulses[n], 0.0)
        return carry

    lax.fori_loop(0, size_x, kick, 0)

    for copy in gathers:
        copy.wait()
    depth_c = slabs.shape[2]
    for s in range(shots):
        for a in range(rows_a):
            latents[pl.ds(a * cells + s * depth_c, depth_c)] = slabs[s, a]
    for h in range(halves):
        lanes = slice(h * wide, (h + 1) * wide)
        state = jnp.tanh(mm3(split(latents[:, lanes]), big_first))
        hidden[:, lanes] = state
        outputs = mm3(split(state), big_second)
        for a in range(rows_a):
            rows = slice(a * cells, (a + 1) * cells)
            stacked = jnp.concatenate(
                [outputs[rows, k * block : (k + 1) * block] for k in range(4)], axis=0
            )
            sig = logistic(mm2(split(jnp.transpose(stacked)), depth_pick))
            gates[h, a] = sig
            speed = 0.15 + 0.25 * sig[: block // 2]
            density = 1.0 + 1.5 * sig[block // 2 :]
            modulus = density * speed * speed
            buoyancy = 1.0 / density
            deep_y = 4 * GROUP
            for i in range(4):
                part = slice(i * deep_y, (i + 1) * deep_y)
                mod[4 * a + i, pl.ds(h * deep_y, deep_y)] = modulus[part]
                buoy_x[VRIM + 4 * a + i, pl.ds(h * deep_y, deep_y)] = buoyancy[part]
                buoy_y[4 * a + i, pl.ds(VRIM + h * deep_y, deep_y)] = buoyancy[part]
    buoy_link.send()

    along = [
        split(matrix) for matrix in depth_matrices(size_z)
    ]
    tables = [
        jnp.concatenate(
            [
                jnp.concatenate([high, low], axis=1),
                jnp.concatenate([high, jnp.zeros_like(low)], axis=1),
            ],
            axis=0,
        )
        for high, low in along
    ]

    low_rows, high_rows = (0, RIM), (size_x - RIM, size_x)
    mid_rows = (RIM, size_x - RIM)
    columns = size_y // 8

    def column_of(c, base):
        return pl.ds(pl.multiple_of(8 * c, 8) + base, 8)

    def weigh(ahead, behind):
        summed = 0.0
        for order_at, weight in enumerate(coeffs):
            summed = summed + weight * (ahead[order_at] - behind[order_at])
        return summed

    def along_z(values, table):
        flat = values.reshape(size_x * size_y, size_z)
        both = mm(jnp.concatenate(split(flat), axis=1), table)
        return (both[:, :size_z] + both[:, size_z:]).reshape(values.shape)

    def depth_part(state, way, moment):
        slope = along_z(press[state, pl.ds(RIM, size_x), mid_y], tables[0])
        if way == 0:
            slope_z[moment] = slope
        moved = vel_z[way] - buoy_x[mid_v] * slope
        vel_z[way] = moved
        diverge_z[...] = along_z(moved, tables[1])

    def faces_x(state, way, moment, first, last):
        def one(c, carry):
            here, there = column_of(c, 0), column_of(c, PAD)
            rows = {
                i: press[state, i + RIM, there] for i in range(first - 3, last + 4)
            }
            for x in range(first, last):
                slope = weigh([rows[x + r] for r in (1, 2, 3, 4)], [rows[x - r + 1] for r in (1, 2, 3, 4)])
                vel_x[way, x + VRIM, here] = (
                    vel_x[way, x + VRIM, here] - buoy_x[x + VRIM, here] * slope
                )
                if way == 0 and 0 <= x < size_x:
                    slope_x[moment, x, here] = slope
            return carry

        lax.fori_loop(0, columns, one, 0)

    def faces_y(state, way, moment, rows):
        def one(x, carry):
            def at(r):
                return press[state, x + RIM, pl.ds(VRIM + r, size_y + 2 * VRIM)]

            slope = weigh([at(r) for r in (1, 2, 3, 4)], [at(1 - r) for r in (1, 2, 3, 4)])
            vel_y[way, x] = vel_y[way, x] - buoy_y[x] * slope
            if way == 0:
                slope_y[moment, x] = slope
            return carry

        lax.fori_loop(rows[0], rows[1], one, 0, unroll=2)

    def finish(state, way, moment, rows):
        first, last = rows

        def one(c, carry):
            here, there = column_of(c, 0), column_of(c, PAD)
            speeds = {
                i: vel_x[way, i + VRIM, here] for i in range(first - VRIM, last + VRIM - 1)
            }

            def at(x, r):
                return vel_y[way, x, column_of(c, VRIM + r)]

            for x in range(first, last):
                div = diverge_z[x, here] + weigh(
                    [speeds[x + r - 1] for r in (1, 2, 3, 4)], [speeds[x - r] for r in (1, 2, 3, 4)]
                )
                div = div + weigh(
                    [at(x, r - 1) for r in (1, 2, 3, 4)], [at(x, -r) for r in (1, 2, 3, 4)]
                )
                value = press[state, x + RIM, there] - mod[x, here] * div
                if way == 0:
                    value = value + kicks[moment, x, here]
                    residue = hits[x, here] * value - recorded[moment, x, here]
                    div_at[moment, x, here] = div
                    if moment == STEPS - 1:
                        press[state + 1, x + RIM, there] = start_adj[x, here] + residue
                    else:
                        misfit[moment, x, here] = residue
                        press[state + 1, x + RIM, there] = value
                else:
                    part_mod = value * div_at[moment, x, here]
                    part_buoy = (
                        speeds[x] * slope_x[moment, x, here]
                        + at(x, 0) * slope_y[moment, x, column_of(c, VRIM)]
                        + vel_z[way, x, here] * slope_z[moment, x, here]
                    )
                    if moment == STEPS - 1:
                        totals[0, x, here] = -part_mod
                        totals[1, x, here] = -part_buoy
                    else:
                        totals[0, x, here] = totals[0, x, here] - part_mod
                        totals[1, x, here] = totals[1, x, here] - part_buoy
                    if moment > 0:
                        press[state + 1, x + RIM, there] = value + misfit[moment - 1, x, here]
            return carry

        lax.fori_loop(0, columns, one, 0)

    def step(state, way, moment):
        depth_part(state, way, moment)
        faces_x(state, way, moment, 3, size_x - 4)
        if state == 0:
            buoy_link.receive()
        if state % STEPS == 0:
            vel_links[way].receive()
        ends = [(0, low_rows, (-VRIM, 3)), (1, high_rows, (size_x - 4, size_x + 3))]
        if state % 2:
            ends.reverse()
        more = state + 1 < 2 * STEPS
        for side, rows, ghosts in ends:
            links_x[state].receive(side)
            links_y[state][side].receive()
            faces_x(state, way, moment, *ghosts)
            faces_y(state, way, moment, rows)
            finish(state, way, moment, rows)
            if more:
                links_x[state + 1].send(side)
                links_y[state + 1][side].send()
        links_y[state][2].receive()
        faces_y(state, way, moment, mid_rows)
        finish(state, way, moment, mid_rows)
        if more:
            links_y[state + 1][2].send()

    for moment in range(STEPS):
        step(moment, 0, moment)
    for turn in range(STEPS):
        step(STEPS + turn, 1, STEPS - 1 - turn)

    for h in range(halves):
        for a in range(rows_a):
            sig = gates[h, a]
            deep_y = 4 * GROUP
            here = pl.ds(h * deep_y, deep_y)
            grad_mod = jnp.concatenate([totals[0, 4 * a + i, here] for i in range(4)], axis=0)
            grad_buoy = jnp.concatenate([totals[1, 4 * a + i, here] for i in range(4)], axis=0)
            sig_speed, sig_dens = sig[: block // 2], sig[block // 2 :]
            speed = 0.15 + 0.25 * sig_speed
            density = 1.0 + 1.5 * sig_dens
            grad_speed = grad_mod * 2.0 * density * speed
            grad_dens = grad_mod * speed * speed - grad_buoy / (density * density)
            fine = jnp.concatenate(
                [
                    grad_speed * 0.25 * sig_speed * (1.0 - sig_speed),
                    grad_dens * 1.5 * sig_dens * (1.0 - sig_dens),
                ],
                axis=0,
            )
            rows = jnp.transpose(mm2(split(fine), depth_pick, rows_by_rows))
            for k in range(4):
                turned[h, pl.ds(a * cells, cells), k * block : (k + 1) * block] = rows[
                    k * cells : (k + 1) * cells
                ]
    big_gf = 0.0
    big_gs = 0.0
    scatters = []
    for h in range(halves):
        lanes = slice(h * wide, (h + 1) * wide)
        state = hidden[:, lanes]
        outer = split(turned[h])
        grad_pre = mm3(outer, big_second, rows_by_rows) * (1.0 - state * state)
        inner = split(grad_pre)
        grad_rows = mm3(inner, big_first, rows_by_rows)
        for s in range(shots):
            for a in range(rows_a):
                first = a * cells + s * depth_c
                share[s, a, :, lanes] = grad_rows[first : first + depth_c]
        for d in range(1, shots):
            there = axis_peers("shot", d)
            window = pl.ds(h * wide, wide)
            copy = remote(
                share.at[there["shot"], :, :, window],
                landed.at[me, :, :, window],
                shot_send.at[1 + h, d - 1],
                shot_recv.at[1 + h, d - 1],
                there,
            )
            copy.start()
            scatters.append(copy)
        big_gf = big_gf + mm3(split(jnp.transpose(latents[:, lanes])), inner)
        big_gs = big_gs + mm3(split(jnp.transpose(state)), outer)
    landed[me] = share[me]

    sum_f = 0.0
    sum_s = 0.0
    for b in range(GROUP):
        mine = slice(b * CH, (b + 1) * CH)
        sum_f = sum_f + jnp.where(
            one_hot((CH, wide), lambda r, c: c // CH == b), big_gf[mine], 0.0
        )
        sum_s = sum_s + jnp.where(
            one_hot((CH, 4 * block), lambda r, c: c % 16 // 4 == b), big_gs[mine], 0.0
        )
    grad_second = mm2(split(sum_s), order, rows_by_rows)
    grad_first = 0.0
    for side in range(2):
        fold = as_pick(one_hot((wide, outs), lambda r, c: r % CH + side * CH == c))
        grad_first = grad_first + mm2(
            split(sum_f[side * CH // 2 : (side + 1) * CH // 2]), fold
        )
    weights = jnp.concatenate([grad_second, grad_first], axis=0)
    piece = weights.shape[0] // shots
    for s in range(shots):
        w_share[s] = weights[s * piece : (s + 1) * piece]

    def total(stack):
        summed = stack[0]
        for n in range(1, stack.shape[0]):
            summed = summed + stack[n]
        return summed

    hops = [
        remote(
            w_share.at[axis_peers("shot", d)["shot"]],
            w_landed.at[me],
            shot_send.at[1 + halves, d - 1],
            shot_recv.at[1 + halves, d - 1],
            axis_peers("shot", d),
        )
        for d in range(1, shots)
    ]
    for hop in hops:
        hop.start()
    w_landed[me] = w_share[me]
    for hop in hops:
        hop.wait()
    spot = me_x * lax.axis_size("gy") + me_y
    w_plane[spot] = total(w_landed)
    hops = [
        remote(w_plane.at[spot], w_plane.at[spot], plane_send.at[n], plane_recv.at[n], peer)
        for n, peer in enumerate(plane_peers())
    ]
    for hop in hops:
        hop.start()
    for hop in hops:
        hop.wait()
    sums_ref[me] = total(w_plane)
    hops = [
        remote(
            sums_ref.at[me],
            sums_ref.at[me],
            shot_send.at[2 + halves, d - 1],
            shot_recv.at[2 + halves, d - 1],
            axis_peers("shot", d),
        )
        for d in range(1, shots)
    ]
    for hop in hops:
        hop.start()
    for copy in scatters:
        copy.wait()
    own_ref[...] = total(landed)
    for hop in hops:
        hop.wait()
    for link in links:
        link.sent()


def depth_matrices(size_z):
    source = lax.broadcasted_iota(jnp.int32, (size_z, size_z), 0)
    dest = lax.broadcasted_iota(jnp.int32, (size_z, size_z), 1)
    plus = jnp.zeros((size_z, size_z), jnp.float32)
    minus = plus
    for order, weight in enumerate(coeffs):
        r = order + 1
        plus = plus + jnp.where(source == dest + r, weight, 0.0)
        plus = plus - jnp.where(source == dest - r + 1, weight, 0.0)
        minus = minus + jnp.where(source == dest + r - 1, weight, 0.0)
        minus = minus - jnp.where(source == dest - r, weight, 0.0)
    return plus, minus


def finish_kernel(own_ref, sums_ref, latent_ref, first_ref, second_ref, joined):
    latent_ref[...] = own_ref[...]
    piece = sums_ref.shape[1]
    for s in range(sums_ref.shape[0]):
        joined[pl.ds(s * piece, piece)] = sums_ref[s]
    second_ref[...] = joined[pl.ds(0, CH)]
    packed = joined[pl.ds(CH, CH // 2)]
    first_ref[pl.ds(0, CH // 2)] = packed[:, :CH]
    first_ref[pl.ds(CH // 2, CH // 2)] = packed[:, CH:]


def body(
    latent,
    w_first,
    w_second,
    fwd_press,
    fwd_vel,
    adj_press,
    adj_vel,
    src_pos,
    src_amp,
    rec_pos,
    observed,
):
    field = fwd_press.shape[1:]
    size_x, size_y, size_z = field
    tall = size_y + 2 * PAD
    depth_c, rows_a, merged = latent.shape
    cells = size_z // 4
    shots = lax.axis_size("shot")
    tiles = lax.axis_size("gx") * lax.axis_size("gy")
    halves = size_y // (4 * GROUP)
    outs = w_second.shape[1]
    count = rec_pos.shape[2]
    anywhere = pl.BlockSpec(memory_space=pl.ANY)
    vmem = pl.BlockSpec(memory_space=pltpu.VMEM)
    slots = 4 * 2 * STEPS + 3
    piece = (CH + CH // 2) // shots

    def scratch(*shape, kind=jnp.float32):
        return pltpu.VMEM(shape, kind)

    def sems(*shape):
        return pltpu.SemaphoreType.DMA(shape)

    own, sums = pl.pallas_call(
        whole_kernel,
        out_shape=(
            jax.ShapeDtypeStruct((rows_a, depth_c, merged), jnp.float32),
            jax.ShapeDtypeStruct((shots, piece, outs), jnp.float32),
        ),
        in_specs=[anywhere] * 11,
        out_specs=(vmem, vmem),
        scratch_shapes=[
            scratch(*w_first.shape),
            scratch(*w_second.shape),
            scratch(*src_pos.shape[::-1], kind=jnp.int32),
            scratch(*src_amp.shape[::-1]),
            scratch(3, 1, count, kind=jnp.int32),
            scratch(STEPS, 1, count),
            scratch(*field),
            scratch(shots, rows_a, depth_c, merged),
            scratch(rows_a * cells, merged),
            scratch(rows_a * cells, merged),
            scratch(halves, rows_a, GROUP * outs // 4, size_z),
            scratch(*field),
            scratch(STEPS, *field),
            scratch((2 * STEPS + 1) * size_z, count, kind=half),
            scratch(*field),
            scratch(2 * STEPS, size_x + 2 * RIM, tall, size_z),
            scratch(size_x + 2 * VRIM, size_y, size_z),
            scratch(size_x, size_y + 2 * VRIM, size_z),
            scratch(STEPS, *field),
            scratch(2, size_x + 2 * VRIM, size_y, size_z),
            scratch(2, size_x, size_y + 2 * VRIM, size_z),
            scratch(2, *field),
            scratch(*field),
            scratch(STEPS - 1, *field),
            scratch(STEPS, *field),
            scratch(STEPS, *field),
            scratch(STEPS, size_x, size_y + 2 * VRIM, size_z),
            scratch(STEPS, *field),
            scratch(2, *field),
            scratch(halves, rows_a * cells, GROUP * outs),
            scratch(shots, rows_a, depth_c, merged),
            scratch(shots, rows_a, depth_c, merged),
            scratch(shots, piece, outs),
            scratch(shots, piece, outs),
            scratch(tiles, piece, outs),
            sems(15),
            sems(slots, 4),
            sems(slots, 4),
            sems(3 + halves, shots),
            sems(3 + halves, shots),
            sems(tiles),
            sems(tiles),
        ],
        compiler_params=pltpu.CompilerParams(
            collective_id=0, has_side_effects=True, vmem_limit_bytes=60 * 1024 * 1024
        ),
    )(
        latent.transpose(1, 0, 2),
        w_first,
        w_second,
        fwd_press[0],
        fwd_vel[0],
        adj_press[0],
        adj_vel[0],
        src_pos.T,
        src_amp.T,
        rec_pos.transpose(1, 0, 2),
        observed.transpose(1, 0, 2),
    )
    grad_latent, grad_first, grad_second = pl.pallas_call(
        finish_kernel,
        out_shape=(
            jax.ShapeDtypeStruct(own.shape, jnp.float32),
            jax.ShapeDtypeStruct(w_first.shape, jnp.float32),
            jax.ShapeDtypeStruct(w_second.shape, jnp.float32),
        ),
        scratch_shapes=[scratch(shots * piece, outs)],
    )(own, sums)
    return grad_latent.transpose(1, 0, 2), grad_first, grad_second


def solution(mesh):
    in_specs = (
        P("shot", "gx", "gy"),
        P(),
        P(),
        P("shot", "gx", "gy", None),
        P("shot", None, "gx", "gy", None),
        P("shot", "gx", "gy", None),
        P("shot", None, "gx", "gy", None),
        P(None, "shot"),
        P(None, "shot"),
        P("shot", None, None),
        P("shot", None, None),
    )
    out_specs = (P("shot", "gx", "gy"), P(), P())
    return jax.shard_map(body, mesh=mesh, in_specs=in_specs, out_specs=out_specs, check_vma=False)
```

```python
import jax
import jax.numpy as jnp
from jax import lax
from jax.experimental import pallas as pl
from jax.experimental.pallas import tpu as pltpu
from jax.sharding import PartitionSpec as P

CH = 64
STEPS = 3
RIM = 7
VRIM = 4
PAD = 8
GROUP = 4
PARTS = 2
LANES = 128

coeffs = (1225.0 / 1024.0, -245.0 / 3072.0, 49.0 / 5120.0, -5.0 / 7168.0)

rows_by_cols = (((1,), (0,)), ((), ()))
rows_by_rows = (((1,), (1,)), ((), ()))
half = jnp.bfloat16


def split(values):
    high = values.astype(half)
    return high, (values - high.astype(jnp.float32)).astype(half)


def mm(left, right, how=rows_by_cols):
    return lax.dot_general(left, right, how, preferred_element_type=jnp.float32)


def mm3(left, right, how=rows_by_cols):
    return (
        mm(left[0], right[0], how) + mm(left[1], right[0], how) + mm(left[0], right[1], how)
    )


def mm2(left, pick, how=rows_by_cols):
    return mm(left[0], pick, how) + mm(left[1], pick, how)


def one_hot(shape, rule):
    rows = lax.broadcasted_iota(jnp.int32, shape, 0)
    cols = lax.broadcasted_iota(jnp.int32, shape, 1)
    return rule(rows, cols)


def as_pick(mask):
    return jnp.where(mask, 1.0, 0.0).astype(half)


def axis_peers(axis, distance):
    count = lax.axis_size(axis)
    return {axis: lax.rem(lax.axis_index(axis) + distance, count)}


def plane_peers():
    near, wide = lax.axis_size("gy"), lax.axis_size("gx")
    for dx in range(wide):
        for dy in range(near):
            if dx or dy:
                yield {
                    "gx": lax.rem(lax.axis_index("gx") + dx, wide),
                    "gy": lax.rem(lax.axis_index("gy") + dy, near),
                }


def everyone():
    for d in range(1, lax.axis_size("shot")):
        yield axis_peers("shot", d)
    yield from plane_peers()


def remote(source, dest, send_sem, recv_sem, peer):
    return pltpu.make_async_remote_copy(
        src_ref=source,
        dst_ref=dest,
        send_sem=send_sem,
        recv_sem=recv_sem,
        device_id=peer,
        device_id_type=pl.DeviceIdType.MESH,
    )


def logistic(values):
    return 0.5 * jnp.tanh(0.5 * values) + 0.5


def whole_kernel(
    latent_ref,
    first_ref,
    second_ref,
    fwd_press,
    fwd_vel,
    adj_press,
    adj_vel,
    src_pos,
    src_amp,
    rec_pos,
    observed,
    own_ref,
    sums_ref,
    w_first,
    w_second,
    place,
    amps,
    rec_at,
    seen,
    start_adj,
    slabs,
    latents,
    hidden,
    gates,
    hits,
    recorded,
    rec_weights,
    mod,
    press,
    buoy_x,
    buoy_y,
    kicks,
    vel_x,
    vel_y,
    vel_z,
    diverge_z,
    misfit,
    div_at,
    slope_x,
    slope_y,
    slope_z,
    totals,
    turned,
    share,
    paired,
    summed,
    landed,
    w_share,
    w_landed,
    w_plane,
    local_sem,
    send_sem,
    recv_sem,
    shot_send,
    shot_recv,
    plane_send,
    plane_recv,
):
    size_x, size_y, size_z = mod.shape
    cells = size_z // 4
    mid_y = pl.ds(PAD, size_y)
    mid_v = pl.ds(VRIM, size_x)
    rows_a = size_x // 4
    wide = GROUP * CH
    halves = size_y // (4 * GROUP)
    shots = lax.axis_size("shot")
    me = lax.axis_index("shot")
    me_x, me_y = lax.axis_index("gx"), lax.axis_index("gy")
    has = (
        me_x > 0,
        me_x < lax.axis_size("gx") - 1,
        me_y > 0,
        me_y < lax.axis_size("gy") - 1,
    )
    target = ({"gx": me_x - 1}, {"gx": me_x + 1}, {"gy": me_y - 1}, {"gy": me_y + 1})

    barrier = pltpu.get_barrier_semaphore()
    greeted = 0
    for peer in everyone():
        pl.semaphore_signal(
            barrier, inc=1, device_id=peer, device_id_type=pl.DeviceIdType.MESH
        )
        greeted += 1

    loads = [
        (latent_ref, slabs.at[me]),
        (first_ref, w_first),
        (second_ref, w_second),
        (rec_pos, rec_at),
        (observed, seen),
        (src_pos, place),
        (src_amp, amps),
        (fwd_press, press.at[0, pl.ds(RIM, size_x), mid_y]),
        (adj_press, start_adj),
    ]
    for way, vel in enumerate((fwd_vel, adj_vel)):
        loads.append((vel.at[0], vel_x.at[way, pl.ds(VRIM, size_x)]))
        loads.append((vel.at[1], vel_y.at[way, :, pl.ds(VRIM, size_y)]))
        loads.append((vel.at[2], vel_z.at[way]))
    moves = [
        pltpu.make_async_copy(source, dest, local_sem.at[n])
        for n, (source, dest) in enumerate(loads)
    ]
    for move in moves:
        move.start()

    class Link:
        def __init__(self, slot, pairs):
            self.copies = {
                side: remote(
                    *pair,
                    send_sem.at[slot, side],
                    recv_sem.at[slot, side ^ 1],
                    target[side],
                )
                for side, pair in pairs.items()
            }

        def send(self, *sides):
            for side in sides or self.copies:
                pl.when(has[side])(self.copies[side].start)

        def receive(self, *sides):
            for side in sides or self.copies:
                pl.when(has[side])(self.copies[side ^ 1].wait_recv)

        def sent(self):
            for side in self.copies:
                pl.when(has[side])(self.copies[side].wait_send)

    def x_pairs(low, high, dest, rim):
        return {0: (low, dest(size_x + rim, rim)), 1: (high, dest(0, rim))}

    def y_pairs(low, high, dest, at_low, at_high):
        return {2: (low, dest(at_high)), 3: (high, dest(at_low))}

    slot = 0
    links_x, links_y = [], []
    deep_part = size_y // PARTS
    spans = (pl.ds(0, RIM), pl.ds(size_x - RIM, RIM), pl.ds(RIM, size_x - 2 * RIM))
    inner = (pl.ds(RIM, RIM), pl.ds(size_x, RIM), pl.ds(2 * RIM, size_x - 2 * RIM))
    for state in range(2 * STEPS):
        parts = []
        for part in range(PARTS):
            inside = pl.ds(part * deep_part, deep_part)

            def plane(first, count, state=state, part=part):
                return press.at[
                    state, pl.ds(first, count), pl.ds(PAD + part * deep_part, deep_part)
                ]

            low, high = plane(RIM, RIM), plane(size_x, RIM)
            if state == 0:
                low, high = fwd_press.at[spans[0], inside], fwd_press.at[spans[1], inside]
            parts.append(Link(slot, x_pairs(low, high, plane, RIM)))
            slot += 1
        links_x.append(parts)
        parts = []
        for span, rows in zip(spans, inner):

            def strip(first, state=state, rows=rows):
                return press.at[state, rows, pl.ds(first, PAD)]

            low, high = strip(PAD), strip(size_y)
            if state == 0:
                low = fwd_press.at[span, pl.ds(0, PAD)]
                high = fwd_press.at[span, pl.ds(size_y - PAD, PAD)]
            parts.append(Link(slot, y_pairs(low, high, strip, 0, size_y + PAD)))
            slot += 1
        links_y.append(parts)

    def strips(ref):
        return lambda first: ref.at[:, pl.ds(first, VRIM)]

    def layers(ref):
        return lambda first, count: ref.at[pl.ds(first, count)]

    vel_links = []
    for way, vel in enumerate((fwd_vel, adj_vel)):
        pairs = x_pairs(
            vel.at[0, pl.ds(0, VRIM)],
            vel.at[0, pl.ds(size_x - VRIM, VRIM)],
            layers(vel_x.at[way]),
            VRIM,
        )
        pairs.update(
            y_pairs(
                vel.at[1, :, pl.ds(0, VRIM)],
                vel.at[1, :, pl.ds(size_y - VRIM, VRIM)],
                strips(vel_y.at[way]),
                0,
                size_y + VRIM,
            )
        )
        vel_links.append(Link(slot, pairs))
        slot += 1
    pairs = x_pairs(
        buoy_x.at[pl.ds(VRIM, VRIM)], buoy_x.at[pl.ds(size_x, VRIM)], layers(buoy_x), VRIM
    )
    pairs.update(
        y_pairs(
            buoy_y.at[:, pl.ds(VRIM, VRIM)],
            buoy_y.at[:, pl.ds(size_y, VRIM)],
            strips(buoy_y),
            0,
            size_y + VRIM,
        )
    )
    buoy_link = Link(slot, pairs)
    links = [*sum(links_x, []), *sum(links_y, []), *vel_links, buoy_link]

    for side in range(4):

        @pl.when(jnp.logical_not(has[side]))
        def _():
            far = side % 2
            if side < 2:
                rows = pl.ds(far * (size_x + RIM), RIM)
                vrows = pl.ds(far * (size_x + VRIM), VRIM)
                for state in range(2 * STEPS):
                    press[state, rows, mid_y] = jnp.zeros((RIM, size_y, size_z), jnp.float32)
                blank = jnp.zeros((VRIM, size_y, size_z), jnp.float32)
                buoy_x[vrows] = blank
                for way in range(2):
                    vel_x[way, vrows] = blank
            else:
                cols = pl.ds(far * (size_y + PAD), PAD)
                for state in range(2 * STEPS):
                    press[state, pl.ds(RIM, size_x), cols] = jnp.zeros(
                        (size_x, PAD, size_z), jnp.float32
                    )
                vcols = pl.ds(far * (size_y + VRIM), VRIM)
                blank = jnp.zeros((size_x, VRIM, size_z), jnp.float32)
                buoy_y[:, vcols] = blank
                for way in range(2):
                    vel_y[way, :, vcols] = blank

    pl.semaphore_wait(barrier, greeted)

    moves[0].wait()
    gathers = [
        remote(
            slabs.at[me],
            slabs.at[me],
            shot_send.at[0, d - 1],
            shot_recv.at[0, d - 1],
            axis_peers("shot", d),
        )
        for d in range(1, shots)
    ]
    for copy in gathers:
        copy.start()
    for link in (*links_x[0], *links_y[0], *vel_links):
        link.send()
    for move in moves[1:]:
        move.wait()

    spread_rows = as_pick(one_hot((wide, CH), lambda r, c: r % CH == c))
    same_cell = one_hot((wide, wide), lambda r, c: r // CH == c // CH)
    big_first = tuple(
        jnp.where(same_cell, mm(mm(spread_rows, part).astype(half), spread_rows, rows_by_rows), 0.0)
        .astype(half)
        for part in split(w_first[...])
    )
    outs = w_second.shape[1]
    block = outs // 4 * GROUP

    def source_of(c):
        return c % block // 64 * 64 + c % 64 // 16 * 16 + c % 4 * 4 + c // block

    order = as_pick(one_hot((outs, 4 * block), lambda r, c: source_of(c) == r))
    same_out = one_hot((wide, 4 * block), lambda r, c: c % 16 // 4 == r // CH)
    big_second = tuple(
        jnp.where(same_out, mm(mm(spread_rows, part).astype(half), order), 0.0).astype(half)
        for part in split(w_second[...])
    )
    to_depth = as_pick(
        one_hot((2 * size_z, size_z), lambda r, c: 4 * (r % cells) + r % size_z // cells == c)
    )
    from_depth = as_pick(
        one_hot((2 * size_z, size_z), lambda r, c: 4 * (c % cells) + c // cells == r % size_z)
    )

    def side_by_side(values):
        return jnp.concatenate(split(values), axis=1)


    count = rec_at.shape[2]
    local_x = rec_at[0] - me_x * size_x
    local_y = rec_at[1] - me_y * size_y
    inside = (local_x >= 0) & (local_x < size_x) & (local_y >= 0) & (local_y < size_y)
    column = jnp.where(inside, local_x * size_y + local_y, -1)
    deep = jnp.where(
        lax.broadcasted_iota(jnp.int32, (size_z, count), 0) == rec_at[2], 1.0, 0.0
    )
    rec_weights[pl.ds(0, size_z)] = deep.astype(half)
    for moment in range(STEPS):
        for part, values in enumerate(split(seen[moment])):
            rec_weights[pl.ds((1 + 2 * moment + part) * size_z, size_z)] = (
                deep * values.astype(jnp.float32)
            ).astype(half)
    chunk = 8 if size_x % 8 == 0 else 1
    some = chunk * size_y

    def planes(step, carry):
        index = lax.broadcasted_iota(jnp.int32, (some, count), 0) + step * some
        summed = mm(as_pick(index == column), rec_weights[...], rows_by_rows).reshape(
            chunk, size_y, (2 * STEPS + 1) * size_z
        )
        here = pl.ds(step * chunk, chunk)
        hits[here] = summed[:, :, :size_z]
        for moment in range(STEPS):
            first = (1 + 2 * moment) * size_z
            recorded[moment, here] = (
                summed[:, :, first : first + size_z]
                + summed[:, :, first + size_z : first + 2 * size_z]
            )
        return carry

    lax.fori_loop(0, size_x // chunk, planes, 0)

    src_x = place[:, 0:1] - me_x * size_x
    src_y = place[:, 1:2] - me_y * size_y
    at_source = (lax.broadcasted_iota(jnp.int32, (size_y, size_z), 0) == src_y) & (
        lax.broadcasted_iota(jnp.int32, (size_y, size_z), 1) == place[:, 2:3]
    )
    impulses = [jnp.where(at_source, amps[:, n : n + 1], 0.0) for n in range(STEPS)]

    def kick(x, carry):
        for n in range(STEPS):
            kicks[n, x] = jnp.where(src_x == x, impulses[n], 0.0)
        return carry

    lax.fori_loop(0, size_x, kick, 0)

    for copy in gathers:
        copy.wait()
    depth_c = slabs.shape[2]
    for s in range(shots):
        for a in range(rows_a):
            for h in range(halves):
                latents[pl.ds((h * rows_a + a) * cells + s * depth_c, depth_c)] = slabs[
                    s, a, :, h * wide : (h + 1) * wide
                ]
    hidden[...] = jnp.tanh(mm3(split(latents[...]), big_first))
    outputs = mm3(split(hidden[...]), big_second)
    blocks = [(h, a) for h in range(halves) for a in range(rows_a)]
    stacked = jnp.concatenate(
        [
            jnp.transpose(
                jnp.concatenate(
                    [
                        outputs[n * cells : (n + 1) * cells, k * block : (k + 1) * block]
                        for k in range(4)
                    ],
                    axis=0,
                )
            )
            for n in range(len(blocks))
        ],
        axis=0,
    )
    gates[...] = logistic(mm(side_by_side(stacked), to_depth)).reshape(gates.shape)
    deep_y = 4 * GROUP
    for n, (h, a) in enumerate(blocks):
        sig = gates[n]
        speed = 0.15 + 0.25 * sig[: block // 2]
        density = 1.0 + 1.5 * sig[block // 2 :]
        modulus = density * speed * speed
        buoyancy = 1.0 / density
        for i in range(4):
            part = slice(i * deep_y, (i + 1) * deep_y)
            mod[4 * a + i, pl.ds(h * deep_y, deep_y)] = modulus[part]
            buoy_x[VRIM + 4 * a + i, pl.ds(h * deep_y, deep_y)] = buoyancy[part]
            buoy_y[4 * a + i, pl.ds(VRIM + h * deep_y, deep_y)] = buoyancy[part]
    buoy_link.send()

    along = [
        split(matrix) for matrix in depth_matrices(size_z)
    ]
    tables = [
        jnp.concatenate(
            [
                jnp.concatenate([high, low], axis=1),
                jnp.concatenate([high, jnp.zeros_like(low)], axis=1),
            ],
            axis=0,
        )
        for high, low in along
    ]

    low_rows, high_rows = (0, RIM), (size_x - RIM, size_x)
    mid_rows = (RIM, size_x - RIM)
    columns = size_y // 8

    def column_of(c, base):
        return pl.ds(pl.multiple_of(8 * c, 8) + base, 8)

    def weigh(ahead, behind):
        summed = 0.0
        for order_at, weight in enumerate(coeffs):
            summed = summed + weight * (ahead[order_at] - behind[order_at])
        return summed

    def along_z(values, table):
        flat = values.reshape(size_x * size_y, size_z)
        both = mm(jnp.concatenate(split(flat), axis=1), table)
        return (both[:, :size_z] + both[:, size_z:]).reshape(values.shape)

    def depth_part(state, way, moment):
        slope = along_z(press[state, pl.ds(RIM, size_x), mid_y], tables[0])
        if way == 0:
            slope_z[moment] = slope
        moved = vel_z[way] - buoy_x[mid_v] * slope
        vel_z[way] = moved
        diverge_z[...] = along_z(moved, tables[1])

    def faces_x(state, way, moment, first, last, span):
        def one(c, carry):
            here, there = column_of(c, 0), column_of(c, PAD)
            rows = {
                i: press[state, i + RIM, there] for i in range(first - 3, last + 4)
            }
            for x in range(first, last):
                slope = weigh([rows[x + r] for r in (1, 2, 3, 4)], [rows[x - r + 1] for r in (1, 2, 3, 4)])
                vel_x[way, x + VRIM, here] = (
                    vel_x[way, x + VRIM, here] - buoy_x[x + VRIM, here] * slope
                )
                if way == 0 and 0 <= x < size_x:
                    slope_x[moment, x, here] = slope
            return carry

        lax.fori_loop(*span, one, 0)

    def faces_y(state, way, moment, rows):
        def one(x, carry):
            def at(r):
                return press[state, x + RIM, pl.ds(VRIM + r, size_y + 2 * VRIM)]

            slope = weigh([at(r) for r in (1, 2, 3, 4)], [at(1 - r) for r in (1, 2, 3, 4)])
            vel_y[way, x] = vel_y[way, x] - buoy_y[x] * slope
            if way == 0:
                slope_y[moment, x] = slope
            return carry

        lax.fori_loop(rows[0], rows[1], one, 0, unroll=2)

    def finish(state, way, moment, rows, span):
        first, last = rows

        def one(c, carry):
            here, there = column_of(c, 0), column_of(c, PAD)
            speeds = {
                i: vel_x[way, i + VRIM, here] for i in range(first - VRIM, last + VRIM - 1)
            }

            def at(x, r):
                return vel_y[way, x, column_of(c, VRIM + r)]

            for x in range(first, last):
                div = diverge_z[x, here] + weigh(
                    [speeds[x + r - 1] for r in (1, 2, 3, 4)], [speeds[x - r] for r in (1, 2, 3, 4)]
                )
                div = div + weigh(
                    [at(x, r - 1) for r in (1, 2, 3, 4)], [at(x, -r) for r in (1, 2, 3, 4)]
                )
                value = press[state, x + RIM, there] - mod[x, here] * div
                if way == 0:
                    value = value + kicks[moment, x, here]
                    residue = hits[x, here] * value - recorded[moment, x, here]
                    div_at[moment, x, here] = div
                    if moment == STEPS - 1:
                        press[state + 1, x + RIM, there] = start_adj[x, here] + residue
                    else:
                        misfit[moment, x, here] = residue
                        press[state + 1, x + RIM, there] = value
                else:
                    part_mod = value * div_at[moment, x, here]
                    part_buoy = (
                        speeds[x] * slope_x[moment, x, here]
                        + at(x, 0) * slope_y[moment, x, column_of(c, VRIM)]
                        + vel_z[way, x, here] * slope_z[moment, x, here]
                    )
                    if moment == STEPS - 1:
                        totals[0, x, here] = -part_mod
                        totals[1, x, here] = -part_buoy
                    else:
                        totals[0, x, here] = totals[0, x, here] - part_mod
                        totals[1, x, here] = totals[1, x, here] - part_buoy
                    if moment > 0:
                        press[state + 1, x + RIM, there] = value + misfit[moment - 1, x, here]
            return carry

        lax.fori_loop(*span, one, 0)

    every = (0, columns)
    pieces = [(n * columns // PARTS, (n + 1) * columns // PARTS) for n in range(PARTS)]

    def step(state, way, moment):
        depth_part(state, way, moment)
        faces_x(state, way, moment, 3, size_x - 4, every)
        if state == 0:
            buoy_link.receive()
        if state % STEPS == 0:
            vel_links[way].receive()
        ends = [(0, low_rows, (-VRIM, 3)), (1, high_rows, (size_x - 4, size_x + 3))]
        if state % 2:
            ends.reverse()
        more = state + 1 < 2 * STEPS
        for side, rows, ghosts in ends:
            links_y[state][side].receive()
            faces_y(state, way, moment, rows)
            for part, span in enumerate(pieces):
                links_x[state][part].receive(side)
                faces_x(state, way, moment, *ghosts, span)
                finish(state, way, moment, rows, span)
                if more:
                    links_x[state + 1][part].send(side)
            if more:
                links_y[state + 1][side].send()
        links_y[state][2].receive()
        faces_y(state, way, moment, mid_rows)
        finish(state, way, moment, mid_rows, every)
        if more:
            links_y[state + 1][2].send()

    for moment in range(STEPS):
        step(moment, 0, moment)
    for turn in range(STEPS):
        step(STEPS + turn, 1, STEPS - 1 - turn)

    for n, (h, a) in enumerate(blocks):
        sig = gates[n]
        here = pl.ds(h * deep_y, deep_y)
        grad_mod = jnp.concatenate([totals[0, 4 * a + i, here] for i in range(4)], axis=0)
        grad_buoy = jnp.concatenate([totals[1, 4 * a + i, here] for i in range(4)], axis=0)
        sig_speed, sig_dens = sig[: block // 2], sig[block // 2 :]
        speed = 0.15 + 0.25 * sig_speed
        density = 1.0 + 1.5 * sig_dens
        grad_speed = grad_mod * 2.0 * density * speed
        grad_dens = grad_mod * speed * speed - grad_buoy / (density * density)
        gates[n, pl.ds(0, block // 2)] = grad_speed * 0.25 * sig_speed * (1.0 - sig_speed)
        gates[n, pl.ds(block // 2, block // 2)] = grad_dens * 1.5 * sig_dens * (1.0 - sig_dens)
    permuted = mm(side_by_side(gates[...].reshape(len(blocks) * block, size_z)), from_depth)
    for n in range(len(blocks)):
        rows = jnp.transpose(permuted[n * block : (n + 1) * block])
        for k in range(4):
            turned[pl.ds(n * cells, cells), k * block : (k + 1) * block] = rows[
                k * cells : (k + 1) * cells
            ]
    outer = split(turned[...])
    inner = split(
        mm3(outer, big_second, rows_by_rows) * (1.0 - hidden[...] * hidden[...])
    )
    big_gf = mm3(split(jnp.transpose(latents[...])), inner)
    big_gs = mm3(split(jnp.transpose(hidden[...])), outer)
    sum_f = 0.0
    sum_s = 0.0
    for b in range(GROUP):
        mine = slice(b * CH, (b + 1) * CH)
        sum_f = sum_f + jnp.where(
            one_hot((CH, wide), lambda r, c: c // CH == b), big_gf[mine], 0.0
        )
        sum_s = sum_s + jnp.where(
            one_hot((CH, 4 * block), lambda r, c: c % 16 // 4 == b), big_gs[mine], 0.0
        )
    grad_second = mm2(split(sum_s), order, rows_by_rows)
    grad_first = 0.0
    for side in range(2):
        fold = as_pick(one_hot((wide, outs), lambda r, c: r % CH + side * CH == c))
        grad_first = grad_first + mm2(
            split(sum_f[side * CH // 2 : (side + 1) * CH // 2]), fold
        )
    weights = jnp.concatenate([grad_second, grad_first], axis=0)

    def total(stack):
        summed = stack[0]
        for n in range(1, stack.shape[0]):
            summed = summed + stack[n]
        return summed

    peers = list(plane_peers())
    tiles = len(peers) + 1
    spot = me_x * lax.axis_size("gy") + me_y
    piece = weights.shape[0] // tiles
    for n in range(tiles):
        w_share[n] = weights[n * piece : (n + 1) * piece]
    first_hops = [
        remote(
            w_share.at[peer["gx"] * lax.axis_size("gy") + peer["gy"]],
            w_landed.at[spot],
            plane_send.at[0, n],
            plane_recv.at[0, n],
            peer,
        )
        for n, peer in enumerate(peers)
    ]
    for hop in first_hops:
        hop.start()
    w_landed[spot] = w_share[spot]

    grad_rows = mm3(inner, big_first, rows_by_rows)
    for n, (h, a) in enumerate(blocks):
        for s in range(shots):
            first = n * cells + s * depth_c
            share[s % 2, s // 2, a, :, h * wide : (h + 1) * wide] = grad_rows[
                first : first + depth_c
            ]
    mate = lax.rem(me, 2)
    group = me // 2
    other = 1 - mate
    swap = remote(
        share.at[other],
        paired,
        shot_send.at[1, 0],
        shot_recv.at[1, 0],
        {"shot": 2 * group + other},
    )
    swap.start()
    for hop in first_hops:
        hop.wait()
    w_plane[me] = total(w_landed)
    second_hops = [
        remote(
            w_plane.at[me],
            w_plane.at[me],
            shot_send.at[2, d - 1],
            shot_recv.at[2, d - 1],
            axis_peers("shot", d),
        )
        for d in range(1, shots)
    ]
    for hop in second_hops:
        hop.start()
    swap.wait()
    groups = shots // 2
    for g in range(groups):
        summed[g] = share[mate, g] + paired[g]
    scatters = []
    for d in range(1, groups):
        there = lax.rem(group + d, groups)
        scatters.append(
            remote(
                summed.at[there],
                landed.at[group],
                shot_send.at[3, d - 1],
                shot_recv.at[3, d - 1],
                {"shot": 2 * there + mate},
            )
        )
    for copy in scatters:
        copy.start()
    landed[group] = summed[group]
    for hop in second_hops:
        hop.wait()
    sums_ref[spot] = total(w_plane)
    third_hops = [
        remote(
            sums_ref.at[spot], sums_ref.at[spot], plane_send.at[1, n], plane_recv.at[1, n], peer
        )
        for n, peer in enumerate(peers)
    ]
    for hop in third_hops:
        hop.start()
    for copy in scatters:
        copy.wait()
    own_ref[...] = total(landed)
    for hop in third_hops:
        hop.wait()
    for link in links:
        link.sent()


def depth_matrices(size_z):
    source = lax.broadcasted_iota(jnp.int32, (size_z, size_z), 0)
    dest = lax.broadcasted_iota(jnp.int32, (size_z, size_z), 1)
    plus = jnp.zeros((size_z, size_z), jnp.float32)
    minus = plus
    for order, weight in enumerate(coeffs):
        r = order + 1
        plus = plus + jnp.where(source == dest + r, weight, 0.0)
        plus = plus - jnp.where(source == dest - r + 1, weight, 0.0)
        minus = minus + jnp.where(source == dest + r - 1, weight, 0.0)
        minus = minus - jnp.where(source == dest - r, weight, 0.0)
    return plus, minus


def finish_kernel(own_ref, sums_ref, latent_ref, first_ref, second_ref, joined):
    latent_ref[...] = own_ref[...]
    piece = sums_ref.shape[1]
    for s in range(sums_ref.shape[0]):
        joined[pl.ds(s * piece, piece)] = sums_ref[s]
    second_ref[...] = joined[pl.ds(0, CH)]
    packed = joined[pl.ds(CH, CH // 2)]
    first_ref[pl.ds(0, CH // 2)] = packed[:, :CH]
    first_ref[pl.ds(CH // 2, CH // 2)] = packed[:, CH:]


def body(
    latent,
    w_first,
    w_second,
    fwd_press,
    fwd_vel,
    adj_press,
    adj_vel,
    src_pos,
    src_amp,
    rec_pos,
    observed,
):
    field = fwd_press.shape[1:]
    size_x, size_y, size_z = field
    tall = size_y + 2 * PAD
    depth_c, rows_a, merged = latent.shape
    cells = size_z // 4
    shots = lax.axis_size("shot")
    tiles = lax.axis_size("gx") * lax.axis_size("gy")
    halves = size_y // (4 * GROUP)
    outs = w_second.shape[1]
    count = rec_pos.shape[2]
    anywhere = pl.BlockSpec(memory_space=pl.ANY)
    vmem = pl.BlockSpec(memory_space=pltpu.VMEM)
    slots = (3 + PARTS) * 2 * STEPS + 3
    piece = (CH + CH // 2) // tiles

    def scratch(*shape, kind=jnp.float32):
        return pltpu.VMEM(shape, kind)

    def sems(*shape):
        return pltpu.SemaphoreType.DMA(shape)

    own, sums = pl.pallas_call(
        whole_kernel,
        out_shape=(
            jax.ShapeDtypeStruct((rows_a, depth_c, merged), jnp.float32),
            jax.ShapeDtypeStruct((tiles, piece, outs), jnp.float32),
        ),
        in_specs=[anywhere] * 11,
        out_specs=(vmem, vmem),
        scratch_shapes=[
            scratch(*w_first.shape),
            scratch(*w_second.shape),
            scratch(*src_pos.shape[::-1], kind=jnp.int32),
            scratch(*src_amp.shape[::-1]),
            scratch(3, 1, count, kind=jnp.int32),
            scratch(STEPS, 1, count),
            scratch(*field),
            scratch(shots, rows_a, depth_c, merged),
            scratch(halves * rows_a * cells, GROUP * CH),
            scratch(halves * rows_a * cells, GROUP * CH),
            scratch(halves * rows_a, GROUP * outs // 4, size_z),
            scratch(*field),
            scratch(STEPS, *field),
            scratch((2 * STEPS + 1) * size_z, count, kind=half),
            scratch(*field),
            scratch(2 * STEPS, size_x + 2 * RIM, tall, size_z),
            scratch(size_x + 2 * VRIM, size_y, size_z),
            scratch(size_x, size_y + 2 * VRIM, size_z),
            scratch(STEPS, *field),
            scratch(2, size_x + 2 * VRIM, size_y, size_z),
            scratch(2, size_x, size_y + 2 * VRIM, size_z),
            scratch(2, *field),
            scratch(*field),
            scratch(STEPS - 1, *field),
            scratch(STEPS, *field),
            scratch(STEPS, *field),
            scratch(STEPS, size_x, size_y + 2 * VRIM, size_z),
            scratch(STEPS, *field),
            scratch(2, *field),
            scratch(halves * rows_a * cells, GROUP * outs),
            scratch(2, shots // 2, rows_a, depth_c, merged),
            scratch(shots // 2, rows_a, depth_c, merged),
            scratch(shots // 2, rows_a, depth_c, merged),
            scratch(shots // 2, rows_a, depth_c, merged),
            scratch(tiles, piece, outs),
            scratch(tiles, piece, outs),
            scratch(shots, piece, outs),
            sems(15),
            sems(slots, 4),
            sems(slots, 4),
            sems(4, shots),
            sems(4, shots),
            sems(2, tiles),
            sems(2, tiles),
        ],
        compiler_params=pltpu.CompilerParams(
            collective_id=0, has_side_effects=True, vmem_limit_bytes=60 * 1024 * 1024
        ),
    )(
        latent.transpose(1, 0, 2),
        w_first,
        w_second,
        fwd_press[0],
        fwd_vel[0],
        adj_press[0],
        adj_vel[0],
        src_pos.T,
        src_amp.T,
        rec_pos.transpose(1, 0, 2),
        observed.transpose(1, 0, 2),
    )
    grad_latent, grad_first, grad_second = pl.pallas_call(
        finish_kernel,
        out_shape=(
            jax.ShapeDtypeStruct(own.shape, jnp.float32),
            jax.ShapeDtypeStruct(w_first.shape, jnp.float32),
            jax.ShapeDtypeStruct(w_second.shape, jnp.float32),
        ),
        scratch_shapes=[scratch(tiles * piece, outs)],
    )(own, sums)
    return grad_latent.transpose(1, 0, 2), grad_first, grad_second


def solution(mesh):
    in_specs = (
        P("shot", "gx", "gy"),
        P(),
        P(),
        P("shot", "gx", "gy", None),
        P("shot", None, "gx", "gy", None),
        P("shot", "gx", "gy", None),
        P("shot", None, "gx", "gy", None),
        P(None, "shot"),
        P(None, "shot"),
        P("shot", None, None),
        P("shot", None, None),
    )
    out_specs = (P("shot", "gx", "gy"), P(), P())
    return jax.shard_map(body, mesh=mesh, in_specs=in_specs, out_specs=out_specs, check_vma=False)
```

```python
import jax
import jax.numpy as jnp
from jax import lax
from jax.experimental import pallas as pl
from jax.experimental.pallas import tpu as pltpu
from jax.sharding import PartitionSpec as P

CH = 64
STEPS = 3
RIM = 7
VRIM = 4
PAD = 8
GROUP = 4
PARTS = 2
LANES = 128

coeffs = (1225.0 / 1024.0, -245.0 / 3072.0, 49.0 / 5120.0, -5.0 / 7168.0)

rows_by_cols = (((1,), (0,)), ((), ()))
rows_by_rows = (((1,), (1,)), ((), ()))
half = jnp.bfloat16


def split(values):
    high = values.astype(half)
    return high, (values - high.astype(jnp.float32)).astype(half)


def mm(left, right, how=rows_by_cols):
    return lax.dot_general(left, right, how, preferred_element_type=jnp.float32)


def mm3(left, right, how=rows_by_cols):
    return (
        mm(left[0], right[0], how) + mm(left[1], right[0], how) + mm(left[0], right[1], how)
    )


def mm2(left, pick, how=rows_by_cols):
    return mm(left[0], pick, how) + mm(left[1], pick, how)


def one_hot(shape, rule):
    rows = lax.broadcasted_iota(jnp.int32, shape, 0)
    cols = lax.broadcasted_iota(jnp.int32, shape, 1)
    return rule(rows, cols)


def low_part(values, size):
    assert size & (size - 1) == 0
    return values & (size - 1)


def high_part(values, size):
    assert size & (size - 1) == 0
    return values >> (size.bit_length() - 1)


def as_pick(mask):
    return jnp.where(mask, 1.0, 0.0).astype(half)


def axis_peers(axis, distance):
    count = lax.axis_size(axis)
    return {axis: lax.rem(lax.axis_index(axis) + distance, count)}


def plane_peers():
    near, wide = lax.axis_size("gy"), lax.axis_size("gx")
    for dx in range(wide):
        for dy in range(near):
            if dx or dy:
                yield {
                    "gx": lax.rem(lax.axis_index("gx") + dx, wide),
                    "gy": lax.rem(lax.axis_index("gy") + dy, near),
                }


def everyone():
    for d in range(1, lax.axis_size("shot")):
        yield axis_peers("shot", d)
    yield from plane_peers()


def remote(source, dest, send_sem, recv_sem, peer):
    return pltpu.make_async_remote_copy(
        src_ref=source,
        dst_ref=dest,
        send_sem=send_sem,
        recv_sem=recv_sem,
        device_id=peer,
        device_id_type=pl.DeviceIdType.MESH,
    )


def logistic(values):
    return 0.5 * jnp.tanh(0.5 * values) + 0.5


def whole_kernel(
    latent_ref,
    first_ref,
    second_ref,
    fwd_press,
    fwd_vel,
    adj_press,
    adj_vel,
    src_pos,
    src_amp,
    rec_pos,
    observed,
    own_ref,
    sums_ref,
    w_first,
    w_second,
    place,
    amps,
    rec_at,
    seen,
    start_adj,
    slabs,
    latents,
    hidden,
    gates,
    hits,
    recorded,
    rec_weights,
    mod,
    press,
    buoy_x,
    buoy_y,
    kicks,
    vel_x,
    vel_y,
    vel_z,
    diverge_z,
    div_at,
    slope_x,
    slope_y,
    slope_z,
    totals,
    turned,
    share,
    paired,
    summed,
    landed,
    w_share,
    w_landed,
    w_plane,
    local_sem,
    send_sem,
    recv_sem,
    gather_send,
    gather_recv,
    shot_send,
    shot_recv,
    plane_send,
    plane_recv,
):
    size_x, size_y, size_z = mod.shape
    cells = size_z // 4
    mid_y = pl.ds(PAD, size_y)
    mid_v = pl.ds(VRIM, size_x)
    rows_a = size_x // 4
    wide = GROUP * CH
    halves = size_y // (4 * GROUP)
    shots = lax.axis_size("shot")
    me = lax.axis_index("shot")
    me_x, me_y = lax.axis_index("gx"), lax.axis_index("gy")
    has = (
        me_x > 0,
        me_x < lax.axis_size("gx") - 1,
        me_y > 0,
        me_y < lax.axis_size("gy") - 1,
    )
    target = ({"gx": me_x - 1}, {"gx": me_x + 1}, {"gy": me_y - 1}, {"gy": me_y + 1})

    barrier = pltpu.get_barrier_semaphore()
    greeted = 0
    for peer in everyone():
        pl.semaphore_signal(
            barrier, inc=1, device_id=peer, device_id_type=pl.DeviceIdType.MESH
        )
        greeted += 1

    loads = [
        (latent_ref, slabs.at[me]),
        (first_ref, w_first),
        (second_ref, w_second),
        (rec_pos, rec_at),
        (observed, seen),
        (src_pos, place),
        (src_amp, amps),
        (fwd_press, press.at[0, pl.ds(RIM, size_x), mid_y]),
        (adj_press, start_adj),
    ]
    for way, vel in enumerate((fwd_vel, adj_vel)):
        loads.append((vel.at[0], vel_x.at[way, pl.ds(VRIM, size_x)]))
        loads.append((vel.at[1], vel_y.at[way, :, pl.ds(VRIM, size_y)]))
        loads.append((vel.at[2], vel_z.at[way]))
    moves = [
        pltpu.make_async_copy(source, dest, local_sem.at[n])
        for n, (source, dest) in enumerate(loads)
    ]
    for move in moves:
        move.start()

    class Link:
        def __init__(self, slot, pairs):
            self.copies = {
                side: remote(
                    *pair,
                    send_sem.at[slot, side],
                    recv_sem.at[slot, side ^ 1],
                    target[side],
                )
                for side, pair in pairs.items()
            }

        def send(self, *sides):
            for side in sides or self.copies:
                pl.when(has[side])(self.copies[side].start)

        def receive(self, *sides):
            for side in sides or self.copies:
                pl.when(has[side])(self.copies[side ^ 1].wait_recv)

        def sent(self):
            for side in self.copies:
                pl.when(has[side])(self.copies[side].wait_send)

    def x_pairs(low, high, dest, rim):
        return {0: (low, dest(size_x + rim, rim)), 1: (high, dest(0, rim))}

    def y_pairs(low, high, dest, at_low, at_high):
        return {2: (low, dest(at_high)), 3: (high, dest(at_low))}

    slot = 0
    links_x, links_y = [], []
    deep_part = size_y // PARTS
    spans = (pl.ds(0, RIM), pl.ds(size_x - RIM, RIM), pl.ds(RIM, size_x - 2 * RIM))
    inner = (pl.ds(RIM, RIM), pl.ds(size_x, RIM), pl.ds(2 * RIM, size_x - 2 * RIM))
    for state in range(2 * STEPS):
        parts = []
        for part in range(PARTS):
            inside = pl.ds(part * deep_part, deep_part)

            def plane(first, count, state=state, part=part):
                return press.at[
                    state, pl.ds(first, count), pl.ds(PAD + part * deep_part, deep_part)
                ]

            low, high = plane(RIM, RIM), plane(size_x, RIM)
            if state == 0:
                low, high = fwd_press.at[spans[0], inside], fwd_press.at[spans[1], inside]
            parts.append(Link(slot, x_pairs(low, high, plane, RIM)))
            slot += 1
        links_x.append(parts)
        parts = []
        for span, rows in zip(spans, inner):

            def strip(first, state=state, rows=rows):
                return press.at[state, rows, pl.ds(first, PAD)]

            low, high = strip(PAD), strip(size_y)
            if state == 0:
                low = fwd_press.at[span, pl.ds(0, PAD)]
                high = fwd_press.at[span, pl.ds(size_y - PAD, PAD)]
            parts.append(Link(slot, y_pairs(low, high, strip, 0, size_y + PAD)))
            slot += 1
        links_y.append(parts)

    def strips(ref):
        return lambda first: ref.at[:, pl.ds(first, VRIM)]

    def layers(ref):
        return lambda first, count: ref.at[pl.ds(first, count)]

    vel_links = []
    for way, vel in enumerate((fwd_vel, adj_vel)):
        pairs = x_pairs(
            vel.at[0, pl.ds(0, VRIM)],
            vel.at[0, pl.ds(size_x - VRIM, VRIM)],
            layers(vel_x.at[way]),
            VRIM,
        )
        pairs.update(
            y_pairs(
                vel.at[1, :, pl.ds(0, VRIM)],
                vel.at[1, :, pl.ds(size_y - VRIM, VRIM)],
                strips(vel_y.at[way]),
                0,
                size_y + VRIM,
            )
        )
        vel_links.append(Link(slot, pairs))
        slot += 1
    pairs = x_pairs(
        buoy_x.at[pl.ds(VRIM, VRIM)], buoy_x.at[pl.ds(size_x, VRIM)], layers(buoy_x), VRIM
    )
    pairs.update(
        y_pairs(
            buoy_y.at[:, pl.ds(VRIM, VRIM)],
            buoy_y.at[:, pl.ds(size_y, VRIM)],
            strips(buoy_y),
            0,
            size_y + VRIM,
        )
    )
    buoy_link = Link(slot, pairs)
    links = [*sum(links_x, []), *sum(links_y, []), *vel_links, buoy_link]

    for side in range(4):

        @pl.when(jnp.logical_not(has[side]))
        def _():
            far = side % 2
            if side < 2:
                rows = pl.ds(far * (size_x + RIM), RIM)
                vrows = pl.ds(far * (size_x + VRIM), VRIM)
                for state in range(2 * STEPS):
                    press[state, rows, mid_y] = jnp.zeros((RIM, size_y, size_z), jnp.float32)
                blank = jnp.zeros((VRIM, size_y, size_z), jnp.float32)
                buoy_x[vrows] = blank
                for way in range(2):
                    vel_x[way, vrows] = blank
            else:
                cols = pl.ds(far * (size_y + PAD), PAD)
                for state in range(2 * STEPS):
                    press[state, pl.ds(RIM, size_x), cols] = jnp.zeros(
                        (size_x, PAD, size_z), jnp.float32
                    )
                vcols = pl.ds(far * (size_y + VRIM), VRIM)
                blank = jnp.zeros((size_x, VRIM, size_z), jnp.float32)
                buoy_y[:, vcols] = blank
                for way in range(2):
                    vel_y[way, :, vcols] = blank

    pl.semaphore_wait(barrier, greeted)

    moves[0].wait()
    mate = lax.rem(me, 2)
    group = me // 2
    groups = shots // 2
    other_core = {"shot": 2 * group + 1 - mate}
    cut = rows_a // 2
    layers_of = (pl.ds(0, cut), pl.ds(cut, rows_a - cut))

    def pass_on(owner, part, peer, row, column):
        rows = slabs.at[owner, layers_of[part]]
        return remote(
            rows, rows, gather_send.at[part, row, column], gather_recv.at[part, row, column], peer
        )

    afar, passed = [], []
    for part in range(2):
        for d in range(1, groups):
            there = {"shot": 2 * lax.rem(group + d, groups) + mate}
            afar.append(pass_on(me, part, there, 0, d))
            owner = 2 * lax.rem(group - d + groups, groups) + mate
            passed.append(pass_on(owner, part, other_core, 1, d))
    beside = [pass_on(me, part, other_core, 1, 0) for part in range(2)]
    for copy in afar + beside:
        copy.start()
    for link in (*links_x[0], *links_y[0], *vel_links):
        link.send()
    for move in moves[1:]:
        move.wait()

    spread_rows = as_pick(one_hot((wide, CH), lambda r, c: low_part(r, CH) == c))
    same_cell = one_hot((wide, wide), lambda r, c: high_part(r, CH) == high_part(c, CH))
    big_first = tuple(
        jnp.where(same_cell, mm(mm(spread_rows, part).astype(half), spread_rows, rows_by_rows), 0.0)
        .astype(half)
        for part in split(w_first[...])
    )
    outs = w_second.shape[1]
    block = outs // 4 * GROUP

    def source_of(c):
        return (c & (block - 16)) + 4 * low_part(c, 4) + high_part(c, block)

    order = as_pick(one_hot((outs, 4 * block), lambda r, c: source_of(c) == r))
    same_out = one_hot((wide, 4 * block), lambda r, c: high_part(c & 12, 4) == high_part(r, CH))
    big_second = tuple(
        jnp.where(same_out, mm(mm(spread_rows, part).astype(half), order), 0.0).astype(half)
        for part in split(w_second[...])
    )
    to_depth = as_pick(
        one_hot((2 * size_z, size_z), lambda r, c: 4 * low_part(r, cells) + high_part(low_part(r, size_z), cells) == c)
    )
    from_depth = as_pick(
        one_hot((2 * size_z, size_z), lambda r, c: 4 * low_part(c, cells) + high_part(c, cells) == low_part(r, size_z))
    )

    def side_by_side(values):
        return jnp.concatenate(split(values), axis=1)


    count = rec_at.shape[2]
    local_x = rec_at[0] - me_x * size_x
    local_y = rec_at[1] - me_y * size_y
    inside = (local_x >= 0) & (local_x < size_x) & (local_y >= 0) & (local_y < size_y)
    column = jnp.where(inside, local_x * size_y + local_y, -1)
    deep = jnp.where(
        lax.broadcasted_iota(jnp.int32, (size_z, count), 0) == rec_at[2], 1.0, 0.0
    )
    rec_weights[pl.ds(0, size_z)] = deep.astype(half)
    for moment in range(STEPS):
        for part, values in enumerate(split(seen[moment])):
            rec_weights[pl.ds((1 + 2 * moment + part) * size_z, size_z)] = (
                deep * values.astype(jnp.float32)
            ).astype(half)
    chunk = 8 if size_x % 8 == 0 else 1
    some = chunk * size_y

    def planes(step, carry):
        index = lax.broadcasted_iota(jnp.int32, (some, count), 0) + step * some
        summed = mm(as_pick(index == column), rec_weights[...], rows_by_rows).reshape(
            chunk, size_y, (2 * STEPS + 1) * size_z
        )
        here = pl.ds(step * chunk, chunk)
        hits[here] = summed[:, :, :size_z]
        for moment in range(STEPS):
            first = (1 + 2 * moment) * size_z
            recorded[moment, here] = (
                summed[:, :, first : first + size_z]
                + summed[:, :, first + size_z : first + 2 * size_z]
            )
        return carry


    src_x = place[:, 0:1] - me_x * size_x
    src_y = place[:, 1:2] - me_y * size_y
    at_source = (lax.broadcasted_iota(jnp.int32, (size_y, size_z), 0) == src_y) & (
        lax.broadcasted_iota(jnp.int32, (size_y, size_z), 1) == place[:, 2:3]
    )
    impulses = [jnp.where(at_source, amps[:, n : n + 1], 0.0) for n in range(STEPS)]

    def kick(x, carry):
        for n in range(STEPS):
            kicks[n, x] = jnp.where(src_x == x, impulses[n], 0.0)
        return carry

    lax.fori_loop(0, size_x, kick, 0)

    for arriving, forward in zip(afar, passed):
        arriving.wait_recv()
        forward.start()
    for copy in beside + passed:
        copy.wait_recv()
    depth_c = slabs.shape[2]
    for s in range(shots):
        for a in range(rows_a):
            for h in range(halves):
                latents[pl.ds((h * rows_a + a) * cells + s * depth_c, depth_c)] = slabs[
                    s, a, :, h * wide : (h + 1) * wide
                ]
    hidden[...] = jnp.tanh(mm3(split(latents[...]), big_first))
    outputs = mm3(split(hidden[...]), big_second)
    blocks = [(h, a) for h in range(halves) for a in range(rows_a)]
    stacked = jnp.concatenate(
        [
            jnp.transpose(
                jnp.concatenate(
                    [
                        outputs[n * cells : (n + 1) * cells, k * block : (k + 1) * block]
                        for k in range(4)
                    ],
                    axis=0,
                )
            )
            for n in range(len(blocks))
        ],
        axis=0,
    )
    gates[...] = logistic(mm(side_by_side(stacked), to_depth)).reshape(gates.shape)
    deep_y = 4 * GROUP
    for n, (h, a) in enumerate(blocks):
        sig = gates[n]
        speed = 0.15 + 0.25 * sig[: block // 2]
        density = 1.0 + 1.5 * sig[block // 2 :]
        modulus = density * speed * speed
        buoyancy = 1.0 / density
        for i in range(4):
            part = slice(i * deep_y, (i + 1) * deep_y)
            mod[4 * a + i, pl.ds(h * deep_y, deep_y)] = modulus[part]
            buoy_x[VRIM + 4 * a + i, pl.ds(h * deep_y, deep_y)] = buoyancy[part]
            buoy_y[4 * a + i, pl.ds(VRIM + h * deep_y, deep_y)] = buoyancy[part]
    buoy_link.send()

    along = [
        split(matrix) for matrix in depth_matrices(size_z)
    ]
    tables = [
        jnp.concatenate(
            [
                jnp.concatenate([high, low], axis=1),
                jnp.concatenate([high, jnp.zeros_like(low)], axis=1),
            ],
            axis=0,
        )
        for high, low in along
    ]

    low_rows, high_rows = (0, RIM), (size_x - RIM, size_x)
    mid_rows = (RIM, size_x - RIM)
    columns = size_y // 8

    def column_of(c, base):
        return pl.ds(pl.multiple_of(8 * c, 8) + base, 8)

    def weigh(ahead, behind):
        summed = 0.0
        for order_at, weight in enumerate(coeffs):
            summed = summed + weight * (ahead[order_at] - behind[order_at])
        return summed

    def along_z(values, table):
        flat = values.reshape(size_x * size_y, size_z)
        both = mm(jnp.concatenate(split(flat), axis=1), table)
        return (both[:, :size_z] + both[:, size_z:]).reshape(values.shape)

    def depth_part(state, way, moment):
        slope = along_z(press[state, pl.ds(RIM, size_x), mid_y], tables[0])
        if way == 0:
            slope_z[moment] = slope
        moved = vel_z[way] - buoy_x[mid_v] * slope
        vel_z[way] = moved
        diverge_z[...] = along_z(moved, tables[1])

    def faces_x(state, way, moment, first, last, span):
        def one(c, carry):
            here, there = column_of(c, 0), column_of(c, PAD)
            rows = {
                i: press[state, i + RIM, there] for i in range(first - 3, last + 4)
            }
            for x in range(first, last):
                slope = weigh([rows[x + r] for r in (1, 2, 3, 4)], [rows[x - r + 1] for r in (1, 2, 3, 4)])
                vel_x[way, x + VRIM, here] = (
                    vel_x[way, x + VRIM, here] - buoy_x[x + VRIM, here] * slope
                )
                if way == 0 and 0 <= x < size_x:
                    slope_x[moment, x, here] = slope
            return carry

        lax.fori_loop(*span, one, 0)

    def faces_y(state, way, moment, rows):
        def one(x, carry):
            def at(r):
                return press[state, x + RIM, pl.ds(VRIM + r, size_y + 2 * VRIM)]

            slope = weigh([at(r) for r in (1, 2, 3, 4)], [at(1 - r) for r in (1, 2, 3, 4)])
            vel_y[way, x] = vel_y[way, x] - buoy_y[x] * slope
            if way == 0:
                slope_y[moment, x] = slope
            return carry

        lax.fori_loop(rows[0], rows[1], one, 0, unroll=2)

    def finish(state, way, moment, rows, span):
        first, last = rows

        def one(c, carry):
            here, there = column_of(c, 0), column_of(c, PAD)
            speeds = {
                i: vel_x[way, i + VRIM, here] for i in range(first - VRIM, last + VRIM - 1)
            }

            def at(x, r):
                return vel_y[way, x, column_of(c, VRIM + r)]

            for x in range(first, last):
                div = diverge_z[x, here] + weigh(
                    [speeds[x + r - 1] for r in (1, 2, 3, 4)], [speeds[x - r] for r in (1, 2, 3, 4)]
                )
                div = div + weigh(
                    [at(x, r - 1) for r in (1, 2, 3, 4)], [at(x, -r) for r in (1, 2, 3, 4)]
                )
                value = press[state, x + RIM, there] - mod[x, here] * div
                if way == 0:
                    value = value + kicks[moment, x, here]
                    div_at[moment, x, here] = div
                    if moment == STEPS - 1:
                        residue = hits[x, here] * value - recorded[moment, x, here]
                        value = start_adj[x, here] + residue
                    press[state + 1, x + RIM, there] = value
                else:
                    part_mod = value * div_at[moment, x, here]
                    part_buoy = (
                        speeds[x] * slope_x[moment, x, here]
                        + at(x, 0) * slope_y[moment, x, column_of(c, VRIM)]
                        + vel_z[way, x, here] * slope_z[moment, x, here]
                    )
                    if moment == STEPS - 1:
                        totals[0, x, here] = -part_mod
                        totals[1, x, here] = -part_buoy
                    else:
                        totals[0, x, here] = totals[0, x, here] - part_mod
                        totals[1, x, here] = totals[1, x, here] - part_buoy
                    if moment > 0:
                        modelled = press[moment, x + RIM, there]
                        residue = hits[x, here] * modelled - recorded[moment - 1, x, here]
                        press[state + 1, x + RIM, there] = value + residue
            return carry

        lax.fori_loop(*span, one, 0)

    every = (0, columns)
    pieces = [(n * columns // PARTS, (n + 1) * columns // PARTS) for n in range(PARTS)]

    def step(state, way, moment):
        depth_part(state, way, moment)
        faces_x(state, way, moment, 3, size_x - 4, every)
        if state < STEPS:
            turns = size_x // chunk
            lax.fori_loop(state * turns // STEPS, (state + 1) * turns // STEPS, planes, 0)
        if state == 0:
            buoy_link.receive()
        if state % STEPS == 0:
            vel_links[way].receive()
        ends = [(0, low_rows, (-VRIM, 3)), (1, high_rows, (size_x - 4, size_x + 3))]
        if state % 2:
            ends.reverse()
        more = state + 1 < 2 * STEPS
        for side, rows, ghosts in ends:
            links_y[state][side].receive()
            faces_y(state, way, moment, rows)
            for part, span in enumerate(pieces):
                links_x[state][part].receive(side)
                faces_x(state, way, moment, *ghosts, span)
                finish(state, way, moment, rows, span)
                if more:
                    links_x[state + 1][part].send(side)
            if more:
                links_y[state + 1][side].send()
        links_y[state][2].receive()
        faces_y(state, way, moment, mid_rows)
        finish(state, way, moment, mid_rows, every)
        if more:
            links_y[state + 1][2].send()

    for moment in range(STEPS):
        step(moment, 0, moment)
    for turn in range(STEPS):
        step(STEPS + turn, 1, STEPS - 1 - turn)

    for n, (h, a) in enumerate(blocks):
        sig = gates[n]
        here = pl.ds(h * deep_y, deep_y)
        grad_mod = jnp.concatenate([totals[0, 4 * a + i, here] for i in range(4)], axis=0)
        grad_buoy = jnp.concatenate([totals[1, 4 * a + i, here] for i in range(4)], axis=0)
        sig_speed, sig_dens = sig[: block // 2], sig[block // 2 :]
        speed = 0.15 + 0.25 * sig_speed
        density = 1.0 + 1.5 * sig_dens
        grad_speed = grad_mod * 2.0 * density * speed
        grad_dens = grad_mod * speed * speed - grad_buoy / (density * density)
        gates[n, pl.ds(0, block // 2)] = grad_speed * 0.25 * sig_speed * (1.0 - sig_speed)
        gates[n, pl.ds(block // 2, block // 2)] = grad_dens * 1.5 * sig_dens * (1.0 - sig_dens)
    permuted = mm(side_by_side(gates[...].reshape(len(blocks) * block, size_z)), from_depth)
    for n in range(len(blocks)):
        rows = jnp.transpose(permuted[n * block : (n + 1) * block])
        for k in range(4):
            turned[pl.ds(n * cells, cells), k * block : (k + 1) * block] = rows[
                k * cells : (k + 1) * cells
            ]
    outer = split(turned[...])
    inner = split(
        mm3(outer, big_second, rows_by_rows) * (1.0 - hidden[...] * hidden[...])
    )
    big_gf = mm3(split(jnp.transpose(latents[...])), inner)
    big_gs = mm3(split(jnp.transpose(hidden[...])), outer)
    sum_f = 0.0
    sum_s = 0.0
    for b in range(GROUP):
        mine = slice(b * CH, (b + 1) * CH)
        sum_f = sum_f + jnp.where(
            one_hot((CH, wide), lambda r, c: high_part(c, CH) == b), big_gf[mine], 0.0
        )
        sum_s = sum_s + jnp.where(
            one_hot((CH, 4 * block), lambda r, c: high_part(c & 12, 4) == b), big_gs[mine], 0.0
        )
    grad_second = mm2(split(sum_s), order, rows_by_rows)
    grad_first = 0.0
    for side in range(2):
        fold = as_pick(one_hot((wide, outs), lambda r, c: low_part(r, CH) + side * CH == c))
        grad_first = grad_first + mm2(
            split(sum_f[side * CH // 2 : (side + 1) * CH // 2]), fold
        )
    weights = jnp.concatenate([grad_second, grad_first], axis=0)

    def total(stack):
        summed = stack[0]
        for n in range(1, stack.shape[0]):
            summed = summed + stack[n]
        return summed

    peers = list(plane_peers())
    spot = me_x * lax.axis_size("gy") + me_y
    piece = weights.shape[0] // shots
    for n in range(shots):
        w_share[n] = weights[n * piece : (n + 1) * piece]
    first_hops = [
        remote(
            w_share.at[axis_peers("shot", d)["shot"]],
            w_landed.at[me],
            shot_send.at[0, d - 1],
            shot_recv.at[0, d - 1],
            axis_peers("shot", d),
        )
        for d in range(1, shots)
    ]
    for hop in first_hops:
        hop.start()
    w_landed[me] = w_share[me]

    grad_rows = mm3(inner, big_first, rows_by_rows)
    for n, (h, a) in enumerate(blocks):
        for s in range(shots):
            first = n * cells + s * depth_c
            share[s % 2, s // 2, a, :, h * wide : (h + 1) * wide] = grad_rows[
                first : first + depth_c
            ]
    swap = remote(
        share.at[1 - mate],
        paired,
        shot_send.at[1, 0],
        shot_recv.at[1, 0],
        other_core,
    )
    swap.start()
    for hop in first_hops:
        hop.wait()
    w_plane[spot] = total(w_landed)
    second_hops = [
        remote(w_plane.at[spot], w_plane.at[spot], plane_send.at[n], plane_recv.at[n], peer)
        for n, peer in enumerate(peers)
    ]
    for hop in second_hops:
        hop.start()
    swap.wait()
    for g in range(groups):
        summed[g] = share[mate, g] + paired[g]
    scatters = []
    for d in range(1, groups):
        there = lax.rem(group + d, groups)
        scatters.append(
            remote(
                summed.at[there],
                landed.at[group],
                shot_send.at[3, d - 1],
                shot_recv.at[3, d - 1],
                {"shot": 2 * there + mate},
            )
        )
    for copy in scatters:
        copy.start()
    landed[group] = summed[group]
    for hop in second_hops:
        hop.wait()
    sums_ref[me] = total(w_plane)
    third_hops = [
        remote(
            sums_ref.at[me],
            sums_ref.at[me],
            shot_send.at[4, d - 1],
            shot_recv.at[4, d - 1],
            axis_peers("shot", d),
        )
        for d in range(1, shots)
    ]
    for hop in third_hops:
        hop.start()
    for copy in scatters:
        copy.wait()
    own_ref[...] = total(landed)
    for hop in third_hops:
        hop.wait()
    for copy in afar + beside + passed:
        copy.wait_send()
    for link in links:
        link.sent()


def depth_matrices(size_z):
    source = lax.broadcasted_iota(jnp.int32, (size_z, size_z), 0)
    dest = lax.broadcasted_iota(jnp.int32, (size_z, size_z), 1)
    plus = jnp.zeros((size_z, size_z), jnp.float32)
    minus = plus
    for order, weight in enumerate(coeffs):
        r = order + 1
        plus = plus + jnp.where(source == dest + r, weight, 0.0)
        plus = plus - jnp.where(source == dest - r + 1, weight, 0.0)
        minus = minus + jnp.where(source == dest + r - 1, weight, 0.0)
        minus = minus - jnp.where(source == dest - r, weight, 0.0)
    return plus, minus


def finish_kernel(own_ref, sums_ref, latent_ref, first_ref, second_ref, joined):
    latent_ref[...] = own_ref[...]
    piece = sums_ref.shape[1]
    for s in range(sums_ref.shape[0]):
        joined[pl.ds(s * piece, piece)] = sums_ref[s]
    second_ref[...] = joined[pl.ds(0, CH)]
    packed = joined[pl.ds(CH, CH // 2)]
    first_ref[pl.ds(0, CH // 2)] = packed[:, :CH]
    first_ref[pl.ds(CH // 2, CH // 2)] = packed[:, CH:]


def body(
    latent,
    w_first,
    w_second,
    fwd_press,
    fwd_vel,
    adj_press,
    adj_vel,
    src_pos,
    src_amp,
    rec_pos,
    observed,
):
    field = fwd_press.shape[1:]
    size_x, size_y, size_z = field
    tall = size_y + 2 * PAD
    depth_c, rows_a, merged = latent.shape
    cells = size_z // 4
    shots = lax.axis_size("shot")
    tiles = lax.axis_size("gx") * lax.axis_size("gy")
    halves = size_y // (4 * GROUP)
    outs = w_second.shape[1]
    count = rec_pos.shape[2]
    anywhere = pl.BlockSpec(memory_space=pl.ANY)
    vmem = pl.BlockSpec(memory_space=pltpu.VMEM)
    slots = (3 + PARTS) * 2 * STEPS + 3
    piece = (CH + CH // 2) // shots

    def scratch(*shape, kind=jnp.float32):
        return pltpu.VMEM(shape, kind)

    def sems(*shape):
        return pltpu.SemaphoreType.DMA(shape)

    own, sums = pl.pallas_call(
        whole_kernel,
        out_shape=(
            jax.ShapeDtypeStruct((rows_a, depth_c, merged), jnp.float32),
            jax.ShapeDtypeStruct((shots, piece, outs), jnp.float32),
        ),
        in_specs=[anywhere] * 11,
        out_specs=(vmem, vmem),
        scratch_shapes=[
            scratch(*w_first.shape),
            scratch(*w_second.shape),
            scratch(*src_pos.shape[::-1], kind=jnp.int32),
            scratch(*src_amp.shape[::-1]),
            scratch(3, 1, count, kind=jnp.int32),
            scratch(STEPS, 1, count),
            scratch(*field),
            scratch(shots, rows_a, depth_c, merged),
            scratch(halves * rows_a * cells, GROUP * CH),
            scratch(halves * rows_a * cells, GROUP * CH),
            scratch(halves * rows_a, GROUP * outs // 4, size_z),
            scratch(*field),
            scratch(STEPS, *field),
            scratch((2 * STEPS + 1) * size_z, count, kind=half),
            scratch(*field),
            scratch(2 * STEPS, size_x + 2 * RIM, tall, size_z),
            scratch(size_x + 2 * VRIM, size_y, size_z),
            scratch(size_x, size_y + 2 * VRIM, size_z),
            scratch(STEPS, *field),
            scratch(2, size_x + 2 * VRIM, size_y, size_z),
            scratch(2, size_x, size_y + 2 * VRIM, size_z),
            scratch(2, *field),
            scratch(*field),
            scratch(STEPS, *field),
            scratch(STEPS, *field),
            scratch(STEPS, size_x, size_y + 2 * VRIM, size_z),
            scratch(STEPS, *field),
            scratch(2, *field),
            scratch(halves * rows_a * cells, GROUP * outs),
            scratch(2, shots // 2, rows_a, depth_c, merged),
            scratch(shots // 2, rows_a, depth_c, merged),
            scratch(shots // 2, rows_a, depth_c, merged),
            scratch(shots // 2, rows_a, depth_c, merged),
            scratch(shots, piece, outs),
            scratch(shots, piece, outs),
            scratch(tiles, piece, outs),
            sems(15),
            sems(slots, 4),
            sems(slots, 4),
            sems(2, 2, shots // 2),
            sems(2, 2, shots // 2),
            sems(5, shots),
            sems(5, shots),
            sems(tiles),
            sems(tiles),
        ],
        compiler_params=pltpu.CompilerParams(
            collective_id=0, has_side_effects=True, vmem_limit_bytes=60 * 1024 * 1024
        ),
    )(
        latent.transpose(1, 0, 2),
        w_first,
        w_second,
        fwd_press[0],
        fwd_vel[0],
        adj_press[0],
        adj_vel[0],
        src_pos.T,
        src_amp.T,
        rec_pos.transpose(1, 0, 2),
        observed.transpose(1, 0, 2),
    )
    grad_latent, grad_first, grad_second = pl.pallas_call(
        finish_kernel,
        out_shape=(
            jax.ShapeDtypeStruct(own.shape, jnp.float32),
            jax.ShapeDtypeStruct(w_first.shape, jnp.float32),
            jax.ShapeDtypeStruct(w_second.shape, jnp.float32),
        ),
        scratch_shapes=[scratch(shots * piece, outs)],
    )(own, sums)
    return grad_latent.transpose(1, 0, 2), grad_first, grad_second


def solution(mesh):
    in_specs = (
        P("shot", "gx", "gy"),
        P(),
        P(),
        P("shot", "gx", "gy", None),
        P("shot", None, "gx", "gy", None),
        P("shot", "gx", "gy", None),
        P("shot", None, "gx", "gy", None),
        P(None, "shot"),
        P(None, "shot"),
        P("shot", None, None),
        P("shot", None, None),
    )
    out_specs = (P("shot", "gx", "gy"), P(), P())
    return jax.shard_map(body, mesh=mesh, in_specs=in_specs, out_specs=out_specs, check_vma=False)
```

```python
import jax
import jax.numpy as jnp
from jax import lax
from jax.experimental import pallas as pl
from jax.experimental.pallas import tpu as pltpu
from jax.sharding import PartitionSpec as P

CH = 64
STEPS = 3
RIM = 7
VRIM = 4
PAD = 8
GROUP = 4
LANES = 128

coeffs = (1225.0 / 1024.0, -245.0 / 3072.0, 49.0 / 5120.0, -5.0 / 7168.0)

rows_by_cols = (((1,), (0,)), ((), ()))
rows_by_rows = (((1,), (1,)), ((), ()))
half = jnp.bfloat16


def split(values):
    high = values.astype(half)
    return high, (values - high.astype(jnp.float32)).astype(half)


def mm(left, right, how=rows_by_cols):
    return lax.dot_general(left, right, how, preferred_element_type=jnp.float32)


def mm3(left, right, how=rows_by_cols):
    return (
        mm(left[0], right[0], how) + mm(left[1], right[0], how) + mm(left[0], right[1], how)
    )


def mm2(left, pick, how=rows_by_cols):
    return mm(left[0], pick, how) + mm(left[1], pick, how)


def one_hot(shape, rule):
    rows = lax.broadcasted_iota(jnp.int32, shape, 0)
    cols = lax.broadcasted_iota(jnp.int32, shape, 1)
    return rule(rows, cols)


def low_part(values, size):
    assert size & (size - 1) == 0
    return values & (size - 1)


def high_part(values, size):
    assert size & (size - 1) == 0
    return values >> (size.bit_length() - 1)


def as_pick(mask):
    return jnp.where(mask, 1.0, 0.0).astype(half)


def axis_peers(axis, distance):
    count = lax.axis_size(axis)
    return {axis: lax.rem(lax.axis_index(axis) + distance, count)}


def plane_peers():
    near, wide = lax.axis_size("gy"), lax.axis_size("gx")
    for dx in range(wide):
        for dy in range(near):
            if dx or dy:
                yield {
                    "gx": lax.rem(lax.axis_index("gx") + dx, wide),
                    "gy": lax.rem(lax.axis_index("gy") + dy, near),
                }


def everyone():
    for d in range(1, lax.axis_size("shot")):
        yield axis_peers("shot", d)
    yield from plane_peers()


def remote(source, dest, send_sem, recv_sem, peer):
    return pltpu.make_async_remote_copy(
        src_ref=source,
        dst_ref=dest,
        send_sem=send_sem,
        recv_sem=recv_sem,
        device_id=peer,
        device_id_type=pl.DeviceIdType.MESH,
    )


def logistic(values):
    return 0.5 * jnp.tanh(0.5 * values) + 0.5


def whole_kernel(
    latent_ref,
    first_ref,
    second_ref,
    fwd_press,
    fwd_vel,
    adj_press,
    adj_vel,
    src_pos,
    src_amp,
    rec_pos,
    observed,
    own_ref,
    sums_ref,
    w_first,
    w_second,
    place,
    amps,
    rec_at,
    seen,
    start_adj,
    slabs,
    latents,
    hidden,
    gates,
    factors,
    across,
    hits,
    recorded,
    rec_weights,
    mod,
    press,
    buoy_x,
    buoy_y,
    kicks,
    vel_x,
    vel_y,
    vel_z,
    diverge_z,
    div_at,
    slope_x,
    slope_y,
    slope_z,
    totals,
    turned,
    share,
    paired,
    summed,
    landed,
    w_share,
    w_landed,
    w_plane,
    local_sem,
    send_sem,
    recv_sem,
    gather_send,
    gather_recv,
    shot_send,
    shot_recv,
    plane_send,
    plane_recv,
):
    size_x, size_y, size_z = mod.shape
    cells = size_z // 4
    mid_y = pl.ds(PAD, size_y)
    mid_v = pl.ds(VRIM, size_x)
    rows_a = size_x // 4
    wide = GROUP * CH
    halves = size_y // (4 * GROUP)
    shots = lax.axis_size("shot")
    me = lax.axis_index("shot")
    me_x, me_y = lax.axis_index("gx"), lax.axis_index("gy")
    has = (
        me_x > 0,
        me_x < lax.axis_size("gx") - 1,
        me_y > 0,
        me_y < lax.axis_size("gy") - 1,
    )
    target = ({"gx": me_x - 1}, {"gx": me_x + 1}, {"gy": me_y - 1}, {"gy": me_y + 1})

    barrier = pltpu.get_barrier_semaphore()
    greeted = 0
    for peer in everyone():
        pl.semaphore_signal(
            barrier, inc=1, device_id=peer, device_id_type=pl.DeviceIdType.MESH
        )
        greeted += 1

    loads = [
        (latent_ref, slabs.at[me]),
        (first_ref, w_first),
        (second_ref, w_second),
        (rec_pos, rec_at),
        (observed, seen),
        (src_pos, place),
        (src_amp, amps),
        (fwd_press, press.at[0, pl.ds(RIM, size_x), mid_y]),
        (adj_press, start_adj),
    ]
    for way, vel in enumerate((fwd_vel, adj_vel)):
        loads.append((vel.at[0], vel_x.at[way, pl.ds(VRIM, size_x)]))
        loads.append((vel.at[1], vel_y.at[way, :, pl.ds(VRIM, size_y)]))
        loads.append((vel.at[2], vel_z.at[way]))
    moves = [
        pltpu.make_async_copy(source, dest, local_sem.at[n])
        for n, (source, dest) in enumerate(loads)
    ]
    for move in moves:
        move.start()

    class Link:
        def __init__(self, slot, pairs):
            self.copies = {
                side: remote(
                    *pair,
                    send_sem.at[slot, side],
                    recv_sem.at[slot, side ^ 1],
                    target[side],
                )
                for side, pair in pairs.items()
            }

        def send(self, *sides):
            for side in sides or self.copies:
                pl.when(has[side])(self.copies[side].start)

        def receive(self, *sides):
            for side in sides or self.copies:
                pl.when(has[side])(self.copies[side ^ 1].wait_recv)

        def sent(self):
            for side in self.copies:
                pl.when(has[side])(self.copies[side].wait_send)

    def x_pairs(low, high, dest, rim):
        return {0: (low, dest(size_x + rim, rim)), 1: (high, dest(0, rim))}

    def y_pairs(low, high, dest, at_low, at_high):
        return {2: (low, dest(at_high)), 3: (high, dest(at_low))}

    slot = 0
    links_x, links_y = [], []
    spans = (pl.ds(0, RIM), pl.ds(size_x - RIM, RIM), pl.ds(RIM, size_x - 2 * RIM))
    inner = (pl.ds(RIM, RIM), pl.ds(size_x, RIM), pl.ds(2 * RIM, size_x - 2 * RIM))
    for state in range(2 * STEPS):
        parts = []
        for at_y, deep in ((PAD, size_y - 2 * PAD), (0, PAD), (size_y - PAD, PAD)):
            inside = pl.ds(at_y, deep)

            def plane(first, count, state=state, at_y=at_y, deep=deep):
                return press.at[state, pl.ds(first, count), pl.ds(PAD + at_y, deep)]

            low, high = plane(RIM, RIM), plane(size_x, RIM)
            if state == 0:
                low, high = fwd_press.at[spans[0], inside], fwd_press.at[spans[1], inside]
            parts.append(Link(slot, x_pairs(low, high, plane, RIM)))
            slot += 1
        links_x.append(parts)
        parts = []
        for span, rows in zip(spans, inner):

            def strip(first, state=state, rows=rows):
                return press.at[state, rows, pl.ds(first, PAD)]

            low, high = strip(PAD), strip(size_y)
            if state == 0:
                low = fwd_press.at[span, pl.ds(0, PAD)]
                high = fwd_press.at[span, pl.ds(size_y - PAD, PAD)]
            parts.append(Link(slot, y_pairs(low, high, strip, 0, size_y + PAD)))
            slot += 1
        links_y.append(parts)

    def strips(ref):
        return lambda first: ref.at[:, pl.ds(first, VRIM)]

    def layers(ref):
        return lambda first, count: ref.at[pl.ds(first, count)]

    vel_links = []
    for way, vel in enumerate((fwd_vel, adj_vel)):
        pairs = x_pairs(
            vel.at[0, pl.ds(0, VRIM)],
            vel.at[0, pl.ds(size_x - VRIM, VRIM)],
            layers(vel_x.at[way]),
            VRIM,
        )
        pairs.update(
            y_pairs(
                vel.at[1, :, pl.ds(0, VRIM)],
                vel.at[1, :, pl.ds(size_y - VRIM, VRIM)],
                strips(vel_y.at[way]),
                0,
                size_y + VRIM,
            )
        )
        vel_links.append(Link(slot, pairs))
        slot += 1
    pairs = x_pairs(
        buoy_x.at[pl.ds(VRIM, VRIM)], buoy_x.at[pl.ds(size_x, VRIM)], layers(buoy_x), VRIM
    )
    pairs.update(
        y_pairs(
            buoy_y.at[:, pl.ds(VRIM, VRIM)],
            buoy_y.at[:, pl.ds(size_y, VRIM)],
            strips(buoy_y),
            0,
            size_y + VRIM,
        )
    )
    buoy_link = Link(slot, pairs)
    links = [*sum(links_x, []), *sum(links_y, []), *vel_links, buoy_link]

    for side in range(4):

        @pl.when(jnp.logical_not(has[side]))
        def _():
            far = side % 2
            if side < 2:
                rows = pl.ds(far * (size_x + RIM), RIM)
                vrows = pl.ds(far * (size_x + VRIM), VRIM)
                for state in range(2 * STEPS):
                    press[state, rows, mid_y] = jnp.zeros((RIM, size_y, size_z), jnp.float32)
                blank = jnp.zeros((VRIM, size_y, size_z), jnp.float32)
                buoy_x[vrows] = blank
                for way in range(2):
                    vel_x[way, vrows] = blank
            else:
                cols = pl.ds(far * (size_y + PAD), PAD)
                for state in range(2 * STEPS):
                    press[state, pl.ds(RIM, size_x), cols] = jnp.zeros(
                        (size_x, PAD, size_z), jnp.float32
                    )
                vcols = pl.ds(far * (size_y + VRIM), VRIM)
                blank = jnp.zeros((size_x, VRIM, size_z), jnp.float32)
                buoy_y[:, vcols] = blank
                for way in range(2):
                    vel_y[way, :, vcols] = blank

    pl.semaphore_wait(barrier, greeted)

    moves[0].wait()
    mate = lax.rem(me, 2)
    group = me // 2
    groups = shots // 2
    other_core = {"shot": 2 * group + 1 - mate}
    cut = rows_a // 2
    layers_of = (pl.ds(0, cut), pl.ds(cut, rows_a - cut))

    def pass_on(owner, part, peer, row, column):
        rows = slabs.at[owner, layers_of[part]]
        return remote(
            rows, rows, gather_send.at[part, row, column], gather_recv.at[part, row, column], peer
        )

    afar, passed = [], []
    for part in range(2):
        for d in range(1, groups):
            there = {"shot": 2 * lax.rem(group + d, groups) + mate}
            afar.append(pass_on(me, part, there, 0, d))
            owner = 2 * lax.rem(group - d + groups, groups) + mate
            passed.append(pass_on(owner, part, other_core, 1, d))
    beside = [pass_on(me, part, other_core, 1, 0) for part in range(2)]
    for copy in afar + beside:
        copy.start()
    for link in (*links_x[0], *links_y[0], *vel_links):
        link.send()
    for move in moves[1:]:
        move.wait()

    spread_rows = as_pick(one_hot((wide, CH), lambda r, c: low_part(r, CH) == c))
    same_cell = one_hot((wide, wide), lambda r, c: high_part(r, CH) == high_part(c, CH))
    big_first = tuple(
        jnp.where(same_cell, mm(mm(spread_rows, part).astype(half), spread_rows, rows_by_rows), 0.0)
        .astype(half)
        for part in split(w_first[...])
    )
    outs = w_second.shape[1]
    block = outs // 4 * GROUP

    def source_of(c):
        return (c & (block - 16)) + 4 * low_part(c, 4) + high_part(c, block)

    order = as_pick(one_hot((outs, 4 * block), lambda r, c: source_of(c) == r))
    same_out = one_hot((wide, 4 * block), lambda r, c: high_part(c & 12, 4) == high_part(r, CH))
    big_second = tuple(
        jnp.where(same_out, mm(mm(spread_rows, part).astype(half), order), 0.0).astype(half)
        for part in split(w_second[...])
    )
    to_depth = as_pick(
        one_hot((2 * size_z, size_z), lambda r, c: 4 * low_part(r, cells) + high_part(low_part(r, size_z), cells) == c)
    )
    from_depth = as_pick(
        one_hot((2 * size_z, size_z), lambda r, c: 4 * low_part(c, cells) + high_part(c, cells) == low_part(r, size_z))
    )

    def side_by_side(values):
        return jnp.concatenate(split(values), axis=1)


    count = rec_at.shape[2]
    local_x = rec_at[0] - me_x * size_x
    local_y = rec_at[1] - me_y * size_y
    inside = (local_x >= 0) & (local_x < size_x) & (local_y >= 0) & (local_y < size_y)
    column = jnp.where(inside, local_x * size_y + local_y, -1)
    deep = jnp.where(
        lax.broadcasted_iota(jnp.int32, (size_z, count), 0) == rec_at[2], 1.0, 0.0
    )
    rec_weights[pl.ds(0, size_z)] = deep.astype(half)
    for moment in range(STEPS):
        for part, values in enumerate(split(seen[moment])):
            rec_weights[pl.ds((1 + 2 * moment + part) * size_z, size_z)] = (
                deep * values.astype(jnp.float32)
            ).astype(half)
    chunk = 8 if size_x % 8 == 0 else 1
    some = chunk * size_y

    def planes(step, carry):
        index = lax.broadcasted_iota(jnp.int32, (some, count), 0) + step * some
        summed = mm(as_pick(index == column), rec_weights[...], rows_by_rows).reshape(
            chunk, size_y, (2 * STEPS + 1) * size_z
        )
        here = pl.ds(step * chunk, chunk)
        hits[here] = summed[:, :, :size_z]
        for moment in range(STEPS):
            first = (1 + 2 * moment) * size_z
            recorded[moment, here] = (
                summed[:, :, first : first + size_z]
                + summed[:, :, first + size_z : first + 2 * size_z]
            )
        return carry


    src_x = place[:, 0:1] - me_x * size_x
    src_y = place[:, 1:2] - me_y * size_y
    at_source = (lax.broadcasted_iota(jnp.int32, (size_y, size_z), 0) == src_y) & (
        lax.broadcasted_iota(jnp.int32, (size_y, size_z), 1) == place[:, 2:3]
    )
    impulses = [jnp.where(at_source, amps[:, n : n + 1], 0.0) for n in range(STEPS)]

    def kick(x, carry):
        for n in range(STEPS):
            kicks[n, x] = jnp.where(src_x == x, impulses[n], 0.0)
        return carry

    lax.fori_loop(0, size_x, kick, 0)

    for arriving, forward in zip(afar, passed):
        arriving.wait_recv()
        forward.start()
    for copy in beside + passed:
        copy.wait_recv()
    depth_c = slabs.shape[2]
    for s in range(shots):
        for a in range(rows_a):
            for h in range(halves):
                latents[pl.ds((h * rows_a + a) * cells + s * depth_c, depth_c)] = slabs[
                    s, a, :, h * wide : (h + 1) * wide
                ]
    hidden[...] = jnp.tanh(mm3(split(latents[...]), big_first))
    outputs = mm3(split(hidden[...]), big_second)
    blocks = [(h, a) for h in range(halves) for a in range(rows_a)]
    deep_y = 4 * GROUP

    def materials(group_of):
        stacked = jnp.concatenate(
            [
                jnp.transpose(
                    jnp.concatenate(
                        [
                            outputs[n * cells : (n + 1) * cells, k * block : (k + 1) * block]
                            for k in range(4)
                        ],
                        axis=0,
                    )
                )
                for n in group_of
            ],
            axis=0,
        )
        sigs = logistic(mm(side_by_side(stacked), to_depth))
        for at, n in enumerate(group_of):
            h, a = blocks[n]
            sig = sigs[at * block : (at + 1) * block]
            gates[n] = sig
            speed = 0.15 + 0.25 * sig[: block // 2]
            density = 1.0 + 1.5 * sig[block // 2 :]
            modulus = density * speed * speed
            buoyancy = 1.0 / density
            for i in range(4):
                part = slice(i * deep_y, (i + 1) * deep_y)
                mod[4 * a + i, pl.ds(h * deep_y, deep_y)] = modulus[part]
                buoy_x[VRIM + 4 * a + i, pl.ds(h * deep_y, deep_y)] = buoyancy[part]
                buoy_y[4 * a + i, pl.ds(VRIM + h * deep_y, deep_y)] = buoyancy[part]

    at_ends = [n for n, (h, a) in enumerate(blocks) if a in (0, rows_a - 1)]
    materials(at_ends)
    buoy_link.send(0, 1)
    materials([n for n in range(len(blocks)) if n not in at_ends])
    buoy_link.send(2, 3)

    along = [
        split(matrix) for matrix in depth_matrices(size_z)
    ]
    tables = [
        jnp.concatenate(
            [
                jnp.concatenate([high, low], axis=1),
                jnp.concatenate([high, jnp.zeros_like(low)], axis=1),
            ],
            axis=0,
        )
        for high, low in along
    ]

    low_rows, high_rows = (0, RIM), (size_x - RIM, size_x)
    mid_rows = (RIM, size_x - RIM)
    columns = size_y // 8

    def column_of(c, base):
        return pl.ds(pl.multiple_of(8 * c, 8) + base, 8)

    def weigh(ahead, behind):
        summed = 0.0
        for order_at, weight in enumerate(coeffs):
            summed = summed + weight * (ahead[order_at] - behind[order_at])
        return summed

    def along_z(values, table):
        flat = values.reshape(size_x * size_y, size_z)
        both = mm(jnp.concatenate(split(flat), axis=1), table)
        return (both[:, :size_z] + both[:, size_z:]).reshape(values.shape)

    def depth_part(state, way, moment):
        slope = along_z(press[state, pl.ds(RIM, size_x), mid_y], tables[0])
        if way == 0:
            slope_z[moment] = slope
        moved = vel_z[way] - buoy_x[mid_v] * slope
        vel_z[way] = moved
        diverge_z[...] = along_z(moved, tables[1])

    def faces_x(state, way, moment, first, last, span):
        def one(n, carry):
            c = n * span[2]
            here, there = column_of(c, 0), column_of(c, PAD)
            rows = {
                i: press[state, i + RIM, there] for i in range(first - 3, last + 4)
            }
            for x in range(first, last):
                slope = weigh([rows[x + r] for r in (1, 2, 3, 4)], [rows[x - r + 1] for r in (1, 2, 3, 4)])
                vel_x[way, x + VRIM, here] = (
                    vel_x[way, x + VRIM, here] - buoy_x[x + VRIM, here] * slope
                )
                if way == 0 and 0 <= x < size_x:
                    slope_x[moment, x, here] = slope
            return carry

        lax.fori_loop(span[0], span[1], one, 0)

    def faces_y(state, way, moment, rows, strips_of):
        def one(x, carry):
            for first, deep in strips_of:

                def at(r):
                    return press[state, x + RIM, pl.ds(VRIM + first + r, deep)]

                here = pl.ds(first, deep)
                slope = weigh([at(r) for r in (1, 2, 3, 4)], [at(1 - r) for r in (1, 2, 3, 4)])
                vel_y[way, x, here] = vel_y[way, x, here] - buoy_y[x, here] * slope
                if way == 0:
                    slope_y[moment, x, here] = slope
            return carry

        lax.fori_loop(rows[0], rows[1], one, 0, unroll=2)

    def finish(state, way, moment, rows, span):
        first, last = rows

        def one(n, carry):
            c = n * span[2]
            here, there = column_of(c, 0), column_of(c, PAD)
            speeds = {
                i: vel_x[way, i + VRIM, here] for i in range(first - VRIM, last + VRIM - 1)
            }

            def at(x, r):
                return vel_y[way, x, column_of(c, VRIM + r)]

            for x in range(first, last):
                div = diverge_z[x, here] + weigh(
                    [speeds[x + r - 1] for r in (1, 2, 3, 4)], [speeds[x - r] for r in (1, 2, 3, 4)]
                )
                div = div + weigh(
                    [at(x, r - 1) for r in (1, 2, 3, 4)], [at(x, -r) for r in (1, 2, 3, 4)]
                )
                value = press[state, x + RIM, there] - mod[x, here] * div
                if way == 0:
                    value = value + kicks[moment, x, here]
                    div_at[moment, x, here] = div
                    if moment == STEPS - 1:
                        residue = hits[x, here] * value - recorded[moment, x, here]
                        value = start_adj[x, here] + residue
                    press[state + 1, x + RIM, there] = value
                else:
                    part_mod = value * div_at[moment, x, here]
                    part_buoy = (
                        speeds[x] * slope_x[moment, x, here]
                        + at(x, 0) * slope_y[moment, x, column_of(c, VRIM)]
                        + vel_z[way, x, here] * slope_z[moment, x, here]
                    )
                    if moment == STEPS - 1:
                        totals[0, x, here] = -part_mod
                        totals[1, x, here] = -part_buoy
                    else:
                        totals[0, x, here] = totals[0, x, here] - part_mod
                        totals[1, x, here] = totals[1, x, here] - part_buoy
                    if moment > 0:
                        modelled = press[moment, x + RIM, there]
                        residue = hits[x, here] * modelled - recorded[moment - 1, x, here]
                        press[state + 1, x + RIM, there] = value + residue
            return carry

        lax.fori_loop(span[0], span[1], one, 0)

    def prepare_gates():
        for n in range(len(blocks)):
            sig = gates[n]
            sig_speed, sig_dens = sig[: block // 2], sig[block // 2 :]
            speed = 0.15 + 0.25 * sig_speed
            density = 1.0 + 1.5 * sig_dens
            inverse = 1.0 / density
            bend = 1.5 * sig_dens * (1.0 - sig_dens)
            factors[0, n] = 0.5 * density * speed * sig_speed * (1.0 - sig_speed)
            factors[1, n] = speed * speed * bend
            factors[2, n] = inverse * inverse * bend

    def prepare_rows():
        for n, rows in enumerate((latents, hidden)):
            high, low = split(jnp.transpose(rows[...]))
            across[n, 0] = high
            across[n, 1] = low

    every, inner_columns, outer_columns = (0, columns, 1), (1, columns - 1, 1), (0, 2, columns - 1)
    inner_strips = ((8, size_y + 2 * VRIM - 16),)
    outer_strips = ((0, 8), (size_y + 2 * VRIM - 8, 8))

    def step(state, way, moment):
        depth_part(state, way, moment)
        faces_x(state, way, moment, 3, size_x - 4, every)
        if state < STEPS:
            turns = size_x // chunk
            lax.fori_loop(state * turns // STEPS, (state + 1) * turns // STEPS, planes, 0)
        ends = [(0, low_rows, (-VRIM, 3)), (1, high_rows, (size_x - 4, size_x + 3))]
        if state % 2:
            ends.reverse()
        more = state + 1 < 2 * STEPS
        if state == 0:
            buoy_link.receive(0, 1)
        if state % STEPS == 0:
            vel_links[way].receive(0, 1)
        for side, rows, ghosts in ends:
            faces_y(state, way, moment, rows, inner_strips)
            links_x[state][0].receive(side)
            faces_x(state, way, moment, *ghosts, inner_columns)
            finish(state, way, moment, rows, inner_columns)
            if more:
                links_x[state + 1][0].send(side)
        faces_y(state, way, moment, mid_rows, inner_strips)
        finish(state, way, moment, mid_rows, inner_columns)
        if state == STEPS + 1:
            prepare_gates()
        if state == STEPS + 2:
            prepare_rows()
        if state == 0:
            buoy_link.receive(2, 3)
        if state % STEPS == 0:
            vel_links[way].receive(2, 3)
        for side, rows, ghosts in ends:
            links_y[state][side].receive()
            for part in (1, 2):
                links_x[state][part].receive(side)
            faces_x(state, way, moment, *ghosts, outer_columns)
            faces_y(state, way, moment, rows, outer_strips)
            finish(state, way, moment, rows, outer_columns)
            if more:
                links_y[state + 1][side].send()
                for part in (1, 2):
                    links_x[state + 1][part].send(side)
        links_y[state][2].receive()
        faces_y(state, way, moment, mid_rows, outer_strips)
        finish(state, way, moment, mid_rows, outer_columns)
        if more:
            links_y[state + 1][2].send()

    for moment in range(STEPS):
        step(moment, 0, moment)
    for turn in range(STEPS):
        step(STEPS + turn, 1, STEPS - 1 - turn)

    for n, (h, a) in enumerate(blocks):
        here = pl.ds(h * deep_y, deep_y)
        grad_mod = jnp.concatenate([totals[0, 4 * a + i, here] for i in range(4)], axis=0)
        grad_buoy = jnp.concatenate([totals[1, 4 * a + i, here] for i in range(4)], axis=0)
        gates[n, pl.ds(0, block // 2)] = grad_mod * factors[0, n]
        gates[n, pl.ds(block // 2, block // 2)] = (
            grad_mod * factors[1, n] - grad_buoy * factors[2, n]
        )
    permuted = mm(side_by_side(gates[...].reshape(len(blocks) * block, size_z)), from_depth)
    for n in range(len(blocks)):
        rows = jnp.transpose(permuted[n * block : (n + 1) * block])
        for k in range(4):
            turned[pl.ds(n * cells, cells), k * block : (k + 1) * block] = rows[
                k * cells : (k + 1) * cells
            ]
    outer = split(turned[...])
    inner = split(
        mm3(outer, big_second, rows_by_rows) * (1.0 - hidden[...] * hidden[...])
    )
    big_gf = mm3((across[0, 0], across[0, 1]), inner)
    big_gs = mm3((across[1, 0], across[1, 1]), outer)
    sum_f = 0.0
    sum_s = 0.0
    for b in range(GROUP):
        mine = slice(b * CH, (b + 1) * CH)
        sum_f = sum_f + jnp.where(
            one_hot((CH, wide), lambda r, c: high_part(c, CH) == b), big_gf[mine], 0.0
        )
        sum_s = sum_s + jnp.where(
            one_hot((CH, 4 * block), lambda r, c: high_part(c & 12, 4) == b), big_gs[mine], 0.0
        )
    grad_second = mm2(split(sum_s), order, rows_by_rows)
    grad_first = 0.0
    for side in range(2):
        fold = as_pick(one_hot((wide, outs), lambda r, c: low_part(r, CH) + side * CH == c))
        grad_first = grad_first + mm2(
            split(sum_f[side * CH // 2 : (side + 1) * CH // 2]), fold
        )
    weights = jnp.concatenate([grad_second, grad_first], axis=0)

    def total(stack):
        summed = stack[0]
        for n in range(1, stack.shape[0]):
            summed = summed + stack[n]
        return summed

    peers = list(plane_peers())
    spot = me_x * lax.axis_size("gy") + me_y
    piece = weights.shape[0] // shots
    for n in range(shots):
        w_share[n] = weights[n * piece : (n + 1) * piece]
    first_hops = [
        remote(
            w_share.at[axis_peers("shot", d)["shot"]],
            w_landed.at[me],
            shot_send.at[0, d - 1],
            shot_recv.at[0, d - 1],
            axis_peers("shot", d),
        )
        for d in range(1, shots)
    ]
    for hop in first_hops:
        hop.start()
    w_landed[me] = w_share[me]

    grad_rows = mm3(inner, big_first, rows_by_rows)
    for n, (h, a) in enumerate(blocks):
        for s in range(shots):
            first = n * cells + s * depth_c
            share[s % 2, s // 2, a, :, h * wide : (h + 1) * wide] = grad_rows[
                first : first + depth_c
            ]
    swap = remote(
        share.at[1 - mate],
        paired,
        shot_send.at[1, 0],
        shot_recv.at[1, 0],
        other_core,
    )
    swap.start()
    for hop in first_hops:
        hop.wait()
    w_plane[spot] = total(w_landed)
    second_hops = [
        remote(w_plane.at[spot], w_plane.at[spot], plane_send.at[n], plane_recv.at[n], peer)
        for n, peer in enumerate(peers)
    ]
    for hop in second_hops:
        hop.start()
    swap.wait()
    for g in range(groups):
        summed[g] = share[mate, g] + paired[g]
    scatters = []
    for d in range(1, groups):
        there = lax.rem(group + d, groups)
        scatters.append(
            remote(
                summed.at[there],
                landed.at[group],
                shot_send.at[3, d - 1],
                shot_recv.at[3, d - 1],
                {"shot": 2 * there + mate},
            )
        )
    for copy in scatters:
        copy.start()
    landed[group] = summed[group]
    for hop in second_hops:
        hop.wait()
    sums_ref[me] = total(w_plane)
    third_hops = [
        remote(
            sums_ref.at[me],
            sums_ref.at[me],
            shot_send.at[4, d - 1],
            shot_recv.at[4, d - 1],
            axis_peers("shot", d),
        )
        for d in range(1, shots)
    ]
    for hop in third_hops:
        hop.start()
    for copy in scatters:
        copy.wait()
    own_ref[...] = total(landed)
    for hop in third_hops:
        hop.wait()
    for copy in afar + beside + passed:
        copy.wait_send()
    for link in links:
        link.sent()


def depth_matrices(size_z):
    source = lax.broadcasted_iota(jnp.int32, (size_z, size_z), 0)
    dest = lax.broadcasted_iota(jnp.int32, (size_z, size_z), 1)
    plus = jnp.zeros((size_z, size_z), jnp.float32)
    minus = plus
    for order, weight in enumerate(coeffs):
        r = order + 1
        plus = plus + jnp.where(source == dest + r, weight, 0.0)
        plus = plus - jnp.where(source == dest - r + 1, weight, 0.0)
        minus = minus + jnp.where(source == dest + r - 1, weight, 0.0)
        minus = minus - jnp.where(source == dest - r, weight, 0.0)
    return plus, minus


def finish_kernel(own_ref, sums_ref, latent_ref, first_ref, second_ref, joined):
    latent_ref[...] = own_ref[...]
    piece = sums_ref.shape[1]
    for s in range(sums_ref.shape[0]):
        joined[pl.ds(s * piece, piece)] = sums_ref[s]
    second_ref[...] = joined[pl.ds(0, CH)]
    packed = joined[pl.ds(CH, CH // 2)]
    first_ref[pl.ds(0, CH // 2)] = packed[:, :CH]
    first_ref[pl.ds(CH // 2, CH // 2)] = packed[:, CH:]


def body(
    latent,
    w_first,
    w_second,
    fwd_press,
    fwd_vel,
    adj_press,
    adj_vel,
    src_pos,
    src_amp,
    rec_pos,
    observed,
):
    field = fwd_press.shape[1:]
    size_x, size_y, size_z = field
    tall = size_y + 2 * PAD
    depth_c, rows_a, merged = latent.shape
    cells = size_z // 4
    shots = lax.axis_size("shot")
    tiles = lax.axis_size("gx") * lax.axis_size("gy")
    halves = size_y // (4 * GROUP)
    outs = w_second.shape[1]
    count = rec_pos.shape[2]
    anywhere = pl.BlockSpec(memory_space=pl.ANY)
    vmem = pl.BlockSpec(memory_space=pltpu.VMEM)
    slots = 6 * 2 * STEPS + 3
    piece = (CH + CH // 2) // shots

    def scratch(*shape, kind=jnp.float32):
        return pltpu.VMEM(shape, kind)

    def sems(*shape):
        return pltpu.SemaphoreType.DMA(shape)

    own, sums = pl.pallas_call(
        whole_kernel,
        out_shape=(
            jax.ShapeDtypeStruct((rows_a, depth_c, merged), jnp.float32),
            jax.ShapeDtypeStruct((shots, piece, outs), jnp.float32),
        ),
        in_specs=[anywhere] * 11,
        out_specs=(vmem, vmem),
        scratch_shapes=[
            scratch(*w_first.shape),
            scratch(*w_second.shape),
            scratch(*src_pos.shape[::-1], kind=jnp.int32),
            scratch(*src_amp.shape[::-1]),
            scratch(3, 1, count, kind=jnp.int32),
            scratch(STEPS, 1, count),
            scratch(*field),
            scratch(shots, rows_a, depth_c, merged),
            scratch(halves * rows_a * cells, GROUP * CH),
            scratch(halves * rows_a * cells, GROUP * CH),
            scratch(halves * rows_a, GROUP * outs // 4, size_z),
            scratch(3, halves * rows_a, GROUP * outs // 8, size_z),
            scratch(2, 2, GROUP * CH, halves * rows_a * cells, kind=half),
            scratch(*field),
            scratch(STEPS, *field),
            scratch((2 * STEPS + 1) * size_z, count, kind=half),
            scratch(*field),
            scratch(2 * STEPS, size_x + 2 * RIM, tall, size_z),
            scratch(size_x + 2 * VRIM, size_y, size_z),
            scratch(size_x, size_y + 2 * VRIM, size_z),
            scratch(STEPS, *field),
            scratch(2, size_x + 2 * VRIM, size_y, size_z),
            scratch(2, size_x, size_y + 2 * VRIM, size_z),
            scratch(2, *field),
            scratch(*field),
            scratch(STEPS, *field),
            scratch(STEPS, *field),
            scratch(STEPS, size_x, size_y + 2 * VRIM, size_z),
            scratch(STEPS, *field),
            scratch(2, *field),
            scratch(halves * rows_a * cells, GROUP * outs),
            scratch(2, shots // 2, rows_a, depth_c, merged),
            scratch(shots // 2, rows_a, depth_c, merged),
            scratch(shots // 2, rows_a, depth_c, merged),
            scratch(shots // 2, rows_a, depth_c, merged),
            scratch(shots, piece, outs),
            scratch(shots, piece, outs),
            scratch(tiles, piece, outs),
            sems(15),
            sems(slots, 4),
            sems(slots, 4),
            sems(2, 2, shots // 2),
            sems(2, 2, shots // 2),
            sems(5, shots),
            sems(5, shots),
            sems(tiles),
            sems(tiles),
        ],
        compiler_params=pltpu.CompilerParams(
            collective_id=0, has_side_effects=True, vmem_limit_bytes=60 * 1024 * 1024
        ),
    )(
        latent.transpose(1, 0, 2),
        w_first,
        w_second,
        fwd_press[0],
        fwd_vel[0],
        adj_press[0],
        adj_vel[0],
        src_pos.T,
        src_amp.T,
        rec_pos.transpose(1, 0, 2),
        observed.transpose(1, 0, 2),
    )
    grad_latent, grad_first, grad_second = pl.pallas_call(
        finish_kernel,
        out_shape=(
            jax.ShapeDtypeStruct(own.shape, jnp.float32),
            jax.ShapeDtypeStruct(w_first.shape, jnp.float32),
            jax.ShapeDtypeStruct(w_second.shape, jnp.float32),
        ),
        scratch_shapes=[scratch(shots * piece, outs)],
    )(own, sums)
    return grad_latent.transpose(1, 0, 2), grad_first, grad_second


def solution(mesh):
    in_specs = (
        P("shot", "gx", "gy"),
        P(),
        P(),
        P("shot", "gx", "gy", None),
        P("shot", None, "gx", "gy", None),
        P("shot", "gx", "gy", None),
        P("shot", None, "gx", "gy", None),
        P(None, "shot"),
        P(None, "shot"),
        P("shot", None, None),
        P("shot", None, None),
    )
    out_specs = (P("shot", "gx", "gy"), P(), P())
    return jax.shard_map(body, mesh=mesh, in_specs=in_specs, out_specs=out_specs, check_vma=False)
```

```python
import jax
import jax.numpy as jnp
from jax import lax
from jax.experimental import pallas as pl
from jax.experimental.pallas import tpu as pltpu
from jax.sharding import PartitionSpec as P

CH = 64
STEPS = 3
RIM = 7
VRIM = 4
PAD = 8
GROUP = 4
LANES = 128

coeffs = (1225.0 / 1024.0, -245.0 / 3072.0, 49.0 / 5120.0, -5.0 / 7168.0)

rows_by_cols = (((1,), (0,)), ((), ()))
rows_by_rows = (((1,), (1,)), ((), ()))
half = jnp.bfloat16


def split(values):
    high = values.astype(half)
    return high, (values - high.astype(jnp.float32)).astype(half)


def mm(left, right, how=rows_by_cols):
    return lax.dot_general(left, right, how, preferred_element_type=jnp.float32)


def mm3(left, right, how=rows_by_cols):
    return (
        mm(left[0], right[0], how) + mm(left[1], right[0], how) + mm(left[0], right[1], how)
    )


def mm2(left, pick, how=rows_by_cols):
    return mm(left[0], pick, how) + mm(left[1], pick, how)


def one_hot(shape, rule):
    rows = lax.broadcasted_iota(jnp.int32, shape, 0)
    cols = lax.broadcasted_iota(jnp.int32, shape, 1)
    return rule(rows, cols)


def low_part(values, size):
    assert size & (size - 1) == 0
    return values & (size - 1)


def high_part(values, size):
    assert size & (size - 1) == 0
    return values >> (size.bit_length() - 1)


def as_pick(mask):
    return jnp.where(mask, 1.0, 0.0).astype(half)


def axis_peers(axis, distance):
    count = lax.axis_size(axis)
    return {axis: lax.rem(lax.axis_index(axis) + distance, count)}


def plane_peers():
    near, wide = lax.axis_size("gy"), lax.axis_size("gx")
    for dx in range(wide):
        for dy in range(near):
            if dx or dy:
                yield {
                    "gx": lax.rem(lax.axis_index("gx") + dx, wide),
                    "gy": lax.rem(lax.axis_index("gy") + dy, near),
                }


def everyone():
    for d in range(1, lax.axis_size("shot")):
        yield axis_peers("shot", d)
    yield from plane_peers()


def remote(source, dest, send_sem, recv_sem, peer):
    return pltpu.make_async_remote_copy(
        src_ref=source,
        dst_ref=dest,
        send_sem=send_sem,
        recv_sem=recv_sem,
        device_id=peer,
        device_id_type=pl.DeviceIdType.MESH,
    )


def logistic(values):
    return 0.5 * jnp.tanh(0.5 * values) + 0.5


def whole_kernel(
    latent_ref,
    first_ref,
    second_ref,
    fwd_press,
    fwd_vel,
    adj_press,
    adj_vel,
    src_pos,
    src_amp,
    rec_pos,
    observed,
    own_ref,
    sums_ref,
    w_first,
    w_second,
    place,
    amps,
    rec_at,
    seen,
    start_adj,
    slabs,
    latents,
    hidden,
    gates,
    factors,
    across,
    hits,
    recorded,
    rec_weights,
    mod,
    press,
    buoy_x,
    buoy_y,
    kicks,
    vel_x,
    vel_y,
    vel_z,
    diverge_z,
    div_at,
    slope_x,
    slope_y,
    slope_z,
    totals,
    turned,
    share,
    paired,
    summed,
    landed,
    w_share,
    w_landed,
    w_plane,
    local_sem,
    send_sem,
    recv_sem,
    gather_send,
    gather_recv,
    shot_send,
    shot_recv,
    plane_send,
    plane_recv,
):
    size_x, size_y, size_z = mod.shape
    cells = size_z // 4
    mid_y = pl.ds(PAD, size_y)
    mid_v = pl.ds(VRIM, size_x)
    rows_a = size_x // 4
    wide = GROUP * CH
    halves = size_y // (4 * GROUP)
    shots = lax.axis_size("shot")
    me = lax.axis_index("shot")
    me_x, me_y = lax.axis_index("gx"), lax.axis_index("gy")
    has = (
        me_x > 0,
        me_x < lax.axis_size("gx") - 1,
        me_y > 0,
        me_y < lax.axis_size("gy") - 1,
    )
    target = ({"gx": me_x - 1}, {"gx": me_x + 1}, {"gy": me_y - 1}, {"gy": me_y + 1})

    barrier = pltpu.get_barrier_semaphore()
    greeted = 0
    for peer in everyone():
        pl.semaphore_signal(
            barrier, inc=1, device_id=peer, device_id_type=pl.DeviceIdType.MESH
        )
        greeted += 1

    loads = [
        (latent_ref, slabs.at[me]),
        (first_ref, w_first),
        (second_ref, w_second),
        (rec_pos, rec_at),
        (observed, seen),
        (src_pos, place),
        (src_amp, amps),
        (fwd_press, press.at[0, pl.ds(RIM, size_x), mid_y]),
        (adj_press, start_adj),
    ]
    for way, vel in enumerate((fwd_vel, adj_vel)):
        loads.append((vel.at[0], vel_x.at[way, pl.ds(VRIM, size_x)]))
        loads.append((vel.at[1], vel_y.at[way, :, pl.ds(VRIM, size_y)]))
        loads.append((vel.at[2], vel_z.at[way]))
    moves = [
        pltpu.make_async_copy(source, dest, local_sem.at[n])
        for n, (source, dest) in enumerate(loads)
    ]
    for move in moves:
        move.start()

    class Link:
        def __init__(self, slot, pairs):
            self.copies = {
                side: remote(
                    *pair,
                    send_sem.at[slot, side],
                    recv_sem.at[slot, side ^ 1],
                    target[side],
                )
                for side, pair in pairs.items()
            }

        def send(self, *sides):
            for side in sides or self.copies:
                pl.when(has[side])(self.copies[side].start)

        def receive(self, *sides):
            for side in sides or self.copies:
                pl.when(has[side])(self.copies[side ^ 1].wait_recv)

        def sent(self):
            for side in self.copies:
                pl.when(has[side])(self.copies[side].wait_send)

    def x_pairs(low, high, dest, rim):
        return {0: (low, dest(size_x + rim, rim)), 1: (high, dest(0, rim))}

    def y_pairs(low, high, dest, at_low, at_high):
        return {2: (low, dest(at_high)), 3: (high, dest(at_low))}

    slot = 0
    links_x, links_y = [], []
    spans = (pl.ds(0, RIM), pl.ds(size_x - RIM, RIM), pl.ds(RIM, size_x - 2 * RIM))
    inner = (pl.ds(RIM, RIM), pl.ds(size_x, RIM), pl.ds(2 * RIM, size_x - 2 * RIM))
    for state in range(2 * STEPS):
        parts = []
        for at_y, deep in ((PAD, size_y - 2 * PAD), (0, PAD), (size_y - PAD, PAD)):
            inside = pl.ds(at_y, deep)

            def plane(first, count, state=state, at_y=at_y, deep=deep):
                return press.at[state, pl.ds(first, count), pl.ds(PAD + at_y, deep)]

            low, high = plane(RIM, RIM), plane(size_x, RIM)
            if state == 0:
                low, high = fwd_press.at[spans[0], inside], fwd_press.at[spans[1], inside]
            parts.append(Link(slot, x_pairs(low, high, plane, RIM)))
            slot += 1
        links_x.append(parts)
        parts = []
        for span, rows in zip(spans, inner):

            def strip(first, state=state, rows=rows):
                return press.at[state, rows, pl.ds(first, PAD)]

            low, high = strip(PAD), strip(size_y)
            if state == 0:
                low = fwd_press.at[span, pl.ds(0, PAD)]
                high = fwd_press.at[span, pl.ds(size_y - PAD, PAD)]
            parts.append(Link(slot, y_pairs(low, high, strip, 0, size_y + PAD)))
            slot += 1
        links_y.append(parts)

    def strips(ref):
        return lambda first: ref.at[:, pl.ds(first, VRIM)]

    def layers(ref):
        return lambda first, count: ref.at[pl.ds(first, count)]

    vel_links = []
    for way, vel in enumerate((fwd_vel, adj_vel)):
        pairs = x_pairs(
            vel.at[0, pl.ds(0, VRIM)],
            vel.at[0, pl.ds(size_x - VRIM, VRIM)],
            layers(vel_x.at[way]),
            VRIM,
        )
        pairs.update(
            y_pairs(
                vel.at[1, :, pl.ds(0, VRIM)],
                vel.at[1, :, pl.ds(size_y - VRIM, VRIM)],
                strips(vel_y.at[way]),
                0,
                size_y + VRIM,
            )
        )
        vel_links.append(Link(slot, pairs))
        slot += 1
    pairs = x_pairs(
        buoy_x.at[pl.ds(VRIM, VRIM)], buoy_x.at[pl.ds(size_x, VRIM)], layers(buoy_x), VRIM
    )
    pairs.update(
        y_pairs(
            buoy_y.at[:, pl.ds(VRIM, VRIM)],
            buoy_y.at[:, pl.ds(size_y, VRIM)],
            strips(buoy_y),
            0,
            size_y + VRIM,
        )
    )
    buoy_link = Link(slot, pairs)
    links = [*sum(links_x, []), *sum(links_y, []), *vel_links, buoy_link]

    for side in range(4):

        @pl.when(jnp.logical_not(has[side]))
        def _():
            far = side % 2
            if side < 2:
                rows = pl.ds(far * (size_x + RIM), RIM)
                vrows = pl.ds(far * (size_x + VRIM), VRIM)
                for state in range(2 * STEPS):
                    press[state, rows, mid_y] = jnp.zeros((RIM, size_y, size_z), jnp.float32)
                blank = jnp.zeros((VRIM, size_y, size_z), jnp.float32)
                buoy_x[vrows] = blank
                for way in range(2):
                    vel_x[way, vrows] = blank
            else:
                cols = pl.ds(far * (size_y + PAD), PAD)
                for state in range(2 * STEPS):
                    press[state, pl.ds(RIM, size_x), cols] = jnp.zeros(
                        (size_x, PAD, size_z), jnp.float32
                    )
                vcols = pl.ds(far * (size_y + VRIM), VRIM)
                blank = jnp.zeros((size_x, VRIM, size_z), jnp.float32)
                buoy_y[:, vcols] = blank
                for way in range(2):
                    vel_y[way, :, vcols] = blank

    pl.semaphore_wait(barrier, greeted)

    moves[0].wait()
    mate = lax.rem(me, 2)
    group = me // 2
    groups = shots // 2
    other_core = {"shot": 2 * group + 1 - mate}
    cut = rows_a // 2
    layers_of = (pl.ds(0, cut), pl.ds(cut, rows_a - cut))

    def pass_on(owner, part, peer, row, column):
        rows = slabs.at[owner, layers_of[part]]
        return remote(
            rows, rows, gather_send.at[part, row, column], gather_recv.at[part, row, column], peer
        )

    afar, passed = [], []
    for part in range(2):
        for d in range(1, groups):
            there = {"shot": 2 * lax.rem(group + d, groups) + mate}
            afar.append(pass_on(me, part, there, 0, d))
            owner = 2 * lax.rem(group - d + groups, groups) + mate
            passed.append(pass_on(owner, part, other_core, 1, d))
    beside = [pass_on(me, part, other_core, 1, 0) for part in range(2)]
    for copy in afar + beside:
        copy.start()
    for link in (*links_x[0], *links_y[0], *vel_links):
        link.send()
    for move in moves[1:]:
        move.wait()

    spread_rows = as_pick(one_hot((wide, CH), lambda r, c: low_part(r, CH) == c))
    same_cell = one_hot((wide, wide), lambda r, c: high_part(r, CH) == high_part(c, CH))
    big_first = tuple(
        jnp.where(same_cell, mm(mm(spread_rows, part).astype(half), spread_rows, rows_by_rows), 0.0)
        .astype(half)
        for part in split(w_first[...])
    )
    outs = w_second.shape[1]
    block = outs // 4 * GROUP

    def source_of(c):
        return (c & (block - 16)) + 4 * low_part(c, 4) + high_part(c, block)

    order = as_pick(one_hot((outs, 4 * block), lambda r, c: source_of(c) == r))
    same_out = one_hot((wide, 4 * block), lambda r, c: high_part(c & 12, 4) == high_part(r, CH))
    big_second = tuple(
        jnp.where(same_out, mm(mm(spread_rows, part).astype(half), order), 0.0).astype(half)
        for part in split(w_second[...])
    )
    to_depth = as_pick(
        one_hot((2 * size_z, size_z), lambda r, c: 4 * low_part(r, cells) + high_part(low_part(r, size_z), cells) == c)
    )
    from_depth = as_pick(
        one_hot((2 * size_z, size_z), lambda r, c: 4 * low_part(c, cells) + high_part(c, cells) == low_part(r, size_z))
    )

    def side_by_side(values):
        return jnp.concatenate(split(values), axis=1)


    count = rec_at.shape[2]
    local_x = rec_at[0] - me_x * size_x
    local_y = rec_at[1] - me_y * size_y
    inside = (local_x >= 0) & (local_x < size_x) & (local_y >= 0) & (local_y < size_y)
    column = jnp.where(inside, local_x * size_y + local_y, -1)
    deep = jnp.where(
        lax.broadcasted_iota(jnp.int32, (size_z, count), 0) == rec_at[2], 1.0, 0.0
    )
    rec_weights[pl.ds(0, size_z)] = deep.astype(half)
    for moment in range(STEPS):
        for part, values in enumerate(split(seen[moment])):
            rec_weights[pl.ds((1 + 2 * moment + part) * size_z, size_z)] = (
                deep * values.astype(jnp.float32)
            ).astype(half)
    chunk = 8 if size_x % 8 == 0 else 1
    some = chunk * size_y

    def planes(step, carry):
        index = lax.broadcasted_iota(jnp.int32, (some, count), 0) + step * some
        summed = mm(as_pick(index == column), rec_weights[...], rows_by_rows).reshape(
            chunk, size_y, (2 * STEPS + 1) * size_z
        )
        here = pl.ds(step * chunk, chunk)
        hits[here] = summed[:, :, :size_z]
        for moment in range(STEPS):
            first = (1 + 2 * moment) * size_z
            recorded[moment, here] = (
                summed[:, :, first : first + size_z]
                + summed[:, :, first + size_z : first + 2 * size_z]
            )
        return carry


    src_x = place[:, 0:1] - me_x * size_x
    src_y = place[:, 1:2] - me_y * size_y
    at_source = (lax.broadcasted_iota(jnp.int32, (size_y, size_z), 0) == src_y) & (
        lax.broadcasted_iota(jnp.int32, (size_y, size_z), 1) == place[:, 2:3]
    )
    impulses = [jnp.where(at_source, amps[:, n : n + 1], 0.0) for n in range(STEPS)]

    def kick(x, carry):
        for n in range(STEPS):
            kicks[n, x] = jnp.where(src_x == x, impulses[n], 0.0)
        return carry

    lax.fori_loop(0, size_x, kick, 0)

    for arriving, forward in zip(afar, passed):
        arriving.wait_recv()
        forward.start()
    for copy in beside + passed:
        copy.wait_recv()
    depth_c = slabs.shape[2]
    for s in range(shots):
        for a in range(rows_a):
            for h in range(halves):
                latents[pl.ds((h * rows_a + a) * cells + s * depth_c, depth_c)] = slabs[
                    s, a, :, h * wide : (h + 1) * wide
                ]
    hidden[...] = jnp.tanh(mm3(split(latents[...]), big_first))
    outputs = mm3(split(hidden[...]), big_second)
    blocks = [(h, a) for h in range(halves) for a in range(rows_a)]
    deep_y = 4 * GROUP

    def materials(group_of):
        stacked = jnp.concatenate(
            [
                jnp.transpose(
                    jnp.concatenate(
                        [
                            outputs[n * cells : (n + 1) * cells, k * block : (k + 1) * block]
                            for k in range(4)
                        ],
                        axis=0,
                    )
                )
                for n in group_of
            ],
            axis=0,
        )
        sigs = logistic(mm(side_by_side(stacked), to_depth))
        for at, n in enumerate(group_of):
            h, a = blocks[n]
            sig = sigs[at * block : (at + 1) * block]
            gates[n] = sig
            speed = 0.15 + 0.25 * sig[: block // 2]
            density = 1.0 + 1.5 * sig[block // 2 :]
            modulus = density * speed * speed
            buoyancy = 1.0 / density
            for i in range(4):
                part = slice(i * deep_y, (i + 1) * deep_y)
                mod[4 * a + i, pl.ds(h * deep_y, deep_y)] = modulus[part]
                buoy_x[VRIM + 4 * a + i, pl.ds(h * deep_y, deep_y)] = buoyancy[part]
                buoy_y[4 * a + i, pl.ds(VRIM + h * deep_y, deep_y)] = buoyancy[part]

    at_ends = [n for n, (h, a) in enumerate(blocks) if a in (0, rows_a - 1)]
    materials(at_ends)
    buoy_link.send(0, 1)
    materials([n for n in range(len(blocks)) if n not in at_ends])
    buoy_link.send(2, 3)

    along = [
        split(matrix) for matrix in depth_matrices(size_z)
    ]
    tables = [
        jnp.concatenate(
            [
                jnp.concatenate([high, low], axis=1),
                jnp.concatenate([high, jnp.zeros_like(low)], axis=1),
            ],
            axis=0,
        )
        for high, low in along
    ]

    low_rows, high_rows = (0, RIM), (size_x - RIM, size_x)
    mid_rows = (RIM, size_x - RIM)
    columns = size_y // 8

    def column_of(c, base):
        return pl.ds(pl.multiple_of(8 * c, 8) + base, 8)

    def weigh(ahead, behind):
        summed = 0.0
        for order_at, weight in enumerate(coeffs):
            summed = summed + weight * (ahead[order_at] - behind[order_at])
        return summed

    def along_z(values, table):
        flat = values.reshape(size_x * size_y, size_z)
        both = mm(jnp.concatenate(split(flat), axis=1), table)
        return (both[:, :size_z] + both[:, size_z:]).reshape(values.shape)

    def depth_part(state, way, moment):
        slope = along_z(press[state, pl.ds(RIM, size_x), mid_y], tables[0])
        if way == 0:
            slope_z[moment] = slope
        moved = vel_z[way] - buoy_x[mid_v] * slope
        vel_z[way] = moved
        diverge_z[...] = along_z(moved, tables[1])

    def faces_x(state, way, moment, first, last, span):
        def one(n, carry):
            c = n * span[2]
            here, there = column_of(c, 0), column_of(c, PAD)
            rows = {
                i: press[state, i + RIM, there] for i in range(first - 3, last + 4)
            }
            for x in range(first, last):
                slope = weigh([rows[x + r] for r in (1, 2, 3, 4)], [rows[x - r + 1] for r in (1, 2, 3, 4)])
                vel_x[way, x + VRIM, here] = (
                    vel_x[way, x + VRIM, here] - buoy_x[x + VRIM, here] * slope
                )
                if way == 0 and 0 <= x < size_x:
                    slope_x[moment, x, here] = slope
            return carry

        lax.fori_loop(span[0], span[1], one, 0)

    def faces_y(state, way, moment, rows, strips_of):
        def one(x, carry):
            for first, deep in strips_of:

                def at(r):
                    return press[state, x + RIM, pl.ds(VRIM + first + r, deep)]

                here = pl.ds(first, deep)
                slope = weigh([at(r) for r in (1, 2, 3, 4)], [at(1 - r) for r in (1, 2, 3, 4)])
                vel_y[way, x, here] = vel_y[way, x, here] - buoy_y[x, here] * slope
                if way == 0:
                    slope_y[moment, x, here] = slope
            return carry

        lax.fori_loop(rows[0], rows[1], one, 0, unroll=2)

    def finish(state, way, moment, rows, span):
        first, last = rows

        def one(n, carry):
            c = n * span[2]
            here, there = column_of(c, 0), column_of(c, PAD)
            speeds = {
                i: vel_x[way, i + VRIM, here] for i in range(first - VRIM, last + VRIM - 1)
            }

            def at(x, r):
                return vel_y[way, x, column_of(c, VRIM + r)]

            for x in range(first, last):
                div = diverge_z[x, here] + weigh(
                    [speeds[x + r - 1] for r in (1, 2, 3, 4)], [speeds[x - r] for r in (1, 2, 3, 4)]
                )
                div = div + weigh(
                    [at(x, r - 1) for r in (1, 2, 3, 4)], [at(x, -r) for r in (1, 2, 3, 4)]
                )
                value = press[state, x + RIM, there] - mod[x, here] * div
                if way == 0:
                    value = value + kicks[moment, x, here]
                    div_at[moment, x, here] = div
                    if moment == STEPS - 1:
                        residue = hits[x, here] * value - recorded[moment, x, here]
                        value = start_adj[x, here] + residue
                    press[state + 1, x + RIM, there] = value
                else:
                    part_mod = value * div_at[moment, x, here]
                    part_buoy = (
                        speeds[x] * slope_x[moment, x, here]
                        + at(x, 0) * slope_y[moment, x, column_of(c, VRIM)]
                        + vel_z[way, x, here] * slope_z[moment, x, here]
                    )
                    if moment == STEPS - 1:
                        totals[0, x, here] = -part_mod
                        totals[1, x, here] = -part_buoy
                    else:
                        totals[0, x, here] = totals[0, x, here] - part_mod
                        totals[1, x, here] = totals[1, x, here] - part_buoy
                    if moment > 0:
                        modelled = press[moment, x + RIM, there]
                        residue = hits[x, here] * modelled - recorded[moment - 1, x, here]
                        press[state + 1, x + RIM, there] = value + residue
            return carry

        lax.fori_loop(span[0], span[1], one, 0)

    def prepare_gates():
        for n in range(len(blocks)):
            sig = gates[n]
            sig_speed, sig_dens = sig[: block // 2], sig[block // 2 :]
            speed = 0.15 + 0.25 * sig_speed
            density = 1.0 + 1.5 * sig_dens
            inverse = 1.0 / density
            bend = 1.5 * sig_dens * (1.0 - sig_dens)
            factors[0, n] = 0.5 * density * speed * sig_speed * (1.0 - sig_speed)
            factors[1, n] = speed * speed * bend
            factors[2, n] = inverse * inverse * bend

    def prepare_rows():
        for n, rows in enumerate((latents, hidden)):
            high, low = split(jnp.transpose(rows[...]))
            across[n, 0] = high
            across[n, 1] = low

    every, inner_columns, outer_columns = (0, columns, 1), (1, columns - 1, 1), (0, 2, columns - 1)
    inner_strips = ((8, size_y + 2 * VRIM - 16),)
    outer_strips = ((0, 8), (size_y + 2 * VRIM - 8, 8))

    def step(state, way, moment):
        depth_part(state, way, moment)
        faces_x(state, way, moment, 3, size_x - 4, every)
        turns = size_x // chunk
        if state == 0:
            lax.fori_loop(0, 2 * turns // 3, planes, 0)
        if state == 1:
            lax.fori_loop(2 * turns // 3, turns, planes, 0)
        ends = [(0, low_rows, (-VRIM, 3)), (1, high_rows, (size_x - 4, size_x + 3))]
        if state % 2:
            ends.reverse()
        more = state + 1 < 2 * STEPS
        if state == 0:
            buoy_link.receive(0, 1)
        if state % STEPS == 0:
            vel_links[way].receive(0, 1)
        for side, rows, ghosts in ends:
            faces_y(state, way, moment, rows, inner_strips)
            links_x[state][0].receive(side)
            faces_x(state, way, moment, *ghosts, inner_columns)
            finish(state, way, moment, rows, inner_columns)
            if more:
                links_x[state + 1][0].send(side)
        faces_y(state, way, moment, mid_rows, inner_strips)
        finish(state, way, moment, mid_rows, inner_columns)
        if state == STEPS + 1:
            prepare_gates()
        if state == STEPS + 2:
            prepare_rows()
        if state == 0:
            buoy_link.receive(2, 3)
        if state % STEPS == 0:
            vel_links[way].receive(2, 3)
        for side, rows, ghosts in ends:
            links_y[state][side].receive()
            for part in (1, 2):
                links_x[state][part].receive(side)
            faces_x(state, way, moment, *ghosts, outer_columns)
            faces_y(state, way, moment, rows, outer_strips)
            finish(state, way, moment, rows, outer_columns)
            if more:
                links_y[state + 1][side].send()
                for part in (1, 2):
                    links_x[state + 1][part].send(side)
        links_y[state][2].receive()
        faces_y(state, way, moment, mid_rows, outer_strips)
        finish(state, way, moment, mid_rows, outer_columns)
        if more:
            links_y[state + 1][2].send()

    for moment in range(STEPS):
        step(moment, 0, moment)
    for turn in range(STEPS):
        step(STEPS + turn, 1, STEPS - 1 - turn)

    for n, (h, a) in enumerate(blocks):
        here = pl.ds(h * deep_y, deep_y)
        grad_mod = jnp.concatenate([totals[0, 4 * a + i, here] for i in range(4)], axis=0)
        grad_buoy = jnp.concatenate([totals[1, 4 * a + i, here] for i in range(4)], axis=0)
        gates[n, pl.ds(0, block // 2)] = grad_mod * factors[0, n]
        gates[n, pl.ds(block // 2, block // 2)] = (
            grad_mod * factors[1, n] - grad_buoy * factors[2, n]
        )
    permuted = mm(side_by_side(gates[...].reshape(len(blocks) * block, size_z)), from_depth)
    for n in range(len(blocks)):
        rows = jnp.transpose(permuted[n * block : (n + 1) * block])
        for k in range(4):
            turned[pl.ds(n * cells, cells), k * block : (k + 1) * block] = rows[
                k * cells : (k + 1) * cells
            ]
    outer = split(turned[...])
    inner = split(
        mm3(outer, big_second, rows_by_rows) * (1.0 - hidden[...] * hidden[...])
    )
    big_gf = mm3((across[0, 0], across[0, 1]), inner)
    big_gs = mm3((across[1, 0], across[1, 1]), outer)
    sum_f = 0.0
    sum_s = 0.0
    for b in range(GROUP):
        mine = slice(b * CH, (b + 1) * CH)
        sum_f = sum_f + jnp.where(
            one_hot((CH, wide), lambda r, c: high_part(c, CH) == b), big_gf[mine], 0.0
        )
        sum_s = sum_s + jnp.where(
            one_hot((CH, 4 * block), lambda r, c: high_part(c & 12, 4) == b), big_gs[mine], 0.0
        )
    grad_second = mm2(split(sum_s), order, rows_by_rows)
    grad_first = 0.0
    for side in range(2):
        fold = as_pick(one_hot((wide, outs), lambda r, c: low_part(r, CH) + side * CH == c))
        grad_first = grad_first + mm2(
            split(sum_f[side * CH // 2 : (side + 1) * CH // 2]), fold
        )
    weights = jnp.concatenate([grad_second, grad_first], axis=0)

    def total(stack):
        summed = stack[0]
        for n in range(1, stack.shape[0]):
            summed = summed + stack[n]
        return summed

    peers = list(plane_peers())
    spot = me_x * lax.axis_size("gy") + me_y
    piece = weights.shape[0] // shots
    for n in range(shots):
        w_share[n] = weights[n * piece : (n + 1) * piece]
    first_hops = [
        remote(
            w_share.at[axis_peers("shot", d)["shot"]],
            w_landed.at[me],
            shot_send.at[0, d - 1],
            shot_recv.at[0, d - 1],
            axis_peers("shot", d),
        )
        for d in range(1, shots)
    ]
    for hop in first_hops:
        hop.start()
    w_landed[me] = w_share[me]

    grad_rows = mm3(inner, big_first, rows_by_rows)
    for n, (h, a) in enumerate(blocks):
        for s in range(shots):
            first = n * cells + s * depth_c
            share[s % 2, s // 2, a, :, h * wide : (h + 1) * wide] = grad_rows[
                first : first + depth_c
            ]
    swap = remote(
        share.at[1 - mate],
        paired,
        shot_send.at[1, 0],
        shot_recv.at[1, 0],
        other_core,
    )
    swap.start()
    for hop in first_hops:
        hop.wait()
    w_plane[spot] = total(w_landed)
    second_hops = [
        remote(w_plane.at[spot], w_plane.at[spot], plane_send.at[n], plane_recv.at[n], peer)
        for n, peer in enumerate(peers)
    ]
    for hop in second_hops:
        hop.start()
    swap.wait()
    for g in range(groups):
        summed[g] = share[mate, g] + paired[g]
    scatters = []
    for d in range(1, groups):
        there = lax.rem(group + d, groups)
        scatters.append(
            remote(
                summed.at[there],
                landed.at[group],
                shot_send.at[3, d - 1],
                shot_recv.at[3, d - 1],
                {"shot": 2 * there + mate},
            )
        )
    for copy in scatters:
        copy.start()
    landed[group] = summed[group]
    for hop in second_hops:
        hop.wait()
    sums_ref[me] = total(w_plane)
    third_hops = [
        remote(
            sums_ref.at[me],
            sums_ref.at[me],
            shot_send.at[4, d - 1],
            shot_recv.at[4, d - 1],
            axis_peers("shot", d),
        )
        for d in range(1, shots)
    ]
    for hop in third_hops:
        hop.start()
    for copy in scatters:
        copy.wait()
    own_ref[...] = total(landed)
    for hop in third_hops:
        hop.wait()
    for copy in afar + beside + passed:
        copy.wait_send()
    for link in links:
        link.sent()


def depth_matrices(size_z):
    source = lax.broadcasted_iota(jnp.int32, (size_z, size_z), 0)
    dest = lax.broadcasted_iota(jnp.int32, (size_z, size_z), 1)
    plus = jnp.zeros((size_z, size_z), jnp.float32)
    minus = plus
    for order, weight in enumerate(coeffs):
        r = order + 1
        plus = plus + jnp.where(source == dest + r, weight, 0.0)
        plus = plus - jnp.where(source == dest - r + 1, weight, 0.0)
        minus = minus + jnp.where(source == dest + r - 1, weight, 0.0)
        minus = minus - jnp.where(source == dest - r, weight, 0.0)
    return plus, minus


def finish_kernel(own_ref, sums_ref, latent_ref, first_ref, second_ref, joined):
    latent_ref[...] = own_ref[...]
    piece = sums_ref.shape[1]
    for s in range(sums_ref.shape[0]):
        joined[pl.ds(s * piece, piece)] = sums_ref[s]
    second_ref[...] = joined[pl.ds(0, CH)]
    packed = joined[pl.ds(CH, CH // 2)]
    first_ref[pl.ds(0, CH // 2)] = packed[:, :CH]
    first_ref[pl.ds(CH // 2, CH // 2)] = packed[:, CH:]


def body(
    latent,
    w_first,
    w_second,
    fwd_press,
    fwd_vel,
    adj_press,
    adj_vel,
    src_pos,
    src_amp,
    rec_pos,
    observed,
):
    field = fwd_press.shape[1:]
    size_x, size_y, size_z = field
    tall = size_y + 2 * PAD
    depth_c, rows_a, merged = latent.shape
    cells = size_z // 4
    shots = lax.axis_size("shot")
    tiles = lax.axis_size("gx") * lax.axis_size("gy")
    halves = size_y // (4 * GROUP)
    outs = w_second.shape[1]
    count = rec_pos.shape[2]
    anywhere = pl.BlockSpec(memory_space=pl.ANY)
    vmem = pl.BlockSpec(memory_space=pltpu.VMEM)
    slots = 6 * 2 * STEPS + 3
    piece = (CH + CH // 2) // shots

    def scratch(*shape, kind=jnp.float32):
        return pltpu.VMEM(shape, kind)

    def sems(*shape):
        return pltpu.SemaphoreType.DMA(shape)

    own, sums = pl.pallas_call(
        whole_kernel,
        out_shape=(
            jax.ShapeDtypeStruct((rows_a, depth_c, merged), jnp.float32),
            jax.ShapeDtypeStruct((shots, piece, outs), jnp.float32),
        ),
        in_specs=[anywhere] * 11,
        out_specs=(vmem, vmem),
        scratch_shapes=[
            scratch(*w_first.shape),
            scratch(*w_second.shape),
            scratch(*src_pos.shape[::-1], kind=jnp.int32),
            scratch(*src_amp.shape[::-1]),
            scratch(3, 1, count, kind=jnp.int32),
            scratch(STEPS, 1, count),
            scratch(*field),
            scratch(shots, rows_a, depth_c, merged),
            scratch(halves * rows_a * cells, GROUP * CH),
            scratch(halves * rows_a * cells, GROUP * CH),
            scratch(halves * rows_a, GROUP * outs // 4, size_z),
            scratch(3, halves * rows_a, GROUP * outs // 8, size_z),
            scratch(2, 2, GROUP * CH, halves * rows_a * cells, kind=half),
            scratch(*field),
            scratch(STEPS, *field),
            scratch((2 * STEPS + 1) * size_z, count, kind=half),
            scratch(*field),
            scratch(2 * STEPS, size_x + 2 * RIM, tall, size_z),
            scratch(size_x + 2 * VRIM, size_y, size_z),
            scratch(size_x, size_y + 2 * VRIM, size_z),
            scratch(STEPS, *field),
            scratch(2, size_x + 2 * VRIM, size_y, size_z),
            scratch(2, size_x, size_y + 2 * VRIM, size_z),
            scratch(2, *field),
            scratch(*field),
            scratch(STEPS, *field),
            scratch(STEPS, *field),
            scratch(STEPS, size_x, size_y + 2 * VRIM, size_z),
            scratch(STEPS, *field),
            scratch(2, *field),
            scratch(halves * rows_a * cells, GROUP * outs),
            scratch(2, shots // 2, rows_a, depth_c, merged),
            scratch(shots // 2, rows_a, depth_c, merged),
            scratch(shots // 2, rows_a, depth_c, merged),
            scratch(shots // 2, rows_a, depth_c, merged),
            scratch(shots, piece, outs),
            scratch(shots, piece, outs),
            scratch(tiles, piece, outs),
            sems(15),
            sems(slots, 4),
            sems(slots, 4),
            sems(2, 2, shots // 2),
            sems(2, 2, shots // 2),
            sems(5, shots),
            sems(5, shots),
            sems(tiles),
            sems(tiles),
        ],
        compiler_params=pltpu.CompilerParams(
            collective_id=0, has_side_effects=True, vmem_limit_bytes=60 * 1024 * 1024
        ),
    )(
        latent.transpose(1, 0, 2),
        w_first,
        w_second,
        fwd_press[0],
        fwd_vel[0],
        adj_press[0],
        adj_vel[0],
        src_pos.T,
        src_amp.T,
        rec_pos.transpose(1, 0, 2),
        observed.transpose(1, 0, 2),
    )
    grad_latent, grad_first, grad_second = pl.pallas_call(
        finish_kernel,
        out_shape=(
            jax.ShapeDtypeStruct(own.shape, jnp.float32),
            jax.ShapeDtypeStruct(w_first.shape, jnp.float32),
            jax.ShapeDtypeStruct(w_second.shape, jnp.float32),
        ),
        scratch_shapes=[scratch(shots * piece, outs)],
    )(own, sums)
    return grad_latent.transpose(1, 0, 2), grad_first, grad_second


def solution(mesh):
    in_specs = (
        P("shot", "gx", "gy"),
        P(),
        P(),
        P("shot", "gx", "gy", None),
        P("shot", None, "gx", "gy", None),
        P("shot", "gx", "gy", None),
        P("shot", None, "gx", "gy", None),
        P(None, "shot"),
        P(None, "shot"),
        P("shot", None, None),
        P("shot", None, None),
    )
    out_specs = (P("shot", "gx", "gy"), P(), P())
    return jax.shard_map(body, mesh=mesh, in_specs=in_specs, out_specs=out_specs, check_vma=False)
```
